512 devices in a mesh: grp: 32 (over x, z), vocab: 16 (over y, core).
Axes of the slice: x: 4, y: 8, z: 8, core: 2. Of those that a mesh axis runs over, the one named last changes fastest.
Arguments:
- inner_x: bfloat16 [8192, 4096], P('grp', 'vocab'), may hold values from -6 to 6
- gate_z: bfloat16 [8192, 4096], P('grp', 'vocab'), may hold values from -6 to 6
- state_b: bfloat16 [8192, 128], P('grp'), may hold values from -6 to 6
- state_c: bfloat16 [8192, 128], P('grp'), may hold values from -6 to 6
- step_raw: float32 [64, 8192], P('vocab', 'grp'), may hold values from -6 to 6
- decay_log: float32 [64], P('vocab'), may hold values from 0 to 2.77
- step_bias: float32 [64], P('vocab'), may hold values from -7 to -2.3
- skip_gain: float32 [64], P('vocab'), may hold values from 0.5 to 1.5
- norm_gain: float32 [4096], P('vocab'), may hold values from 0.5 to 1.5
- out_weight: bfloat16 [4096, 2048], P('vocab'), may hold values from -0.09375 to 0.09375
- residual: bfloat16 [8192, 2048], P('grp'), may hold values from -6 to 6
- ref_hidden: bfloat16 [8192, 2048], P('grp'), may hold values from -6 to 6
- policy_gain: float32 [2048], replicated, may hold values from 0.5 to 1.5
- ref_gain: float32 [2048], replicated, may hold values from 0.5 to 1.5
- policy_head: bfloat16 [2048, 25216], P('grp', 'vocab')
- ref_head: bfloat16 [2048, 25216], P('grp', 'vocab')
- saved_pages: bfloat16 [128, 4096, 128], P('grp', 'vocab'), may hold values from -0.5 to 0.5
- lengths: int32 [32, 16], P('grp'), may hold values from 1 to 96, 256 in all within a row
- page_owner: int32 [32, 16], replicated, may hold values from 0 to 31, as said below
- page_slot: int32 [32, 16], replicated, may hold values from 0 to 3
- resumed: int32 [32, 16], P('grp'), may hold values 0 or 1
- targets: int32 [8192], P('grp'), may hold values from 0 to 25215
Outputs:
- logprobs: float32 [2, 8192], P(None, 'grp')
- request_sums: float32 [2, 512], P(None, 'grp')
The draws below stay inside these ranges and needn't reach their ends.
Inputs may be any that keep to these rules, and one draw needn't show every extreme that they name: Each group's lengths sum to 256, and its largest is 96. `page_owner`: the 16 requests of one group name 16 different owner groups.
All inputs are finite; a program needn't handle non-finite values. No bound on the sum of `resumed` on one device may be relied on, other than what follows from the above.
Results may differ from the reference program's by a relative error of at most 0.0011.
Values may be sent and summed in bfloat16 or wider, within the bound.
No kernel may reach another device: no remote copies, remote signals or barrier semaphores. Data moves between devices by JAX's collectives and lax.ppermute only.
A program may use at most 64 MiB of HBM per device.

```python
import math
import jax
import jax.numpy as jnp
import numpy as np
from jax import lax

D = 2048
HEADS = 64
HEAD_DIM = 64
STATE = 128
INNER = 4096
VOCAB = 25216
TOK_GRP = 256
REQ_GRP = 16
LEN_MOST = 96
SLOTS = 4
GROUPS = 32
TOKENS = 8192
REQUESTS = 512
PAGES = 128


def draw_head(key, salt_value):
    sub_key = jax.random.fold_in(key, salt_value)
    base_key = jax.random.fold_in(sub_key, 0)
    factor = 3.0 / math.sqrt(D)
    values = jax.random.normal(base_key, (D, VOCAB), jnp.float32)
    return (values * factor).astype(jnp.bfloat16)


def draw_policy_head(key, part):
    return draw_head(key, 17)


def draw_ref_head(key, part):
    return draw_head(key, 23)


def choose_owners(row_key):
    return jax.random.permutation(row_key, GROUPS)[:REQ_GRP]


def draw_page_owner(key, part):
    row_keys = jax.random.split(jax.random.fold_in(key, 29), GROUPS)
    return jax.vmap(choose_owners)(row_keys).astype(jnp.int32)


def with_ends(values, stream_key, least, largest):
    index_at = [jax.random.randint(jax.random.fold_in(stream_key, axis), (), 0, length) for axis, length in enumerate(values.shape)]
    longest = values.shape.index(max(values.shape))
    neighbour = index_at[:longest] + [(index_at[longest] + 1) % values.shape[longest]] + index_at[longest + 1:]
    return values.at[tuple(index_at)].set(least).at[tuple(neighbour)].set(largest)


def block_levels(own_key, dims, pieces, low, top_value):
    loudness = 1.0
    for axis_at, shards_of in pieces:
        draws = jax.random.uniform(jax.random.fold_in(jax.random.fold_in(own_key, 6), axis_at), (shards_of,), jnp.float32, low / len(pieces), top_value / len(pieces))
        loudness = loudness * jnp.repeat(jnp.exp(draws), dims[axis_at] // shards_of).reshape((-1,) + (1,) * (len(dims) - 1 - axis_at))
    return loudness


def cumulative_ranks(amount, skew):
    loads = [(1 << 20) // math.isqrt(rank ** skew) + 1 for rank in range(1, amount + 1)]
    deviation = 1 + sum(loads) // (1 << 30)
    return np.cumsum(np.array([max(1, weight // deviation) for weight in loads]))


def skewed_ids(rng, extent, amount, skew):
    grid = cumulative_ranks(amount, skew)
    pick = jax.random.randint(jax.random.fold_in(rng, 1), extent, 0, int(grid[amount - 1]))
    rank = jnp.searchsorted(jnp.asarray(grid, jnp.int32), pick, side="right")
    return jax.random.permutation(jax.random.fold_in(rng, 2), amount)[rank].astype(jnp.int32)


def split_up(number_of, total, bound, slope):
    portions = [(1 << 20) // math.isqrt(grade ** slope) + 1 for grade in range(2, number_of + 1)]
    surplus, counts = total - bound - (number_of - 1), [1] * (number_of - 1)
    while surplus > 0:
        movable = [i for i in range(number_of - 1) if counts[i] < bound]
        whole, budget = sum([portions[i] for i in movable]), surplus
        for i in movable:
            more = min(bound - counts[i], max(1, budget * portions[i] // whole), surplus)
            counts[i] = counts[i] + more
            surplus = surplus - more
    return np.array([bound] + counts)


def ragged(key, number_of, total, most, lean):
    if number_of == 2:
        one = jax.random.randint(key, (), max(1, total - most), min(most, total - 1) + 1)
        return jnp.stack([one, total - one])
    sizes = jnp.asarray(split_up(number_of, total, most, lean), jnp.int32)
    twos = (number_of - 1) // 2
    giver, sink = sizes[1:1 + 2 * twos:2], sizes[2:2 + 2 * twos:2]
    slack = jnp.minimum(giver - 1, most - sink)
    shifted = jax.random.randint(jax.random.fold_in(key, 1), (twos,), 0, 1 << 20) % (slack + 1)
    sizes = sizes.at[1:1 + 2 * twos:2].set(giver - shifted).at[2:2 + 2 * twos:2].set(sink + shifted)
    return sizes[jax.random.permutation(jax.random.fold_in(key, 2), number_of)]


def gaussian(rng, shape, spread, limit, shards=(), kind=jnp.bfloat16):
    loudness = block_levels(rng, shape, shards, -0.22, 0.18) if shards else 1.0
    entries = jax.random.normal(rng, shape, jnp.float32) * spread * loudness
    return jnp.minimum(jnp.maximum(entries, -limit), limit).astype(kind)


def setup_inputs(seed: int = 0) -> dict:
    seeds = jax.random.split(jax.random.key(seed), 23)
    inner_x = gaussian(seeds[0], (TOKENS, INNER), 1.0, 6.0, ((0, 32), (1, 16)))
    gate_z = gaussian(seeds[1], (TOKENS, INNER), 1.0, 6.0, ((0, 32), (1, 16)))
    state_b = gaussian(seeds[2], (TOKENS, STATE), 1.0, 6.0, ((0, 32),))
    state_c = gaussian(seeds[3], (TOKENS, STATE), 1.0, 6.0, ((0, 32),))
    step_raw = gaussian(seeds[4], (HEADS, TOKENS), 1.0, 6.0, ((0, 16), (1, 32)), jnp.float32)
    decay_log = jnp.clip(2.77 * jax.random.uniform(seeds[5], (HEADS,), jnp.float32) ** block_levels(seeds[5], (HEADS,), ((0, 16),), -0.2, 0.2), 0.0, 2.77)
    step_bias = jnp.clip(-7.0 + 4.7 * jax.random.uniform(seeds[6], (HEADS,), jnp.float32) ** block_levels(seeds[6], (HEADS,), ((0, 16),), -0.2, 0.2), -7.0, -2.3)
    skip_gain = jnp.clip(0.5 + 1.0 * jax.random.uniform(seeds[7], (HEADS,), jnp.float32) ** block_levels(seeds[7], (HEADS,), ((0, 16),), -0.2, 0.2), 0.5, 1.5)
    norm_gain = jnp.clip(1.0 + 0.1 * jax.random.normal(seeds[8], (INNER,), jnp.float32), 0.5, 1.5)
    out_weight = gaussian(seeds[9], (INNER, D), INNER ** -0.5, 0.09375, ((0, 16),))
    residual = gaussian(seeds[10], (TOKENS, D), 1.0, 6.0, ((0, 32),))
    ref_hidden = gaussian(seeds[11], (TOKENS, D), 1.0, 6.0, ((0, 32),))
    policy_gain = jnp.clip(1.0 + 0.1 * jax.random.normal(seeds[12], (D,), jnp.float32), 0.5, 1.5)
    ref_gain = jnp.clip(1.0 + 0.1 * jax.random.normal(seeds[13], (D,), jnp.float32), 0.5, 1.5)
    policy_head = draw_policy_head(jax.random.fold_in(seeds[22], 71), 0)
    ref_head = draw_ref_head(jax.random.fold_in(seeds[22], 71), 0)
    saved_pages = gaussian(seeds[16], (PAGES, INNER, STATE), STATE ** -0.5, 0.5, ((0, 32), (1, 16)))
    lengths = jax.vmap(lambda own: ragged(own, REQ_GRP, TOK_GRP, LEN_MOST, 2))(jax.random.split(seeds[17], GROUPS)).reshape((GROUPS, REQ_GRP)).astype(jnp.int32)
    page_owner = draw_page_owner(jax.random.fold_in(seeds[22], 71), 0)
    page_slot = with_ends(jax.random.randint(seeds[19], (GROUPS, REQ_GRP), 0, SLOTS), jax.random.fold_in(seeds[19], 1), 0, SLOTS - 1).astype(jnp.int32)
    resumed = with_ends((jax.random.randint(seeds[20], (GROUPS, REQ_GRP), 0, 8) < 7).astype(jnp.int32), jax.random.fold_in(seeds[20], 1), 0, 1)
    targets = with_ends(skewed_ids(seeds[21], (TOKENS,), VOCAB, 2), jax.random.fold_in(seeds[21], 3), 0, VOCAB - 1).astype(jnp.int32)
    return {"inner_x": inner_x, "gate_z": gate_z, "state_b": state_b, "state_c": state_c, "step_raw": step_raw, "decay_log": decay_log, "step_bias": step_bias, "skip_gain": skip_gain, "norm_gain": norm_gain, "out_weight": out_weight, "residual": residual, "ref_hidden": ref_hidden, "policy_gain": policy_gain, "ref_gain": ref_gain, "policy_head": policy_head, "ref_head": ref_head, "saved_pages": saved_pages, "lengths": lengths, "page_owner": page_owner, "page_slot": page_slot, "resumed": resumed, "targets": targets}


precise = lax.Precision.HIGHEST
epsilon = 1e-05

def prepare(step_raw, decay_log, step_bias, length_row):
    tok_count = step_raw.shape[1]
    step_size = jax.nn.softplus(step_raw + step_bias[:, None])
    log_decay = -jnp.exp(decay_log)[:, None] * step_size
    cumulative = jnp.cumsum(log_decay, axis=1)
    before = cumulative - log_decay
    ends = jnp.cumsum(length_row).astype(jnp.int32)
    starts = (ends - length_row).astype(jnp.int32)
    position = jnp.arange(tok_count, dtype=jnp.int32)
    member = jnp.logical_and(position[:, None] >= starts[None, :], position[:, None] < ends[None, :]).astype(jnp.float32)
    at_start = jnp.take(before, starts, axis=1)
    start_tok = jnp.dot(at_start, member.T, precision=precise)
    same_req = jnp.dot(member, member.T, precision=precise) > 0.5
    causal = jnp.logical_and(position[:, None] >= position[None, :], same_req)
    return (step_size, cumulative, before, member, start_tok, causal, starts)

def intra_outputs(inner_x, state_b, state_c, step_size, cumulative, causal, head_count):
    tok_count = inner_x.shape[0]
    scores = jnp.dot(state_c, state_b.T, preferred_element_type=jnp.float32)
    gap_val = jnp.where(causal[None], cumulative[:, :, None] - cumulative[:, None, :], 0.0)
    mixing = jnp.where(causal[None], jnp.exp(gap_val), 0.0) * scores[None] * step_size[:, None, :]
    mixing = mixing.astype(jnp.bfloat16)
    values = inner_x.reshape(tok_count, head_count, -1)
    return jnp.einsum('hts,shp->thp', mixing.astype(jnp.float32), values.astype(jnp.float32), precision=precise)

def final_state(inner_x, state_b, step_size, cumulative, before, member, starts, init_last, head_count):
    tok_count = inner_x.shape[0]
    last_col = member[:, -1]
    final_cum = cumulative[:, -1]
    inside = last_col[None, :] > 0.5
    weight = jnp.where(inside, jnp.exp(jnp.where(inside, final_cum[:, None] - cumulative, 0.0)) * step_size, 0.0)
    scaled = inner_x.astype(jnp.float32).reshape(tok_count, head_count, -1) * weight.T[:, :, None]
    summed = jnp.dot(scaled.reshape(tok_count, -1).T, state_b.astype(jnp.float32), precision=precise)
    kept = jnp.exp(final_cum - before[:, starts[-1]])
    return summed.reshape(init_last.shape) + kept[:, None, None] * init_last

def start_outputs(state_c, init_states, member, cumulative, start_tok):
    requests, head_count, head_width, state_width = init_states.shape
    tok_count = state_c.shape[0]
    flat_init = init_states.reshape(-1, state_width)
    project = jnp.einsum('tn,kn->tk', state_c.astype(jnp.float32), flat_init, precision=precise)
    project = project.reshape(tok_count, requests, head_count * head_width)
    picked = jnp.einsum('trk,tr->tk', project, member, precision=precise)
    decay_tok = jnp.exp(cumulative - start_tok).T
    return picked.reshape(tok_count, head_count, head_width) * decay_tok[:, :, None]

def gate_terms(inner_x, gate_z, skip_gain, norm_gain, intra_out, start_out, head_count):
    tok_count = inner_x.shape[0]
    values = inner_x.astype(jnp.float32).reshape(tok_count, head_count, -1)
    mixed = intra_out + start_out + skip_gain[None, :, None] * values
    gated = mixed.reshape(tok_count, -1) * jax.nn.silu(gate_z.astype(jnp.float32))
    squares = lax.optimization_barrier(jnp.sum(gated * gated, axis=1))
    weighted = (gated * norm_gain[None, :]).astype(jnp.bfloat16)
    return (weighted, squares)

def final_norm(hidden, gain_row):
    factor = lax.rsqrt(lax.optimization_barrier(jnp.mean(hidden * hidden, axis=1)) + epsilon)
    return (hidden * factor[:, None] * gain_row[None, :]).astype(jnp.bfloat16)

def score(normed, head_matrix, target_row):
    logits = jnp.dot(normed, head_matrix, preferred_element_type=jnp.float32)
    row_top = lax.optimization_barrier(jnp.max(logits, axis=1))
    total = lax.optimization_barrier(jnp.sum(jnp.exp(logits - row_top[:, None]), axis=1))
    picked = jnp.take_along_axis(logits, target_row[:, None].astype(jnp.int32), axis=1)[:, 0]
    return picked - (row_top + jnp.log(total))

def reference(inner_x, gate_z, state_b, state_c, step_raw, decay_log, step_bias, skip_gain, norm_gain, out_weight, residual, ref_hidden, policy_gain, ref_gain, policy_head, ref_head, saved_pages, lengths, page_owner, page_slot, resumed, targets):
    xs_group = inner_x.reshape(GROUPS, TOK_GRP, INNER)
    zs_group = gate_z.reshape(GROUPS, TOK_GRP, INNER)
    bs_group = state_b.reshape(GROUPS, TOK_GRP, STATE)
    cs_group = state_c.reshape(GROUPS, TOK_GRP, STATE)
    steps_group = step_raw.reshape(HEADS, GROUPS, TOK_GRP).transpose(1, 0, 2)
    resid_group = residual.reshape(GROUPS, TOK_GRP, D)
    refs_group = ref_hidden.reshape(GROUPS, TOK_GRP, D)
    tgts_group = targets.reshape(GROUPS, TOK_GRP)

    def fetch(owner_ids, slot_ids, resume_flags):
        index = (owner_ids * SLOTS + slot_ids).astype(jnp.int32)
        got = jnp.take(saved_pages, index, axis=0).astype(jnp.float32)
        got = got.reshape(REQ_GRP, HEADS, HEAD_DIM, STATE)
        return got * resume_flags.astype(jnp.float32)[:, None, None, None]

    def first_pass(item):
        x_grp, b_grp, s_grp, len_grp, own_grp, slot_grp, res_grp = item
        step_size, cumulative, before, member, start_tok, causal, starts = prepare(s_grp, decay_log, step_bias, len_grp)
        init_states = fetch(own_grp, slot_grp, res_grp)
        return final_state(x_grp, b_grp, step_size, cumulative, before, member, starts, init_states[-1], HEADS)
    ends_all = lax.map(first_pass, (xs_group, bs_group, steps_group, lengths, page_owner, page_slot, resumed))
    previous = jnp.concatenate([jnp.zeros_like(ends_all[:1]), ends_all[:-1]], axis=0)
    group_ids = jnp.arange(GROUPS, dtype=jnp.int32)
    has_carry = group_ids >= 1

    def second_pass(item):
        x_grp, z_grp, b_grp, c_grp, s_grp, len_grp, own_grp, slot_grp, res_grp, prev_grp, flag_grp, resid_grp, ref_grp, tgt_grp = item
        step_size, cumulative, before, member, start_tok, causal, starts = prepare(s_grp, decay_log, step_bias, len_grp)
        init_states = fetch(own_grp, slot_grp, res_grp)
        first_state = jnp.where(flag_grp, prev_grp, init_states[0])
        init_states = jnp.concatenate([first_state[None], init_states[1:]], axis=0)
        intra_out = intra_outputs(x_grp, b_grp, c_grp, step_size, cumulative, causal, HEADS)
        start_out = start_outputs(c_grp, init_states, member, cumulative, start_tok)
        weighted, squares = gate_terms(x_grp, z_grp, skip_gain, norm_gain, intra_out, start_out, HEADS)
        partial_value = jnp.dot(weighted, out_weight, preferred_element_type=jnp.float32)
        hidden = resid_grp.astype(jnp.float32) + partial_value * lax.rsqrt(squares / INNER + epsilon)[:, None]
        policy_lp = score(final_norm(hidden, policy_gain), policy_head, tgt_grp)
        ref_lp = score(final_norm(ref_grp.astype(jnp.float32), ref_gain), ref_head, tgt_grp)
        paired = jnp.stack([policy_lp, policy_lp - ref_lp])
        sums = jnp.dot(paired, member, precision=precise)
        return (jnp.stack([policy_lp, ref_lp]), sums)
    logp_all, sums_all = lax.map(second_pass, (xs_group, zs_group, bs_group, cs_group, steps_group, lengths, page_owner, page_slot, resumed, previous, has_carry, resid_group, refs_group, tgts_group))
    logprobs = logp_all.transpose(1, 0, 2).reshape(2, TOKENS)
    request_sums = sums_all.transpose(1, 0, 2).reshape(2, REQUESTS)
    return (logprobs, request_sums)
```

```python
import functools

import jax
import jax.numpy as jnp
from jax import lax
from jax.experimental import pallas as pl
from jax.experimental.pallas import tpu as pltpu
from jax.sharding import PartitionSpec as P

INNER = 4096
EPS = 1e-05
F32 = jnp.float32
BF16 = jnp.bfloat16
NT = (((1,), (1,)), ((), ()))
TN = (((0,), (0,)), ((), ()))
VM = pl.BlockSpec(memory_space=pltpu.VMEM)
SM = pl.BlockSpec(memory_space=pltpu.SMEM)


def params(limit=48 << 20):
    return pltpu.CompilerParams(vmem_limit_bytes=limit)


def cost(flops, moved, transcendentals=0):
    return pl.CostEstimate(flops=flops, bytes_accessed=moved, transcendentals=transcendentals)


def split(value):
    high = value.astype(BF16)
    low = (value - high.astype(F32)).astype(BF16)
    return high, low


def choose_kernel(slot_ref, pages_ref, out_ref):
    for dest in range(out_ref.shape[0]):
        out_ref[dest] = pages_ref[slot_ref[dest]]


def choose_pages(send_slot, saved_pages):
    groups = send_slot.shape[0]
    shape = (groups,) + saved_pages.shape[1:]
    return pl.pallas_call(
        choose_kernel,
        out_shape=jax.ShapeDtypeStruct(shape, saved_pages.dtype),
        in_specs=[SM, VM],
        out_specs=VM,
        compiler_params=params(),
        cost_estimate=cost(0, 2 * groups * 65536),
        name="choose_pages",
    )(send_slot, saved_pages)


def scan_kernel(
    len_ref, x_ref, z_ref, b_ref, c_ref, raw_ref, par_ref, base_ref, decay_ref, sum_ref, keep_ref
):
    tokens, channels = x_ref.shape
    heads = raw_ref.shape[0]
    width = channels // heads
    rows = lax.broadcasted_iota(jnp.int32, (tokens, tokens), 0)
    cols = lax.broadcasted_iota(jnp.int32, (tokens, tokens), 1)
    row_req = jnp.zeros((tokens, tokens), jnp.int32)
    col_req = jnp.zeros((tokens, tokens), jnp.int32)
    end = jnp.int32(0)
    last_start = jnp.int32(0)
    requests = len_ref.shape[1]
    for r in range(requests):
        last_start = end
        end = end + len_ref[0, r]
        row_req = row_req + (rows >= end).astype(jnp.int32)
        col_req = col_req + (cols >= end).astype(jnp.int32)
    same = row_req == col_req
    causal = jnp.logical_and(same, cols <= rows)
    upto = jnp.logical_and(same, rows <= cols).astype(F32)
    step = jax.nn.softplus(raw_ref[...] + par_ref[1])
    log_decay = -jnp.exp(par_ref[0]) * step
    seg = jnp.dot(
        jnp.concatenate([log_decay, log_decay], axis=0),
        upto,
        precision=lax.Precision.HIGHEST,
        preferred_element_type=F32,
    )
    both = jnp.concatenate([seg[:heads], step], axis=0)
    turned = both.T
    scores = lax.dot_general(c_ref[...], b_ref[...], NT, preferred_element_type=F32)
    x = x_ref[...]
    x_f = x.astype(F32)
    channel_head = lax.broadcasted_iota(jnp.int32, (tokens, channels), 1) // width
    mixed = jnp.zeros((tokens, channels), F32)
    reach = jnp.zeros((tokens, channels), F32)
    weight = jnp.zeros((tokens, channels), F32)
    in_last = rows[:, :1] >= last_start
    for h in range(heads):
        column = turned[:, h : h + 1]
        row = both[h : h + 1, :]
        fade = jnp.exp(jnp.where(causal, column - row, 0.0))
        mixing = jnp.where(causal, fade * scores * both[heads + h : heads + h + 1, :], 0.0)
        out = jnp.dot(mixing.astype(BF16), x, preferred_element_type=F32)
        mine = channel_head == h
        skip = par_ref[2, h : h + 1, :]
        mixed = jnp.where(mine, out + skip * x_f, mixed)
        reach = jnp.where(mine, jnp.exp(column), reach)
        tail = jnp.where(in_last, column[tokens - 1 :, :] - column, 0.0)
        tail = jnp.where(in_last, jnp.exp(tail) * turned[:, heads + h : heads + h + 1], 0.0)
        weight = jnp.where(mine, tail, weight)
    gate = jax.nn.silu(z_ref[...].astype(F32))
    base_ref[...] = mixed * gate
    decay_ref[...] = reach * gate
    high, low = split(x_f * weight)
    b = b_ref[...]
    sum_ref[...] = lax.dot_general(high, b, TN, preferred_element_type=F32) + lax.dot_general(
        low, b, TN, preferred_element_type=F32
    )
    keep_ref[...] = jnp.broadcast_to(reach[tokens - 1 :, :], (128, channels)).T


def scan_parts(lengths, x, z, b, c, raw, per_head):
    tokens, channels = x.shape
    states = b.shape[1]
    big = jax.ShapeDtypeStruct((tokens, channels), F32)
    state = jax.ShapeDtypeStruct((channels, states), F32)
    return pl.pallas_call(
        scan_kernel,
        out_shape=(big, big, state, state),
        in_specs=[SM] + [VM] * 6,
        out_specs=(VM,) * 4,
        compiler_params=params(),
        cost_estimate=cost(400_000_000, 2_000_000, 500_000),
        name="scan_parts",
    )(lengths, x, z, b, c, raw, per_head)


def ending_kernel(own_ref, res_ref, page_ref, sum_ref, keep_ref, out_ref):
    flag = (res_ref[0, 15] > 0).astype(F32)
    out_ref[...] = sum_ref[...] + keep_ref[...] * flag * page_ref[0].astype(F32)


def end_state(owners, resumed, incoming, summed, keep):
    last = owners.shape[0] - 1
    channels, states = summed.shape
    whole = pl.BlockSpec((channels, states), lambda i, own, res: (0, 0))
    return pl.pallas_call(
        ending_kernel,
        out_shape=jax.ShapeDtypeStruct((channels, states), F32),
        grid_spec=pltpu.PrefetchScalarGridSpec(
            num_scalar_prefetch=2,
            grid=(1,),
            in_specs=[
                pl.BlockSpec((1, channels, states), lambda i, own, res: (own[last], 0, 0)),
                whole,
                whole,
            ],
            out_specs=whole,
        ),
        compiler_params=params(),
        cost_estimate=cost(70_000, 400_000),
        name="end_state",
    )(owners, resumed, incoming, summed, keep)


def reads_kernel(len_ref, own_ref, res_ref, group_ref, c_ref, inc_ref, out_ref):
    c = c_ref[...]
    tokens = c.shape[0]
    token = lax.broadcasted_iota(jnp.int32, c.shape, 0)
    requests = len_ref.shape[1]
    first = (group_ref[0] == 0).astype(jnp.int32)
    total = None
    start = jnp.int32(0)
    zero = jnp.zeros_like(c)
    for r in range(0, requests, 2):
        lhs, rhs = [], []
        for k in (r, r + 1):
            size = len_ref[0, k]
            live = res_ref[0, k] if k else res_ref[0, 0] * first
            stop = start + size * live
            lhs.append(jnp.where(jnp.logical_and(token >= start, token < stop), c, zero))
            rhs.append(inc_ref[own_ref[k]])
            start = start + size
        term = lax.dot_general(
            jnp.concatenate(lhs, axis=1),
            jnp.concatenate(rhs, axis=1),
            NT,
            preferred_element_type=F32,
        )
        total = term if total is None else total + term
    out_ref[...] = total


def page_reads(lengths, owners, resumed, group, c, incoming):
    tokens = c.shape[0]
    channels = incoming.shape[1]
    return pl.pallas_call(
        reads_kernel,
        out_shape=jax.ShapeDtypeStruct((tokens, channels), F32),
        in_specs=[SM] * 4 + [VM] * 2,
        out_specs=VM,
        compiler_params=params(),
        cost_estimate=cost(300_000_000, 2_500_000),
        name="page_reads",
    )(lengths, owners, resumed, group, c, incoming)


def project_kernel(
    len_ref, group_ref, c_ref, carry_ref, reads_ref, base_ref, decay_ref, gain_ref, w_ref, out_ref
):
    c = c_ref[...]
    token = lax.broadcasted_iota(jnp.int32, c.shape, 0)
    stop = len_ref[0, 0] * (group_ref[0] > 0).astype(jnp.int32)
    first = jnp.where(token < stop, c, jnp.zeros_like(c))
    high, low = split(carry_ref[...])
    start = reads_ref[...] + lax.dot_general(first, high, NT, preferred_element_type=F32)
    start = start + lax.dot_general(first, low, NT, preferred_element_type=F32)
    gated = base_ref[...] + decay_ref[...] * start
    square = jnp.sum(gated * gated, axis=1, keepdims=True)
    weighted = (gated * gain_ref[...]).astype(BF16)
    model = w_ref.shape[1]
    out_ref[:, :model] = jnp.dot(weighted, w_ref[...], preferred_element_type=F32).astype(BF16)
    lane = lax.broadcasted_iota(jnp.int32, (c.shape[0], 128), 1)
    rounded = square.astype(BF16).astype(F32)
    pair = jnp.where(lane == 0, rounded, jnp.where(lane == 1, square - rounded, 0.0))
    out_ref[:, model:] = pair.astype(BF16)


def project(lengths, group, c, carry, reads, base, decay, gain, w):
    tokens = c.shape[0]
    model = w.shape[1]
    return pl.pallas_call(
        project_kernel,
        out_shape=jax.ShapeDtypeStruct((tokens, model + 128), BF16),
        in_specs=[SM] * 2 + [VM] * 7,
        out_specs=VM,
        compiler_params=params(),
        cost_estimate=cost(300_000_000, 3_500_000),
        name="project",
    )(lengths, group, c, carry, reads, base, decay, gain, w)


def norm_kernel(place_ref, recv_ref, res_ref, gain_ref, out_ref):
    model = res_ref.shape[1]
    total = jnp.sum(recv_ref[...].astype(F32), axis=0)
    square = total[:, model : model + 1] + total[:, model + 1 : model + 2]
    hidden = res_ref[...].astype(F32) + total[:, :model] * lax.rsqrt(square / INNER + EPS)
    factor = lax.rsqrt(jnp.mean(hidden * hidden, axis=1, keepdims=True) + EPS)
    normed = (hidden * factor * gain_ref[...]).astype(BF16)
    for k in range(out_ref.shape[0]):
        out_ref[k] = normed


def norm_rows(place, recv, residual, gain):
    parts, mine, wide = recv.shape
    model = residual.shape[1]
    return pl.pallas_call(
        norm_kernel,
        out_shape=jax.ShapeDtypeStruct((parts, mine, model), BF16),
        grid_spec=pltpu.PrefetchScalarGridSpec(
            num_scalar_prefetch=1,
            grid=(1,),
            in_specs=[
                pl.BlockSpec((parts, mine, wide), lambda i, p: (0, 0, 0)),
                pl.BlockSpec((mine, model), lambda i, p: (p[0], 0)),
                pl.BlockSpec((1, model), lambda i, p: (0, 0)),
            ],
            out_specs=pl.BlockSpec((parts, mine, model), lambda i, p: (0, 0, 0)),
        ),
        compiler_params=params(),
        cost_estimate=cost(1_000_000, 3_200_000),
        name="norm_rows",
    )(place, recv, residual, gain)


def ref_norm_kernel(x_ref, gain_ref, out_ref):
    x = x_ref[...].astype(F32)
    factor = lax.rsqrt(jnp.mean(x * x, axis=1, keepdims=True) + EPS)
    out_ref[...] = (x * factor * gain_ref[...]).astype(BF16)


def ref_norm(x, gain):
    return pl.pallas_call(
        ref_norm_kernel,
        out_shape=jax.ShapeDtypeStruct(x.shape, BF16),
        in_specs=[VM, VM],
        out_specs=VM,
        compiler_params=params(),
        cost_estimate=cost(2_000_000, 2_000_000),
        name="ref_norm",
    )(x, gain)


def score_kernel(columns, place_ref, both_ref, target_ref, head_ref, out_ref, stats):
    model = pl.program_id(0)
    tile = pl.program_id(1)
    block = head_ref.shape[3]
    groups, _, deep, _ = head_ref.shape
    head = head_ref[...].reshape(groups * deep, block)
    logits = jnp.dot(both_ref[0], head, preferred_element_type=F32)
    column = lax.broadcasted_iota(jnp.int32, logits.shape, 1) + tile * block
    inside = column < columns
    logits = jnp.where(inside, logits, -jnp.inf)
    wanted = target_ref[...][:, :1] - place_ref[0] * columns
    pick = jnp.sum(jnp.where(jnp.logical_and(column == wanted, inside), logits, 0.0), axis=1, keepdims=True)
    top = jnp.max(logits, axis=1, keepdims=True)
    lane = lax.broadcasted_iota(jnp.int32, stats.shape, 1)
    at = model * 3

    @pl.when(jnp.logical_and(model == 0, tile == 0))
    def _():
        stats[...] = jnp.zeros_like(stats)

    old = stats[...]

    def read(k):
        return jnp.sum(jnp.where(lane == at + k, old, 0.0), axis=1, keepdims=True)

    fresh = tile == 0
    old_top = jnp.where(fresh, top, read(0))
    new_top = jnp.maximum(old_top, top)
    total = read(1) * jnp.exp(old_top - new_top) + jnp.sum(jnp.exp(logits - new_top), axis=1, keepdims=True)
    picked = read(2) + pick
    new = jnp.where(lane == at, new_top, old)
    new = jnp.where(lane == at + 1, total, new)
    new = jnp.where(lane == at + 2, picked, new)
    stats[...] = new

    @pl.when(jnp.logical_and(model == 1, tile == pl.num_programs(1) - 1))
    def _():
        out_ref[...] = jnp.broadcast_to(new.T[:8, :][None], out_ref.shape)


def scores(place, both, target, heads, parts):
    groups, models, deep, columns = heads.shape
    tokens, depth = both.shape[1:]
    block = 512
    tiles = pl.cdiv(columns, block)
    return pl.pallas_call(
        functools.partial(score_kernel, columns),
        out_shape=jax.ShapeDtypeStruct((parts, 8, tokens), F32),
        grid_spec=pltpu.PrefetchScalarGridSpec(
            num_scalar_prefetch=1,
            grid=(models, tiles),
            in_specs=[
                pl.BlockSpec((1, tokens, depth), lambda m, j, p: (m, 0, 0)),
                pl.BlockSpec((tokens, 128), lambda m, j, p: (0, 0)),
                pl.BlockSpec((groups, 1, deep, block), lambda m, j, p: (0, m, 0, j)),
            ],
            out_specs=pl.BlockSpec((parts, 8, tokens), lambda m, j, p: (0, 0, 0)),
            scratch_shapes=[pltpu.VMEM((tokens, 128), F32)],
        ),
        compiler_params=params(),
        cost_estimate=cost(3_400_000_000, 15_000_000, 800_000),
        name="scores",
    )(place, both, target, heads)


def final_kernel(len_ref, recv_ref, logp_ref, sums_ref):
    recv = recv_ref[...]
    rows = []
    for k in (0, 3):
        tops = recv[:, k]
        top = jnp.max(tops, axis=0, keepdims=True)
        total = jnp.sum(recv[:, k + 1] * jnp.exp(tops - top), axis=0, keepdims=True)
        pick = jnp.sum(recv[:, k + 2], axis=0, keepdims=True)
        rows.append(pick - (top + jnp.log(total)))
    ref, policy = rows
    logp_ref[0:1, :] = policy
    logp_ref[1:2, :] = ref
    token = lax.broadcasted_iota(jnp.int32, policy.shape, 1)
    lane = lax.broadcasted_iota(jnp.int32, sums_ref.shape, 1)
    gap = policy - ref
    total = jnp.zeros(sums_ref.shape, F32)
    row = lax.broadcasted_iota(jnp.int32, sums_ref.shape, 0)
    start = jnp.int32(0)
    for r in range(len_ref.shape[1]):
        stop = start + len_ref[0, r]
        inside = jnp.logical_and(token >= start, token < stop)
        a = jnp.sum(jnp.where(inside, policy, 0.0), axis=1, keepdims=True)
        b = jnp.sum(jnp.where(inside, gap, 0.0), axis=1, keepdims=True)
        total = jnp.where(lane == r, jnp.where(row == 0, a, b), total)
        start = stop
    sums_ref[...] = total


def finish(lengths, recv):
    tokens = recv.shape[2]
    requests = lengths.shape[1]
    return pl.pallas_call(
        final_kernel,
        out_shape=(
            jax.ShapeDtypeStruct((2, tokens), F32),
            jax.ShapeDtypeStruct((2, requests), F32),
        ),
        in_specs=[SM, VM],
        out_specs=(VM, VM),
        compiler_params=params(),
        cost_estimate=cost(200_000, 150_000),
        name="finish",
    )(lengths, recv)


def from_behind(x, axis, by):
    count = lax.axis_size(axis)
    pairs = [(i, i + by) for i in range(count) if 0 <= i + by < count]
    return lax.ppermute(x, axis, pairs)


def body(
    inner_x,
    gate_z,
    state_b,
    state_c,
    step_raw,
    decay_log,
    step_bias,
    skip_gain,
    norm_gain,
    out_weight,
    residual,
    ref_hidden,
    policy_gain,
    ref_gain,
    policy_head,
    ref_head,
    saved_pages,
    lengths,
    page_owner,
    page_slot,
    resumed,
    targets,
):
    parts = lax.axis_size("vocab")
    tokens, channels = inner_x.shape
    group = lax.axis_index("grp")
    place = lax.axis_index("vocab")[None].astype(jnp.int32)
    my_group = group[None].astype(jnp.int32)

    heads = lax.all_gather(jnp.stack([ref_head, policy_head]), "grp", axis=0)

    send_slot = jnp.sum(jnp.where(page_owner == group, page_slot, 0), axis=1)
    owners = lax.dynamic_index_in_dim(page_owner, group, 0, keepdims=False)
    outgoing = choose_pages(send_slot, saved_pages)
    incoming = lax.all_to_all(outgoing, "grp", split_axis=0, concat_axis=0, tiled=True)

    per_head = jnp.broadcast_to(
        jnp.stack([decay_log, step_bias, skip_gain])[:, :, None], (3, decay_log.shape[0], tokens)
    )
    base, decay, summed, keep = scan_parts(
        lengths, inner_x, gate_z, state_b, state_c, step_raw, per_head
    )
    ref_normed = ref_norm(ref_hidden, ref_gain[None])
    target = jnp.broadcast_to(targets[:, None], (tokens, 128))

    ending = end_state(owners, resumed, incoming, summed, keep)
    carried = from_behind(ending, "grp", 1)
    reads = page_reads(lengths, owners, resumed, my_group, state_c, incoming)
    partial = project(
        lengths, my_group, state_c, carried, reads, base, decay, norm_gain[None], out_weight
    )
    recv = lax.all_to_all(
        partial.reshape(parts, tokens // parts, -1), "vocab", split_axis=0, concat_axis=0, tiled=True
    )
    mine = norm_rows(place, recv, residual, policy_gain[None])
    normed = lax.all_to_all(mine, "vocab", split_axis=0, concat_axis=0, tiled=True)
    both = jnp.stack([ref_normed, normed.reshape(tokens, -1)])
    stats = scores(place, both, target, heads, parts)
    recv = lax.all_to_all(stats, "vocab", split_axis=0, concat_axis=0, tiled=True)
    return finish(lengths, recv)


def solution(mesh):
    in_specs = (
        P("grp", "vocab"),
        P("grp", "vocab"),
        P("grp", None),
        P("grp", None),
        P("vocab", "grp"),
        P("vocab"),
        P("vocab"),
        P("vocab"),
        P("vocab"),
        P("vocab", None),
        P("grp", None),
        P("grp", None),
        P(),
        P(),
        P("grp", "vocab"),
        P("grp", "vocab"),
        P("grp", "vocab", None),
        P("grp", None),
        P(),
        P(),
        P("grp", None),
        P("grp"),
    )
    out_specs = (P(None, "grp"), P(None, "grp"))
    return jax.shard_map(body, mesh=mesh, in_specs=in_specs, out_specs=out_specs, check_vma=False)
```

```python
import functools

import jax
import jax.numpy as jnp
from jax import lax
from jax.experimental import pallas as pl
from jax.experimental.pallas import tpu as pltpu
from jax.sharding import PartitionSpec as P

INNER = 4096
EPS = 1e-05
F32 = jnp.float32
BF16 = jnp.bfloat16
NT = (((1,), (1,)), ((), ()))
TN = (((0,), (0,)), ((), ()))
VM = pl.BlockSpec(memory_space=pltpu.VMEM)
SM = pl.BlockSpec(memory_space=pltpu.SMEM)


def params(limit=48 << 20):
    return pltpu.CompilerParams(vmem_limit_bytes=limit)


def cost(flops, moved, transcendentals=0):
    return pl.CostEstimate(flops=flops, bytes_accessed=moved, transcendentals=transcendentals)


def split(value):
    high = value.astype(BF16)
    low = (value - high.astype(F32)).astype(BF16)
    return high, low


def send_kernel(groups, len_ref, own_ref, res_ref, group_ref, first_ref, c_ref, out_ref):
    reach = out_ref.shape[0]
    tokens, states = c_ref.shape
    requests = len_ref.shape[1]
    span = groups // reach
    my_x = group_ref[0] // reach
    c = c_ref[...]
    rows = out_ref.shape[1] - tokens
    sub = lax.broadcasted_iota(jnp.int32, (rows, states), 0)
    token = sub * states + lax.broadcasted_iota(jnp.int32, (rows, states), 1)
    for dest in range(reach):
        number = jnp.full((rows, states), -1, jnp.int32)
        start = jnp.int32(0)
        for r in range(requests):
            stop = start + len_ref[0, r]
            if r:
                owner = own_ref[r]
                page = (my_x - owner // reach + span) % span
                live = res_ref[0, r] > 0
            else:
                owner = first_ref[0]
                page = jnp.int32(span)
                live = jnp.logical_or(group_ref[0] > 0, res_ref[0, 0] > 0)
            hit = jnp.logical_and(owner % reach == dest, live)
            page = jnp.where(hit, page, -1)
            inside = jnp.logical_and(token >= start, token < stop)
            number = jnp.where(inside, page, number)
            start = stop
        out_ref[dest, :tokens, :] = c
        out_ref[dest, tokens:, :] = number.astype(F32).astype(BF16)


def send_rows(groups, lengths, owners, resumed, group, first_owner, c, reach):
    tokens, states = c.shape
    return pl.pallas_call(
        functools.partial(send_kernel, groups),
        out_shape=jax.ShapeDtypeStruct((reach, tokens + 16, states), BF16),
        in_specs=[SM] * 5 + [VM],
        out_specs=VM,
        compiler_params=params(),
        cost_estimate=cost(100_000, 400_000),
        name="send_rows",
    )(lengths, owners, resumed, group, first_owner, c)


def reads_kernel(table_ref, recv_ref, *refs):
    *page_refs, out_ref, pages = refs
    groups, wide, states = recv_ref.shape
    tokens = wide - 16
    count = table_ref.shape[1]
    slots = page_refs[0].shape[0]
    for k, ref in enumerate(page_refs):
        pages[k * slots : (k + 1) * slots] = ref[...]
    for j in range(groups):
        c = recv_ref[j, :tokens, :].astype(F32)
        numbers = recv_ref[j, tokens:, :].astype(F32).T
        blocks = [
            jnp.broadcast_to(numbers[:, k : k + 1], (states, states)) for k in range(tokens // states)
        ]
        number = jnp.concatenate(blocks, axis=0)
        lhs, rhs = [], []
        for s in range(count):
            lhs.append(jnp.where(number == float(s), c, 0.0).astype(BF16))
            rhs.append(pages[table_ref[j, s]])
        term = lax.dot_general(
            jnp.concatenate(lhs, axis=1),
            jnp.concatenate(rhs, axis=1),
            NT,
            preferred_element_type=F32,
        )
        out_ref[j] = term.astype(BF16)


def page_reads(table, recv, pages):
    groups = recv.shape[0]
    tokens = recv.shape[1] - 16
    slots, channels, states = pages[0].shape
    return pl.pallas_call(
        reads_kernel,
        out_shape=jax.ShapeDtypeStruct((groups, tokens, channels), BF16),
        in_specs=[SM] + [VM] * (1 + len(pages)),
        out_specs=VM,
        scratch_shapes=[pltpu.VMEM((len(pages) * slots, channels, states), BF16)],
        compiler_params=params(),
        cost_estimate=cost(700_000_000, 3_000_000),
        name="page_reads",
    )(table, recv, *pages)


def scan_kernel(
    len_ref, res_ref, x_ref, z_ref, b_ref, c_ref, raw_ref, par_ref, base_ref, decay_ref, carry_ref
):
    tokens, channels = x_ref.shape
    heads = raw_ref.shape[0]
    width = channels // heads
    rows = lax.broadcasted_iota(jnp.int32, (tokens, tokens), 0)
    cols = lax.broadcasted_iota(jnp.int32, (tokens, tokens), 1)
    row_req = jnp.zeros((tokens, tokens), jnp.int32)
    col_req = jnp.zeros((tokens, tokens), jnp.int32)
    end = jnp.int32(0)
    last_start = jnp.int32(0)
    requests = len_ref.shape[1]
    for r in range(requests):
        last_start = end
        end = end + len_ref[0, r]
        row_req = row_req + (rows >= end).astype(jnp.int32)
        col_req = col_req + (cols >= end).astype(jnp.int32)
    same = row_req == col_req
    causal = jnp.logical_and(same, cols <= rows)
    upto = jnp.logical_and(same, rows <= cols).astype(F32)
    step = jax.nn.softplus(raw_ref[...] + par_ref[1])
    log_decay = -jnp.exp(par_ref[0]) * step
    seg = jnp.dot(
        jnp.concatenate([log_decay, log_decay], axis=0),
        upto,
        precision=lax.Precision.HIGHEST,
        preferred_element_type=F32,
    )
    both = jnp.concatenate([seg[:heads], step], axis=0)
    turned = both.T
    scores = lax.dot_general(c_ref[...], b_ref[...], NT, preferred_element_type=F32)
    x = x_ref[...]
    x_f = x.astype(F32)
    channel_head = lax.broadcasted_iota(jnp.int32, (tokens, channels), 1) // width
    mixed = jnp.zeros((tokens, channels), F32)
    reach = jnp.zeros((tokens, channels), F32)
    weight = jnp.zeros((tokens, channels), F32)
    in_last = rows[:, :1] >= last_start
    for h in range(heads):
        column = turned[:, h : h + 1]
        row = both[h : h + 1, :]
        fade = jnp.exp(jnp.where(causal, column - row, 0.0))
        mixing = jnp.where(causal, fade * scores * both[heads + h : heads + h + 1, :], 0.0)
        out = jnp.dot(mixing.astype(BF16), x, preferred_element_type=F32)
        mine = channel_head == h
        skip = par_ref[2, h : h + 1, :]
        mixed = jnp.where(mine, out + skip * x_f, mixed)
        reach = jnp.where(mine, jnp.exp(column), reach)
        tail = jnp.where(in_last, column[tokens - 1 :, :] - column, 0.0)
        tail = jnp.where(in_last, jnp.exp(tail) * turned[:, heads + h : heads + h + 1], 0.0)
        weight = jnp.where(mine, tail, weight)
    gate = jax.nn.silu(z_ref[...].astype(F32))
    base_ref[...] = mixed * gate
    decay_ref[...] = reach * gate
    high, low = split(x_f * weight)
    b = b_ref[...]
    states = b.shape[1]
    carry_ref[:channels, :] = lax.dot_general(
        high, b, TN, preferred_element_type=F32
    ) + lax.dot_general(low, b, TN, preferred_element_type=F32)
    live = (res_ref[0, requests - 1] > 0).astype(F32)
    keep = reach[tokens - 1 :, :] * live
    sub = lax.broadcasted_iota(jnp.int32, (8, states), 0)
    tail = jnp.zeros((8, states), F32)
    for k in range(channels // states):
        piece = jnp.broadcast_to(keep[:, k * states : (k + 1) * states], (8, states))
        tail = jnp.where(sub == k, piece, tail)
    carry_ref[channels:, :] = tail


def scan_parts(lengths, resumed, x, z, b, c, raw, per_head):
    tokens, channels = x.shape
    states = b.shape[1]
    big = jax.ShapeDtypeStruct((tokens, channels), F32)
    return pl.pallas_call(
        scan_kernel,
        out_shape=(big, big, jax.ShapeDtypeStruct((channels + 8, states), F32)),
        in_specs=[SM] * 2 + [VM] * 6,
        out_specs=(VM,) * 3,
        compiler_params=params(),
        cost_estimate=cost(400_000_000, 2_000_000, 500_000),
        name="scan_parts",
    )(lengths, resumed, x, z, b, c, raw, per_head)


def project_kernel(
    len_ref, group_ref, c_ref, carry_ref, reads_ref, base_ref, decay_ref, gain_ref, w_ref, out_ref
):
    c = c_ref[...]
    token = lax.broadcasted_iota(jnp.int32, c.shape, 0)
    stop = len_ref[0, 0] * (group_ref[0] > 0).astype(jnp.int32)
    first = jnp.where(token < stop, c, jnp.zeros_like(c))
    tokens, channels = base_ref.shape
    states = c.shape[1]
    high, low = split(carry_ref[:channels, :])
    start = jnp.sum(reads_ref[...].astype(F32), axis=0)
    rows = [carry_ref[channels + k : channels + k + 1, :] for k in range(channels // states)]
    keep = jnp.concatenate(rows, axis=1)
    among = lax.broadcasted_iota(jnp.int32, (tokens, channels), 0) < stop
    start = jnp.where(among, start * keep, start)
    start = start + lax.dot_general(first, high, NT, preferred_element_type=F32)
    start = start + lax.dot_general(first, low, NT, preferred_element_type=F32)
    gated = base_ref[...] + decay_ref[...] * start
    square = jnp.sum(gated * gated, axis=1, keepdims=True)
    weighted = (gated * gain_ref[...]).astype(BF16)
    model = w_ref.shape[1]
    out_ref[:, :model] = jnp.dot(weighted, w_ref[...], preferred_element_type=F32).astype(BF16)
    lane = lax.broadcasted_iota(jnp.int32, (c.shape[0], 128), 1)
    rounded = square.astype(BF16).astype(F32)
    pair = jnp.where(lane == 0, rounded, jnp.where(lane == 1, square - rounded, 0.0))
    out_ref[:, model:] = pair.astype(BF16)


def project(lengths, group, c, carry, reads, base, decay, gain, w):
    tokens = c.shape[0]
    model = w.shape[1]
    return pl.pallas_call(
        project_kernel,
        out_shape=jax.ShapeDtypeStruct((tokens, model + 128), BF16),
        in_specs=[SM] * 2 + [VM] * 7,
        out_specs=VM,
        compiler_params=params(),
        cost_estimate=cost(300_000_000, 3_500_000),
        name="project",
    )(lengths, group, c, carry, reads, base, decay, gain, w)


def norm_kernel(place_ref, recv_ref, res_ref, gain_ref, out_ref):
    model = res_ref.shape[1]
    total = jnp.sum(recv_ref[...].astype(F32), axis=0)
    square = total[:, model : model + 1] + total[:, model + 1 : model + 2]
    hidden = res_ref[...].astype(F32) + total[:, :model] * lax.rsqrt(square / INNER + EPS)
    factor = lax.rsqrt(jnp.mean(hidden * hidden, axis=1, keepdims=True) + EPS)
    normed = (hidden * factor * gain_ref[...]).astype(BF16)
    for k in range(out_ref.shape[0]):
        out_ref[k] = normed


def norm_rows(place, recv, residual, gain):
    parts, mine, wide = recv.shape
    model = residual.shape[1]
    return pl.pallas_call(
        norm_kernel,
        out_shape=jax.ShapeDtypeStruct((parts, mine, model), BF16),
        grid_spec=pltpu.PrefetchScalarGridSpec(
            num_scalar_prefetch=1,
            grid=(1,),
            in_specs=[
                pl.BlockSpec((parts, mine, wide), lambda i, p: (0, 0, 0)),
                pl.BlockSpec((mine, model), lambda i, p: (p[0], 0)),
                pl.BlockSpec((1, model), lambda i, p: (0, 0)),
            ],
            out_specs=pl.BlockSpec((parts, mine, model), lambda i, p: (0, 0, 0)),
        ),
        compiler_params=params(),
        cost_estimate=cost(1_000_000, 3_200_000),
        name="norm_rows",
    )(place, recv, residual, gain)


def ref_norm_kernel(x_ref, gain_ref, out_ref):
    x = x_ref[...].astype(F32)
    factor = lax.rsqrt(jnp.mean(x * x, axis=1, keepdims=True) + EPS)
    out_ref[...] = (x * factor * gain_ref[...]).astype(BF16)


def ref_norm(x, gain):
    return pl.pallas_call(
        ref_norm_kernel,
        out_shape=jax.ShapeDtypeStruct(x.shape, BF16),
        in_specs=[VM, VM],
        out_specs=VM,
        compiler_params=params(),
        cost_estimate=cost(2_000_000, 2_000_000),
        name="ref_norm",
    )(x, gain)


def score_kernel(
    columns, tiles, place_ref, ref_ref, pol_ref, target_ref, head_ref, out_ref,
    rows, logits, tops, sums, picks, stats,
):
    step = pl.program_id(0)
    steps = pl.num_programs(0)
    groups, _, deep, block = head_ref.shape
    low = float(jnp.finfo(F32).min)

    @pl.when(step == 0)
    def _():
        rows[...] = ref_ref[...]
        stats[...] = jnp.zeros_like(stats)

    @pl.when(step == tiles)
    def _():
        rows[...] = pol_ref[...]

    @pl.when(lax.rem(step + tiles - 1, tiles) == 0)
    def _():
        tops[...] = jnp.full_like(tops, low)
        sums[...] = jnp.zeros_like(sums)
        picks[...] = jnp.zeros_like(picks)

    before = jnp.maximum(step - 1, 0)
    tile = lax.rem(before, tiles)
    head = head_ref[...].reshape(groups * deep, block)
    old_slot = lax.rem(step + 1, 2)
    wanted = target_ref[...] - place_ref[0] * columns - tile * block
    room = columns - tile * block
    lane = lax.broadcasted_iota(jnp.int32, wanted.shape, 1)
    pieces, pick = [], picks[...]
    top = tops[...]
    for k in range(block // 128):
        here = lane + k * 128
        piece = logits[old_slot, :, k * 128 : (k + 1) * 128]
        piece = jnp.where(here < room, piece, low)
        pick = pick + jnp.where(jnp.logical_and(here == wanted, here < room), piece, 0.0)
        pieces.append(piece)
        top = jnp.maximum(top, piece)
    total = sums[...] * jnp.exp(tops[...] - top)
    for piece in pieces:
        total = total + jnp.exp(piece - top)
    logits[lax.rem(step, 2)] = jnp.dot(rows[...], head, preferred_element_type=F32)
    tops[...] = top
    sums[...] = total
    picks[...] = pick

    @pl.when(jnp.logical_and(tile == tiles - 1, step > 0))
    def _():
        at = 3 * (before // tiles)
        peak = jnp.max(top, axis=1, keepdims=True)
        whole = jnp.sum(total * jnp.exp(top - peak), axis=1, keepdims=True)
        chosen = jnp.sum(pick, axis=1, keepdims=True)
        new = jnp.where(lane == at, peak, stats[...])
        new = jnp.where(lane == at + 1, whole, new)
        stats[...] = jnp.where(lane == at + 2, chosen, new)

    @pl.when(step == steps - 1)
    def _():
        out_ref[...] = jnp.broadcast_to(stats[...].T[:8, :][None], out_ref.shape)


def scores(place, ref_rows, policy_rows, target, heads, parts):
    groups, models, deep, columns = heads.shape
    tokens, depth = ref_rows.shape
    block = 512
    tiles = pl.cdiv(columns, block)
    last = models * tiles - 1
    plain = pltpu.VMEM((tokens, 128), F32)

    def head_at(i, p):
        now = jnp.minimum(i, last)
        return (0, now // tiles, 0, lax.rem(now, tiles))

    return pl.pallas_call(
        functools.partial(score_kernel, columns, tiles),
        out_shape=jax.ShapeDtypeStruct((parts, 8, tokens), F32),
        grid_spec=pltpu.PrefetchScalarGridSpec(
            num_scalar_prefetch=1,
            grid=(models * tiles + 1,),
            in_specs=[
                pl.BlockSpec((tokens, depth), lambda i, p: (0, 0)),
                pl.BlockSpec((tokens, depth), lambda i, p: (0, 0)),
                pl.BlockSpec((tokens, 128), lambda i, p: (0, 0)),
                pl.BlockSpec((groups, 1, deep, block), head_at),
            ],
            out_specs=pl.BlockSpec((parts, 8, tokens), lambda i, p: (0, 0, 0)),
            scratch_shapes=[
                pltpu.VMEM((tokens, depth), BF16),
                pltpu.VMEM((2, tokens, block), F32),
                plain,
                plain,
                plain,
                plain,
            ],
        ),
        compiler_params=params(),
        cost_estimate=cost(3_400_000_000, 15_000_000, 800_000),
        name="scores",
    )(place, ref_rows, policy_rows, target, heads)


def final_kernel(len_ref, recv_ref, logp_ref, sums_ref):
    recv = recv_ref[...]
    rows = []
    for k in (0, 3):
        tops = recv[:, k]
        top = jnp.max(tops, axis=0, keepdims=True)
        total = jnp.sum(recv[:, k + 1] * jnp.exp(tops - top), axis=0, keepdims=True)
        pick = jnp.sum(recv[:, k + 2], axis=0, keepdims=True)
        rows.append(pick - (top + jnp.log(total)))
    ref, policy = rows
    logp_ref[0:1, :] = policy
    logp_ref[1:2, :] = ref
    token = lax.broadcasted_iota(jnp.int32, policy.shape, 1)
    lane = lax.broadcasted_iota(jnp.int32, sums_ref.shape, 1)
    gap = policy - ref
    total = jnp.zeros(sums_ref.shape, F32)
    row = lax.broadcasted_iota(jnp.int32, sums_ref.shape, 0)
    start = jnp.int32(0)
    for r in range(len_ref.shape[1]):
        stop = start + len_ref[0, r]
        inside = jnp.logical_and(token >= start, token < stop)
        a = jnp.sum(jnp.where(inside, policy, 0.0), axis=1, keepdims=True)
        b = jnp.sum(jnp.where(inside, gap, 0.0), axis=1, keepdims=True)
        total = jnp.where(lane == r, jnp.where(row == 0, a, b), total)
        start = stop
    sums_ref[...] = total


def finish(lengths, recv):
    tokens = recv.shape[2]
    requests = lengths.shape[1]
    return pl.pallas_call(
        final_kernel,
        out_shape=(
            jax.ShapeDtypeStruct((2, tokens), F32),
            jax.ShapeDtypeStruct((2, requests), F32),
        ),
        in_specs=[SM, VM],
        out_specs=(VM, VM),
        compiler_params=params(),
        cost_estimate=cost(200_000, 150_000),
        name="finish",
    )(lengths, recv)


def from_behind(x, axis, by):
    count = lax.axis_size(axis)
    pairs = [(i, i + by) for i in range(count) if 0 <= i + by < count]
    return lax.ppermute(x, axis, pairs)


def body(
    inner_x,
    gate_z,
    state_b,
    state_c,
    step_raw,
    decay_log,
    step_bias,
    skip_gain,
    norm_gain,
    out_weight,
    residual,
    ref_hidden,
    policy_gain,
    ref_gain,
    policy_head,
    ref_head,
    saved_pages,
    lengths,
    page_owner,
    page_slot,
    resumed,
    targets,
):
    parts = lax.axis_size("vocab")
    tokens, channels = inner_x.shape
    groups = lax.axis_size("grp")
    slots = saved_pages.shape[0]
    group = lax.axis_index("grp")
    place = lax.axis_index("vocab")[None].astype(jnp.int32)
    my_group = group[None].astype(jnp.int32)

    ring = 8
    span = groups // ring
    lines = [[x * ring + k for k in range(ring)] for x in range(span)]
    heads = lax.all_gather(jnp.stack([ref_head, policy_head]), "grp", axis=0)

    my_x, my_z = group >> 3, group & 7
    last = page_owner.shape[1] - 1
    before_owner = jnp.concatenate([page_owner[:1, 0], page_owner[:-1, last]])
    before_slot = jnp.concatenate([page_slot[:1, 0], page_slot[:-1, last]])
    first_row = my_x * ring
    asked = lax.dynamic_slice_in_dim(page_owner, first_row, ring, 0)[:, 1:]
    asked_slot = lax.dynamic_slice_in_dim(page_slot, first_row, ring, 0)[:, 1:]
    step = jnp.arange(span, dtype=jnp.int32)
    wanted = ((my_x - step) & (span - 1)) * ring + my_z
    match = asked[:, None, :] == wanted[None, :, None]
    found = jnp.sum(jnp.where(match, asked_slot[:, None, :], 0), axis=2) + slots * step[None, :]
    first_page = ((my_x - (before_owner >> 3)) & (span - 1)) * slots + before_slot
    first_page = lax.dynamic_slice_in_dim(first_page, first_row, ring, 0)
    table = jnp.concatenate([found, first_page[:, None]], axis=1)
    owners = lax.dynamic_index_in_dim(page_owner, group, 0, keepdims=False)
    first_owner = lax.dynamic_slice_in_dim(before_owner, group, 1)

    asking = send_rows(groups, lengths, owners, resumed, my_group, first_owner, state_c, ring)
    asking = lax.all_to_all(
        asking, "grp", split_axis=0, concat_axis=0, tiled=True, axis_index_groups=lines
    )
    pages = [saved_pages]
    for k in range(1, span):
        pairs = [(i, (i + k * ring) % groups) for i in range(groups)]
        pages.append(lax.ppermute(saved_pages, "grp", pairs))
    per_head = jnp.broadcast_to(
        jnp.stack([decay_log, step_bias, skip_gain])[:, :, None], (3, decay_log.shape[0], tokens)
    )
    base, decay, ending = scan_parts(
        lengths, resumed, inner_x, gate_z, state_b, state_c, step_raw, per_head
    )
    carried = from_behind(ending, "grp", 1)
    ref_normed = ref_norm(ref_hidden, ref_gain[None])
    target = jnp.broadcast_to(targets[:, None], (tokens, 128))

    reads = page_reads(table, asking, pages)
    reads = lax.all_to_all(
        reads, "grp", split_axis=0, concat_axis=0, tiled=True, axis_index_groups=lines
    )
    partial = project(
        lengths, my_group, state_c, carried, reads, base, decay, norm_gain[None], out_weight
    )
    recv = lax.all_to_all(
        partial.reshape(parts, tokens // parts, -1), "vocab", split_axis=0, concat_axis=0, tiled=True
    )
    mine = norm_rows(place, recv, residual, policy_gain[None])
    normed = lax.all_to_all(mine, "vocab", split_axis=0, concat_axis=0, tiled=True)
    normed = normed.reshape(tokens, -1)
    stats = scores(place, ref_normed, normed, target, heads, parts)
    recv = lax.all_to_all(stats, "vocab", split_axis=0, concat_axis=0, tiled=True)
    return finish(lengths, recv)


def solution(mesh):
    in_specs = (
        P("grp", "vocab"),
        P("grp", "vocab"),
        P("grp", None),
        P("grp", None),
        P("vocab", "grp"),
        P("vocab"),
        P("vocab"),
        P("vocab"),
        P("vocab"),
        P("vocab", None),
        P("grp", None),
        P("grp", None),
        P(),
        P(),
        P("grp", "vocab"),
        P("grp", "vocab"),
        P("grp", "vocab", None),
        P("grp", None),
        P(),
        P(),
        P("grp", None),
        P("grp"),
    )
    out_specs = (P(None, "grp"), P(None, "grp"))
    return jax.shard_map(body, mesh=mesh, in_specs=in_specs, out_specs=out_specs, check_vma=False)
```

```python
import functools

import jax
import jax.numpy as jnp
from jax import lax
from jax.experimental import pallas as pl
from jax.experimental.pallas import tpu as pltpu
from jax.sharding import PartitionSpec as P

INNER = 4096
EPS = 1e-05
F32 = jnp.float32
BF16 = jnp.bfloat16
NT = (((1,), (1,)), ((), ()))
TN = (((0,), (0,)), ((), ()))


def params(limit=48 << 20):
    return pltpu.CompilerParams(vmem_limit_bytes=limit)


def cost(flops, moved, transcendentals=0):
    return pl.CostEstimate(flops=flops, bytes_accessed=moved, transcendentals=transcendentals)


def settled(x):
    return pltpu.with_memory_space_constraint(x, pltpu.HBM)


def whole(x):
    zeros = (0,) * len(x.shape)
    return pl.BlockSpec(x.shape, lambda *_: zeros)


def call(kernel, name, outs, scalars, arrays, estimate, scratch=()):
    return pl.pallas_call(
        kernel,
        out_shape=outs,
        grid_spec=pltpu.PrefetchScalarGridSpec(
            num_scalar_prefetch=len(scalars),
            grid=(1,),
            in_specs=[whole(x) for x in arrays],
            out_specs=jax.tree.map(whole, outs),
            scratch_shapes=list(scratch),
        ),
        compiler_params=params(),
        cost_estimate=estimate,
        name=name,
    )(*scalars, *arrays)


def split(value):
    high = value.astype(BF16)
    low = (value - high.astype(F32)).astype(BF16)
    return high, low


def send_kernel(own_ref, len_ref, res_ref, group_ref, core_ref, c_ref, out_ref):
    reach = out_ref.shape[0]
    tokens, states = c_ref.shape
    requests = len_ref.shape[1]
    span = own_ref.shape[0] // reach
    my_x = group_ref[0] // reach
    half = tokens // 2
    begin = pl.multiple_of(core_ref[0] * half, half)
    c = c_ref[pl.ds(begin, half)]
    shape = (out_ref.shape[1] - half, states)
    token = lax.broadcasted_iota(jnp.int32, shape, 1) + begin
    group = group_ref[0]
    number = jnp.full(shape, -1, jnp.int32)
    home = jnp.full(shape, -1, jnp.int32)
    start = jnp.int32(0)
    for r in range(requests):
        stop = start + len_ref[0, r]
        if r:
            owner = own_ref[group, r]
            page = (my_x - owner // reach + span) % span
            live = res_ref[0, r]
        else:
            behind = own_ref[jnp.maximum(group - 1, 0), requests - 1]
            owner = jnp.where(group > 0, behind, own_ref[0, 0])
            page = jnp.int32(span)
            live = jnp.where(group > 0, 1, res_ref[0, 0])
        page = jnp.where(live > 0, page, -1)
        inside = jnp.logical_and(token >= start, token < stop)
        number = jnp.where(inside, page, number)
        home = jnp.where(inside, owner % reach, home)
        start = stop
    for dest in range(reach):
        out_ref[dest, :half, :] = c
        mine = jnp.where(home == dest, number, -1)
        out_ref[dest, half:, :] = mine.astype(F32).astype(BF16)


def send_rows(page_owner, lengths, resumed, group, core, c, reach):
    tokens, states = c.shape
    return call(
        send_kernel, "send_rows", jax.ShapeDtypeStruct((reach, tokens // 2 + 16, states), BF16),
        [page_owner, lengths, resumed, group, core], [c], cost(100_000, 700_000),
    )


def after_kernel(_, pages_ref, out_ref):
    out_ref[...] = pages_ref[...]


def after(first, pages):
    return pl.pallas_call(
        after_kernel,
        out_shape=jax.ShapeDtypeStruct(pages.shape, pages.dtype),
        grid=(1,),
        in_specs=[pl.BlockSpec(memory_space=pltpu.HBM), whole(pages)],
        out_specs=whole(pages),
        compiler_params=params(),
        cost_estimate=cost(0, 500_000),
        name="after",
    )(first, pages)


def reads_kernel(table_ref, core_ref, own_ref, far_ref, *refs):
    *page_refs, out_ref, pages = refs
    groups, wide, states = own_ref.shape
    half = wide - 16
    count = table_ref.shape[1]
    slots = page_refs[0].shape[0]
    for k, ref in enumerate(page_refs):
        pages[k * slots : (k + 1) * slots] = ref[...]
    for j in range(groups):
        halves, numbers = [], []
        for ref in (own_ref, far_ref):
            halves.append(ref[j, :half, :].astype(F32))
            turned = ref[j, half:, :].astype(F32).T
            numbers.append(jnp.broadcast_to(turned[:, :1], (half, states)))
        c = jnp.concatenate(halves, axis=0)
        number = jnp.concatenate(numbers, axis=0)
        lhs, rhs = [], []
        for s in range(count):
            lhs.append(jnp.where(number == float(s), c, 0.0).astype(BF16))
            rhs.append(pages[table_ref[j, s]])
        term = lax.dot_general(
            jnp.concatenate(lhs, axis=1),
            jnp.concatenate(rhs, axis=1),
            NT,
            preferred_element_type=F32,
        )
        term = term.astype(BF16)
        out_ref[j, pl.ds(pl.multiple_of(core_ref[0] * half, half), half)] = term[:half]
        out_ref[j, pl.ds(pl.multiple_of((1 - core_ref[0]) * half, half), half)] = term[half:]


def page_reads(table, core, own, far, pages):
    groups = own.shape[0]
    tokens = 2 * (own.shape[1] - 16)
    slots, channels, states = pages[0].shape
    return call(
        reads_kernel, "page_reads", jax.ShapeDtypeStruct((groups, tokens, channels), BF16),
        [table, core], [own, far, *pages], cost(700_000_000, 3_000_000), [pltpu.VMEM((len(pages) * slots, channels, states), BF16)],
    )


def scan_kernel(
    len_ref, res_ref, x_ref, z_ref, b_ref, c_ref, raw_ref, par_ref, base_ref, decay_ref, carry_ref
):
    tokens, channels = x_ref.shape
    heads = raw_ref.shape[0]
    width = channels // heads
    rows = lax.broadcasted_iota(jnp.int32, (tokens, tokens), 0)
    cols = lax.broadcasted_iota(jnp.int32, (tokens, tokens), 1)
    row_req = jnp.zeros((tokens, tokens), jnp.int32)
    col_req = jnp.zeros((tokens, tokens), jnp.int32)
    end = jnp.int32(0)
    last_start = jnp.int32(0)
    requests = len_ref.shape[1]
    for r in range(requests):
        last_start = end
        end = end + len_ref[0, r]
        row_req = row_req + (rows >= end).astype(jnp.int32)
        col_req = col_req + (cols >= end).astype(jnp.int32)
    same = row_req == col_req
    causal = jnp.logical_and(same, cols <= rows)
    upto = jnp.logical_and(same, rows <= cols).astype(F32)
    step = jax.nn.softplus(raw_ref[...] + par_ref[1])
    log_decay = -jnp.exp(par_ref[0]) * step
    seg = jnp.dot(
        jnp.concatenate([log_decay, log_decay], axis=0),
        upto,
        precision=lax.Precision.HIGHEST,
        preferred_element_type=F32,
    )
    both = jnp.concatenate([seg[:heads], step], axis=0)
    turned = both.T
    scores = lax.dot_general(c_ref[...], b_ref[...], NT, preferred_element_type=F32)
    x = x_ref[...]
    x_f = x.astype(F32)
    channel_head = lax.broadcasted_iota(jnp.int32, (tokens, channels), 1) // width
    mixed = jnp.zeros((tokens, channels), F32)
    reach = jnp.zeros((tokens, channels), F32)
    weight = jnp.zeros((tokens, channels), F32)
    in_last = rows[:, :1] >= last_start
    for h in range(heads):
        column = turned[:, h : h + 1]
        row = both[h : h + 1, :]
        fade = jnp.exp(jnp.where(causal, column - row, 0.0))
        mixing = jnp.where(causal, fade * scores * both[heads + h : heads + h + 1, :], 0.0)
        out = jnp.dot(mixing.astype(BF16), x, preferred_element_type=F32)
        mine = channel_head == h
        skip = par_ref[2, h : h + 1, :]
        mixed = jnp.where(mine, out + skip * x_f, mixed)
        reach = jnp.where(mine, jnp.exp(column), reach)
        tail = jnp.where(in_last, column[tokens - 1 :, :] - column, 0.0)
        tail = jnp.where(in_last, jnp.exp(tail) * turned[:, heads + h : heads + h + 1], 0.0)
        weight = jnp.where(mine, tail, weight)
    gate = jax.nn.silu(z_ref[...].astype(F32))
    base_ref[...] = mixed * gate
    decay_ref[...] = reach * gate
    high, low = split(x_f * weight)
    b = b_ref[...]
    states = b.shape[1]
    carry_ref[:channels, :] = lax.dot_general(
        high, b, TN, preferred_element_type=F32
    ) + lax.dot_general(low, b, TN, preferred_element_type=F32)
    live = (res_ref[0, requests - 1] > 0).astype(F32)
    keep = reach[tokens - 1 :, :] * live
    sub = lax.broadcasted_iota(jnp.int32, (8, states), 0)
    tail = jnp.zeros((8, states), F32)
    for k in range(channels // states):
        piece = jnp.broadcast_to(keep[:, k * states : (k + 1) * states], (8, states))
        tail = jnp.where(sub == k, piece, tail)
    carry_ref[channels:, :] = tail


def scan_parts(lengths, resumed, x, z, b, c, raw, per_head):
    tokens, channels = x.shape
    states = b.shape[1]
    big = jax.ShapeDtypeStruct((tokens, channels), F32)
    return call(
        scan_kernel, "scan_parts", (big, big, jax.ShapeDtypeStruct((channels + 8, states), F32)),
        [lengths, resumed], [x, z, b, c, raw, per_head], cost(400_000_000, 2_000_000, 500_000),
    )


def project_kernel(
    len_ref, group_ref, core_ref, c_ref, carry_ref, reads_ref, base_ref, decay_ref, gain_ref, w_ref,
    send_ref, keep_ref, ready, pairs,
):
    c = c_ref[...]
    token = lax.broadcasted_iota(jnp.int32, c.shape, 0)
    stop = len_ref[0, 0] * (group_ref[0] > 0).astype(jnp.int32)
    first = jnp.where(token < stop, c, jnp.zeros_like(c))
    tokens, channels = base_ref.shape
    states = c.shape[1]
    high, low = split(carry_ref[:channels, :])
    start = jnp.sum(reads_ref[...].astype(F32), axis=0)
    rows = [carry_ref[channels + k : channels + k + 1, :] for k in range(channels // states)]
    keep = jnp.concatenate(rows, axis=1)
    among = lax.broadcasted_iota(jnp.int32, (tokens, channels), 0) < stop
    start = jnp.where(among, start * keep, start)
    start = start + lax.dot_general(first, high, NT, preferred_element_type=F32)
    start = start + lax.dot_general(first, low, NT, preferred_element_type=F32)
    gated = base_ref[...] + decay_ref[...] * start
    square = jnp.sum(gated * gated, axis=1, keepdims=True)
    weighted = (gated * gain_ref[...]).astype(BF16)
    model = w_ref.shape[1]
    lane = lax.broadcasted_iota(jnp.int32, (c.shape[0], 128), 1)
    rounded = square.astype(BF16).astype(F32)
    pair = jnp.where(lane == 0, rounded, jnp.where(lane == 1, square - rounded, 0.0))
    ready[...] = weighted
    pairs[...] = pair.astype(BF16)
    half = send_ref.shape[0]
    for out_ref, which in ((send_ref, 1 - core_ref[0]), (keep_ref, core_ref[0])):
        part = pl.ds(pl.multiple_of(which * half, half), half)
        out_ref[:, :model] = jnp.dot(ready[part], w_ref[...], preferred_element_type=F32).astype(BF16)
        out_ref[:, model:] = pairs[part]


def project(lengths, group, core, c, carry, reads, base, decay, gain, w):
    tokens, channels = base.shape
    model = w.shape[1]
    half = jax.ShapeDtypeStruct((tokens // 2, model + 128), BF16)
    return call(
        project_kernel, "project", (half, half),
        [lengths, group, core], [c, carry, reads, base, decay, gain, w], cost(300_000_000, 3_500_000), [pltpu.VMEM((tokens, channels), BF16), pltpu.VMEM((tokens, 128), BF16)],
    )


def pair_kernel(a_ref, b_ref, out_ref):
    model = a_ref.shape[1] - 128
    a, b = a_ref[...].astype(F32), b_ref[...].astype(F32)
    total = a + b
    out_ref[:, :model] = total[:, :model].astype(BF16)
    square = total[:, model : model + 1] + total[:, model + 1 : model + 2]
    lane = lax.broadcasted_iota(jnp.int32, (a.shape[0], 128), 1)
    rounded = square.astype(BF16).astype(F32)
    pair = jnp.where(lane == 0, rounded, jnp.where(lane == 1, square - rounded, 0.0))
    out_ref[:, model:] = pair.astype(BF16)


def pair_sum(a, b):
    return call(
        pair_kernel, "pair_sum", jax.ShapeDtypeStruct(a.shape, BF16),
        [], [a, b], cost(300_000, 1_700_000),
    )


def norm_kernel(place_ref, recv_ref, res_ref, gain_ref, out_ref):
    model = res_ref.shape[1]
    total = jnp.sum(recv_ref[...].astype(F32), axis=0)
    square = total[:, model : model + 1] + total[:, model + 1 : model + 2]
    hidden = res_ref[...].astype(F32) + total[:, :model] * lax.rsqrt(square / INNER + EPS)
    factor = lax.rsqrt(jnp.mean(hidden * hidden, axis=1, keepdims=True) + EPS)
    normed = (hidden * factor * gain_ref[...]).astype(BF16)
    for k in range(out_ref.shape[0]):
        out_ref[k] = normed


def norm_rows(place, recv, residual, gain):
    parts, mine, wide = recv.shape
    model = residual.shape[1]
    return pl.pallas_call(
        norm_kernel,
        out_shape=jax.ShapeDtypeStruct((parts, mine, model), BF16),
        grid_spec=pltpu.PrefetchScalarGridSpec(
            num_scalar_prefetch=1,
            grid=(1,),
            in_specs=[
                pl.BlockSpec((parts, mine, wide), lambda i, p: (0, 0, 0)),
                pl.BlockSpec((mine, model), lambda i, p: (p[0], 0)),
                pl.BlockSpec((1, model), lambda i, p: (0, 0)),
            ],
            out_specs=pl.BlockSpec((parts, mine, model), lambda i, p: (0, 0, 0)),
        ),
        compiler_params=params(),
        cost_estimate=cost(1_000_000, 3_200_000),
        name="norm_rows",
    )(place, recv, residual, gain)


def ref_norm_kernel(x_ref, gain_ref, out_ref):
    x = x_ref[...].astype(F32)
    factor = lax.rsqrt(jnp.mean(x * x, axis=1, keepdims=True) + EPS)
    out_ref[...] = (x * factor * gain_ref[...]).astype(BF16)


def ref_norm(x, gain):
    return call(
        ref_norm_kernel, "ref_norm", jax.ShapeDtypeStruct(x.shape, BF16),
        [], [x, gain], cost(2_000_000, 2_000_000),
    )


def score_kernel(
    columns, tiles, place_ref, core_ref, ref_ref, own_ref, far_ref, target_ref, head_ref, out_ref,
    rows, logits, tops, sums, picks, stats,
):
    step = pl.program_id(0)
    steps = pl.num_programs(0)
    block = head_ref.shape[1]
    low = float(jnp.finfo(F32).min)

    @pl.when(step == 0)
    def _():
        rows[...] = ref_ref[...]
        stats[...] = jnp.zeros_like(stats)

    @pl.when(step == tiles)
    def _():
        half = own_ref.shape[0]
        rows[pl.ds(pl.multiple_of(core_ref[0] * half, half), half)] = own_ref[...]
        rows[pl.ds(pl.multiple_of((1 - core_ref[0]) * half, half), half)] = far_ref[...]

    @pl.when(lax.rem(step + tiles - 1, tiles) == 0)
    def _():
        tops[...] = jnp.full_like(tops, low)
        sums[...] = jnp.zeros_like(sums)
        picks[...] = jnp.zeros_like(picks)

    before = jnp.maximum(step - 1, 0)
    tile = lax.rem(before, tiles)
    old_slot = lax.rem(step + 1, 2)
    lane = lax.broadcasted_iota(jnp.int32, target_ref.shape, 1)
    model = before // tiles
    first = model * columns
    begin = (first // block + tile) * block
    rest = max(columns - (tiles - 1) * block, 2 * columns - (columns // block + tiles - 1) * block)
    rest = (rest + 255) // 256 * 256

    def work(width):
        wanted = target_ref[...] - place_ref[0] * columns + first - begin
        floor = first - begin
        room = floor + columns
        pieces, pick = [], picks[...]
        top = tops[...]
        for k in range(block // 128):
            here = lane + k * 128
            piece = logits[old_slot, :, k * 128 : (k + 1) * 128]
            inside = jnp.logical_and(here >= floor, here < room)
            piece = jnp.where(inside, piece, low)
            pick = pick + jnp.where(jnp.logical_and(here == wanted, inside), piece, 0.0)
            pieces.append(piece)
            top = jnp.maximum(top, piece)
        total = sums[...] * jnp.exp(tops[...] - top)
        for piece in pieces:
            total = total + jnp.exp(piece - top)
        if width:
            logits[lax.rem(step, 2), :, :width] = jnp.dot(
                rows[...], head_ref[:, :width], preferred_element_type=F32
            )
        tops[...] = top
        sums[...] = total
        picks[...] = pick

    is_rest = lax.rem(step, tiles) == tiles - 1

    @pl.when(jnp.logical_and(step < steps - 1, jnp.logical_not(is_rest)))
    def _():
        work(block)

    @pl.when(jnp.logical_and(step < steps - 1, is_rest))
    def _():
        work(min(rest, block))

    @pl.when(step == steps - 1)
    def _():
        work(0)

    @pl.when(jnp.logical_and(tile == tiles - 1, step > 0))
    def _():
        at = 3 * model
        top, total, pick = tops[...], sums[...], picks[...]
        peak = jnp.max(top, axis=1, keepdims=True)
        whole = jnp.sum(total * jnp.exp(top - peak), axis=1, keepdims=True)
        chosen = jnp.sum(pick, axis=1, keepdims=True)
        new = jnp.where(lane == at, peak, stats[...])
        new = jnp.where(lane == at + 1, whole, new)
        stats[...] = jnp.where(lane == at + 2, chosen, new)

    @pl.when(step == steps - 1)
    def _():
        out_ref[...] = jnp.broadcast_to(stats[...].T[:8, :][None], out_ref.shape)


def scores(place, core, ref_rows, own_rows, far_rows, target, heads, parts):
    models, columns = 2, heads.shape[1] // 2
    tokens, depth = ref_rows.shape
    block = 512
    tiles = pl.cdiv(columns, block)
    assert pl.cdiv(2 * columns, block) - columns // block == tiles
    last = models * tiles - 1
    plain = pltpu.VMEM((tokens, 128), F32)

    def head_at(i, p, c):
        now = jnp.minimum(i, last)
        return (0, now // tiles * columns // block + lax.rem(now, tiles))

    return pl.pallas_call(
        functools.partial(score_kernel, columns, tiles),
        out_shape=jax.ShapeDtypeStruct((parts, 8, tokens), F32),
        grid_spec=pltpu.PrefetchScalarGridSpec(
            num_scalar_prefetch=2,
            grid=(models * tiles + 1,),
            in_specs=[
                pl.BlockSpec((tokens, depth), lambda i, p, c: (0, 0)),
                pl.BlockSpec((tokens // 2, depth), lambda i, p, c: (0, 0)),
                pl.BlockSpec((tokens // 2, depth), lambda i, p, c: (0, 0)),
                pl.BlockSpec((tokens, 128), lambda i, p, c: (0, 0)),
                pl.BlockSpec((depth, block), head_at),
            ],
            out_specs=pl.BlockSpec((parts, 8, tokens), lambda i, p, c: (0, 0, 0)),
            scratch_shapes=[
                pltpu.VMEM((tokens, depth), BF16),
                pltpu.VMEM((2, tokens, block), F32),
                plain,
                plain,
                plain,
                plain,
            ],
        ),
        compiler_params=params(),
        cost_estimate=cost(3_400_000_000, 15_000_000, 800_000),
        name="scores",
    )(place, core, ref_rows, own_rows, far_rows, target, heads)


def final_kernel(len_ref, recv_ref, logp_ref, sums_ref):
    recv = recv_ref[...]
    rows = []
    for k in (0, 3):
        tops = recv[:, k]
        top = jnp.max(tops, axis=0, keepdims=True)
        total = jnp.sum(recv[:, k + 1] * jnp.exp(tops - top), axis=0, keepdims=True)
        pick = jnp.sum(recv[:, k + 2], axis=0, keepdims=True)
        rows.append(pick - (top + jnp.log(total)))
    ref, policy = rows
    logp_ref[0:1, :] = policy
    logp_ref[1:2, :] = ref
    token = lax.broadcasted_iota(jnp.int32, policy.shape, 1)
    lane = lax.broadcasted_iota(jnp.int32, sums_ref.shape, 1)
    gap = policy - ref
    total = jnp.zeros(sums_ref.shape, F32)
    row = lax.broadcasted_iota(jnp.int32, sums_ref.shape, 0)
    start = jnp.int32(0)
    for r in range(len_ref.shape[1]):
        stop = start + len_ref[0, r]
        inside = jnp.logical_and(token >= start, token < stop)
        a = jnp.sum(jnp.where(inside, policy, 0.0), axis=1, keepdims=True)
        b = jnp.sum(jnp.where(inside, gap, 0.0), axis=1, keepdims=True)
        total = jnp.where(lane == r, jnp.where(row == 0, a, b), total)
        start = stop
    sums_ref[...] = total


def finish(lengths, recv):
    tokens = recv.shape[2]
    requests = lengths.shape[1]
    return call(
        final_kernel, "finish", (
            jax.ShapeDtypeStruct((2, tokens), F32),
            jax.ShapeDtypeStruct((2, requests), F32),
        ),
        [lengths], [recv], cost(200_000, 150_000),
    )


def from_behind(x, axis, by):
    count = lax.axis_size(axis)
    pairs = [(i, i + by) for i in range(count) if 0 <= i + by < count]
    return lax.ppermute(x, axis, pairs)


def body(
    inner_x,
    gate_z,
    state_b,
    state_c,
    step_raw,
    decay_log,
    step_bias,
    skip_gain,
    norm_gain,
    out_weight,
    residual,
    ref_hidden,
    policy_gain,
    ref_gain,
    policy_head,
    ref_head,
    saved_pages,
    lengths,
    page_owner,
    page_slot,
    resumed,
    targets,
):
    parts = lax.axis_size("vocab")
    tokens, channels = inner_x.shape
    inner_x, gate_z, state_b, state_c, step_raw, out_weight, residual, ref_hidden = map(
        settled, (inner_x, gate_z, state_b, state_c, step_raw, out_weight, residual, ref_hidden)
    )
    lengths, resumed = settled(lengths), settled(resumed)
    norm_gain, policy_gain, ref_gain = map(settled, (norm_gain[None], policy_gain[None], ref_gain[None]))
    groups = lax.axis_size("grp")
    slots = saved_pages.shape[0]
    group = lax.axis_index("grp")
    place = lax.axis_index("vocab")[None].astype(jnp.int32)
    my_group = group[None].astype(jnp.int32)

    core = place & 1
    other = [(i, i ^ 1) for i in range(parts)]
    ring = 8
    span = groups // ring
    lines = [[x * ring + k for k in range(ring)] for x in range(span)]
    heads = lax.all_gather(
        jnp.concatenate([ref_head, policy_head], axis=1), "grp", axis=0, tiled=True
    )

    asking = send_rows(page_owner, lengths, resumed, my_group, core, state_c, ring)
    asking, page_owner, page_slot = lax.optimization_barrier((asking, page_owner, page_slot))
    saved_pages = after(asking, settled(saved_pages))
    asking = lax.all_to_all(
        asking, "grp", split_axis=0, concat_axis=0, tiled=True, axis_index_groups=lines
    )
    far_asking = lax.ppermute(asking, "vocab", other)
    pages = [saved_pages]
    for k in range(1, span):
        pairs = [(i, (i + k * ring) % groups) for i in range(groups)]
        pages.append(lax.ppermute(saved_pages, "grp", pairs))

    my_x, my_z = group >> 3, group & 7
    last = page_owner.shape[1] - 1
    before_owner = jnp.concatenate([page_owner[:1, 0], page_owner[:-1, last]])
    before_slot = jnp.concatenate([page_slot[:1, 0], page_slot[:-1, last]])
    first_row = my_x * ring
    asked = lax.dynamic_slice_in_dim(page_owner, first_row, ring, 0)[:, 1:]
    asked_slot = lax.dynamic_slice_in_dim(page_slot, first_row, ring, 0)[:, 1:]
    step = jnp.arange(span, dtype=jnp.int32)
    wanted = ((my_x - step) & (span - 1)) * ring + my_z
    match = asked[:, None, :] == wanted[None, :, None]
    found = jnp.sum(jnp.where(match, asked_slot[:, None, :], 0), axis=2) + slots * step[None, :]
    first_page = ((my_x - (before_owner >> 3)) & (span - 1)) * slots + before_slot
    first_page = lax.dynamic_slice_in_dim(first_page, first_row, ring, 0)
    table = jnp.concatenate([found, first_page[:, None]], axis=1)

    per_head = jnp.broadcast_to(
        jnp.stack([decay_log, step_bias, skip_gain])[:, :, None], (3, decay_log.shape[0], tokens)
    )
    base, decay, ending = scan_parts(
        lengths, resumed, inner_x, gate_z, state_b, state_c, step_raw, per_head
    )
    carried = from_behind(ending, "grp", 1)
    ref_normed = ref_norm(ref_hidden, ref_gain)
    target = jnp.broadcast_to(targets[:, None], (tokens, 128))

    reads = page_reads(table, core, asking, far_asking, pages)
    reads = lax.all_to_all(
        reads, "grp", split_axis=0, concat_axis=0, tiled=True, axis_index_groups=lines
    )
    rails = [[k * 2 + c for k in range(parts // 2)] for c in range(2)]
    theirs, ours = project(
        lengths, my_group, core, state_c, carried, reads, base, decay, norm_gain, out_weight
    )
    summed = pair_sum(ours, lax.ppermute(theirs, "vocab", other))
    recv = lax.all_to_all(
        summed.reshape(parts // 2, tokens // parts, -1), "vocab",
        split_axis=0, concat_axis=0, tiled=True, axis_index_groups=rails,
    )
    mine = norm_rows(core * (parts // 2) + (place >> 1), recv, residual, policy_gain)
    normed = lax.all_to_all(
        mine, "vocab", split_axis=0, concat_axis=0, tiled=True, axis_index_groups=rails
    )
    normed = normed.reshape(tokens // 2, -1)
    far = lax.ppermute(normed, "vocab", other)
    stats = scores(place, core, ref_normed, normed, far, target, heads, parts)
    recv = lax.all_to_all(stats, "vocab", split_axis=0, concat_axis=0, tiled=True)
    return finish(lengths, recv)


def solution(mesh):
    in_specs = (
        P("grp", "vocab"),
        P("grp", "vocab"),
        P("grp", None),
        P("grp", None),
        P("vocab", "grp"),
        P("vocab"),
        P("vocab"),
        P("vocab"),
        P("vocab"),
        P("vocab", None),
        P("grp", None),
        P("grp", None),
        P(),
        P(),
        P("grp", "vocab"),
        P("grp", "vocab"),
        P("grp", "vocab", None),
        P("grp", None),
        P(),
        P(),
        P("grp", None),
        P("grp"),
    )
    out_specs = (P(None, "grp"), P(None, "grp"))
    return jax.shard_map(body, mesh=mesh, in_specs=in_specs, out_specs=out_specs, check_vma=False)
```

```python
import functools

import jax
import jax.numpy as jnp
from jax import lax
from jax.experimental import pallas as pl
from jax.experimental.pallas import tpu as pltpu
from jax.sharding import PartitionSpec as P

INNER = 4096
EPS = 1e-05
F32 = jnp.float32
BF16 = jnp.bfloat16
NT = (((1,), (1,)), ((), ()))
TN = (((0,), (0,)), ((), ()))


def params(limit=48 << 20):
    return pltpu.CompilerParams(vmem_limit_bytes=limit)


def cost(flops, moved, transcendentals=0):
    return pl.CostEstimate(flops=flops, bytes_accessed=moved, transcendentals=transcendentals)


def settled(x):
    return pltpu.with_memory_space_constraint(x, pltpu.HBM)


def whole(x):
    zeros = (0,) * len(x.shape)
    return pl.BlockSpec(x.shape, lambda *_: zeros)


def call(kernel, name, outs, scalars, arrays, estimate, scratch=()):
    return pl.pallas_call(
        kernel,
        out_shape=outs,
        grid_spec=pltpu.PrefetchScalarGridSpec(
            num_scalar_prefetch=len(scalars),
            grid=(1,),
            in_specs=[whole(x) for x in arrays],
            out_specs=jax.tree.map(whole, outs),
            scratch_shapes=list(scratch),
        ),
        compiler_params=params(),
        cost_estimate=estimate,
        name=name,
    )(*scalars, *arrays)


def split(value):
    high = value.astype(BF16)
    low = (value - high.astype(F32)).astype(BF16)
    return high, low


def send_kernel(own_ref, len_ref, res_ref, group_ref, core_ref, c_ref, out_ref):
    reach = out_ref.shape[0]
    tokens, states = c_ref.shape
    requests = len_ref.shape[1]
    span = own_ref.shape[0] // reach
    my_x = group_ref[0] // reach
    half = tokens // 2
    begin = pl.multiple_of(core_ref[0] * half, half)
    c = c_ref[pl.ds(begin, half)]
    shape = (out_ref.shape[1] - half, states)
    token = lax.broadcasted_iota(jnp.int32, shape, 1) + begin
    group = group_ref[0]
    number = jnp.full(shape, -1, jnp.int32)
    home = jnp.full(shape, -1, jnp.int32)
    start = jnp.int32(0)
    for r in range(requests):
        stop = start + len_ref[0, r]
        if r:
            owner = own_ref[group, r]
            page = (my_x - owner // reach + span) % span
            live = res_ref[0, r]
        else:
            behind = own_ref[jnp.maximum(group - 1, 0), requests - 1]
            owner = jnp.where(group > 0, behind, own_ref[0, 0])
            page = jnp.int32(span)
            live = jnp.where(group > 0, 1, res_ref[0, 0])
        page = jnp.where(live > 0, page, -1)
        inside = jnp.logical_and(token >= start, token < stop)
        number = jnp.where(inside, page, number)
        home = jnp.where(inside, owner % reach, home)
        start = stop
    for dest in range(reach):
        out_ref[dest, :half, :] = c
        mine = jnp.where(home == dest, number, -1)
        out_ref[dest, half:, :] = mine.astype(F32).astype(BF16)


def send_rows(page_owner, lengths, resumed, group, core, c, reach):
    tokens, states = c.shape
    return call(
        send_kernel, "send_rows", jax.ShapeDtypeStruct((reach, tokens // 2 + 16, states), BF16),
        [page_owner, lengths, resumed, group, core], [c], cost(100_000, 700_000),
    )


def after_kernel(_, pages_ref, out_ref):
    out_ref[...] = pages_ref[...]


def after(first, pages):
    return pl.pallas_call(
        after_kernel,
        out_shape=jax.ShapeDtypeStruct(pages.shape, pages.dtype),
        grid=(1,),
        in_specs=[pl.BlockSpec(memory_space=pltpu.HBM), whole(pages)],
        out_specs=whole(pages),
        compiler_params=params(),
        cost_estimate=cost(0, 500_000),
        name="after",
    )(first, pages)


def reads_kernel(table_ref, core_ref, own_ref, far_ref, *refs):
    *page_refs, out_ref, pages = refs
    groups, wide, states = own_ref.shape
    half = wide - 16
    count = table_ref.shape[1]
    slots = page_refs[0].shape[0]
    for k, ref in enumerate(page_refs):
        pages[k * slots : (k + 1) * slots] = ref[...]
    for j in range(groups):
        halves, numbers = [], []
        for ref in (own_ref, far_ref):
            halves.append(ref[j, :half, :].astype(F32))
            turned = ref[j, half:, :].astype(F32).T
            numbers.append(jnp.broadcast_to(turned[:, :1], (half, states)))
        c = jnp.concatenate(halves, axis=0)
        number = jnp.concatenate(numbers, axis=0)
        lhs, rhs = [], []
        for s in range(count):
            lhs.append(jnp.where(number == float(s), c, 0.0).astype(BF16))
            rhs.append(pages[table_ref[j, s]])
        term = lax.dot_general(
            jnp.concatenate(lhs, axis=1),
            jnp.concatenate(rhs, axis=1),
            NT,
            preferred_element_type=F32,
        )
        term = term.astype(BF16)
        out_ref[j, pl.ds(pl.multiple_of(core_ref[0] * half, half), half)] = term[:half]
        out_ref[j, pl.ds(pl.multiple_of((1 - core_ref[0]) * half, half), half)] = term[half:]


def page_reads(table, core, own, far, pages):
    groups = own.shape[0]
    tokens = 2 * (own.shape[1] - 16)
    slots, channels, states = pages[0].shape
    return call(
        reads_kernel, "page_reads", jax.ShapeDtypeStruct((groups, tokens, channels), BF16),
        [table, core], [own, far, *pages], cost(700_000_000, 3_000_000), [pltpu.VMEM((len(pages) * slots, channels, states), BF16)],
    )


def scan_kernel(
    len_ref, res_ref, x_ref, z_ref, b_ref, c_ref, raw_ref, par_ref, base_ref, decay_ref, carry_ref
):
    tokens, channels = x_ref.shape
    heads = raw_ref.shape[0]
    width = channels // heads
    rows = lax.broadcasted_iota(jnp.int32, (tokens, tokens), 0)
    cols = lax.broadcasted_iota(jnp.int32, (tokens, tokens), 1)
    row_req = jnp.zeros((tokens, tokens), jnp.int32)
    col_req = jnp.zeros((tokens, tokens), jnp.int32)
    end = jnp.int32(0)
    last_start = jnp.int32(0)
    requests = len_ref.shape[1]
    for r in range(requests):
        last_start = end
        end = end + len_ref[0, r]
        row_req = row_req + (rows >= end).astype(jnp.int32)
        col_req = col_req + (cols >= end).astype(jnp.int32)
    same = row_req == col_req
    causal = jnp.logical_and(same, cols <= rows)
    upto = jnp.logical_and(same, rows <= cols).astype(F32)
    step = jax.nn.softplus(raw_ref[...] + par_ref[1])
    log_decay = -jnp.exp(par_ref[0]) * step
    seg = jnp.dot(
        jnp.concatenate([log_decay, log_decay], axis=0),
        upto,
        precision=lax.Precision.HIGHEST,
        preferred_element_type=F32,
    )
    both = jnp.concatenate([seg[:heads], step], axis=0)
    turned = both.T
    scores = lax.dot_general(c_ref[...], b_ref[...], NT, preferred_element_type=F32)
    x = x_ref[...]
    x_f = x.astype(F32)
    channel_head = lax.broadcasted_iota(jnp.int32, (tokens, channels), 1) // width
    mixed = jnp.zeros((tokens, channels), F32)
    reach = jnp.zeros((tokens, channels), F32)
    weight = jnp.zeros((tokens, channels), F32)
    in_last = rows[:, :1] >= last_start
    for h in range(heads):
        column = turned[:, h : h + 1]
        row = both[h : h + 1, :]
        fade = jnp.exp(jnp.where(causal, column - row, 0.0))
        mixing = jnp.where(causal, fade * scores * both[heads + h : heads + h + 1, :], 0.0)
        out = jnp.dot(mixing.astype(BF16), x, preferred_element_type=F32)
        mine = channel_head == h
        skip = par_ref[2, h : h + 1, :]
        mixed = jnp.where(mine, out + skip * x_f, mixed)
        reach = jnp.where(mine, jnp.exp(column), reach)
        tail = jnp.where(in_last, column[tokens - 1 :, :] - column, 0.0)
        tail = jnp.where(in_last, jnp.exp(tail) * turned[:, heads + h : heads + h + 1], 0.0)
        weight = jnp.where(mine, tail, weight)
    gate = jax.nn.silu(z_ref[...].astype(F32))
    base_ref[...] = mixed * gate
    decay_ref[...] = reach * gate
    high, low = split(x_f * weight)
    b = b_ref[...]
    states = b.shape[1]
    carry_ref[:channels, :] = lax.dot_general(
        high, b, TN, preferred_element_type=F32
    ) + lax.dot_general(low, b, TN, preferred_element_type=F32)
    live = (res_ref[0, requests - 1] > 0).astype(F32)
    keep = reach[tokens - 1 :, :] * live
    sub = lax.broadcasted_iota(jnp.int32, (8, states), 0)
    tail = jnp.zeros((8, states), F32)
    for k in range(channels // states):
        piece = jnp.broadcast_to(keep[:, k * states : (k + 1) * states], (8, states))
        tail = jnp.where(sub == k, piece, tail)
    carry_ref[channels:, :] = tail


def scan_parts(lengths, resumed, x, z, b, c, raw, per_head):
    tokens, channels = x.shape
    states = b.shape[1]
    big = jax.ShapeDtypeStruct((tokens, channels), F32)
    return call(
        scan_kernel, "scan_parts", (big, big, jax.ShapeDtypeStruct((channels + 8, states), F32)),
        [lengths, resumed], [x, z, b, c, raw, per_head], cost(400_000_000, 2_000_000, 500_000),
    )


def project_kernel(
    len_ref, group_ref, core_ref, c_ref, carry_ref, reads_ref, base_ref, decay_ref, gain_ref, w_ref,
    send_ref, keep_ref, ready, pairs,
):
    c = c_ref[...]
    token = lax.broadcasted_iota(jnp.int32, c.shape, 0)
    stop = len_ref[0, 0] * (group_ref[0] > 0).astype(jnp.int32)
    first = jnp.where(token < stop, c, jnp.zeros_like(c))
    tokens, channels = base_ref.shape
    states = c.shape[1]
    high, low = split(carry_ref[:channels, :])
    start = jnp.sum(reads_ref[...].astype(F32), axis=0)
    rows = [carry_ref[channels + k : channels + k + 1, :] for k in range(channels // states)]
    keep = jnp.concatenate(rows, axis=1)
    among = lax.broadcasted_iota(jnp.int32, (tokens, channels), 0) < stop
    start = jnp.where(among, start * keep, start)
    start = start + lax.dot_general(first, high, NT, preferred_element_type=F32)
    start = start + lax.dot_general(first, low, NT, preferred_element_type=F32)
    gated = base_ref[...] + decay_ref[...] * start
    square = jnp.sum(gated * gated, axis=1, keepdims=True)
    weighted = (gated * gain_ref[...]).astype(BF16)
    model = w_ref.shape[1]
    lane = lax.broadcasted_iota(jnp.int32, (c.shape[0], 128), 1)
    rounded = square.astype(BF16).astype(F32)
    pair = jnp.where(lane == 0, rounded, jnp.where(lane == 1, square - rounded, 0.0))
    ready[...] = weighted
    pairs[...] = pair.astype(BF16)
    half = send_ref.shape[0]
    for out_ref, which in ((send_ref, 1 - core_ref[0]), (keep_ref, core_ref[0])):
        part = pl.ds(pl.multiple_of(which * half, half), half)
        out_ref[:, :model] = jnp.dot(ready[part], w_ref[...], preferred_element_type=F32).astype(BF16)
        out_ref[:, model:] = pairs[part]


def project(lengths, group, core, c, carry, reads, base, decay, gain, w):
    tokens, channels = base.shape
    model = w.shape[1]
    half = jax.ShapeDtypeStruct((tokens // 2, model + 128), BF16)
    return call(
        project_kernel, "project", (half, half),
        [lengths, group, core], [c, carry, reads, base, decay, gain, w], cost(300_000_000, 3_500_000), [pltpu.VMEM((tokens, channels), BF16), pltpu.VMEM((tokens, 128), BF16)],
    )


def pair_kernel(a_ref, b_ref, out_ref):
    model = a_ref.shape[1] - 128
    a, b = a_ref[...].astype(F32), b_ref[...].astype(F32)
    total = a + b
    out_ref[:, :model] = total[:, :model].astype(BF16)
    square = total[:, model : model + 1] + total[:, model + 1 : model + 2]
    lane = lax.broadcasted_iota(jnp.int32, (a.shape[0], 128), 1)
    rounded = square.astype(BF16).astype(F32)
    pair = jnp.where(lane == 0, rounded, jnp.where(lane == 1, square - rounded, 0.0))
    out_ref[:, model:] = pair.astype(BF16)


def pair_sum(a, b):
    return call(
        pair_kernel, "pair_sum", jax.ShapeDtypeStruct(a.shape, BF16),
        [], [a, b], cost(300_000, 1_700_000),
    )


def norm_kernel(place_ref, recv_ref, res_ref, gain_ref, out_ref):
    model = res_ref.shape[1]
    total = jnp.sum(recv_ref[...].astype(F32), axis=0)
    square = total[:, model : model + 1] + total[:, model + 1 : model + 2]
    hidden = res_ref[...].astype(F32) + total[:, :model] * lax.rsqrt(square / INNER + EPS)
    factor = lax.rsqrt(jnp.mean(hidden * hidden, axis=1, keepdims=True) + EPS)
    normed = (hidden * factor * gain_ref[...]).astype(BF16)
    for k in range(out_ref.shape[0]):
        out_ref[k] = normed


def norm_rows(place, recv, residual, gain):
    parts, mine, wide = recv.shape
    model = residual.shape[1]
    return pl.pallas_call(
        norm_kernel,
        out_shape=jax.ShapeDtypeStruct((parts, mine, model), BF16),
        grid_spec=pltpu.PrefetchScalarGridSpec(
            num_scalar_prefetch=1,
            grid=(1,),
            in_specs=[
                pl.BlockSpec((parts, mine, wide), lambda i, p: (0, 0, 0)),
                pl.BlockSpec((mine, model), lambda i, p: (p[0], 0)),
                pl.BlockSpec((1, model), lambda i, p: (0, 0)),
            ],
            out_specs=pl.BlockSpec((parts, mine, model), lambda i, p: (0, 0, 0)),
        ),
        compiler_params=params(),
        cost_estimate=cost(1_000_000, 3_200_000),
        name="norm_rows",
    )(place, recv, residual, gain)


def ref_norm_kernel(x_ref, gain_ref, out_ref):
    x = x_ref[...].astype(F32)
    factor = lax.rsqrt(jnp.mean(x * x, axis=1, keepdims=True) + EPS)
    out_ref[...] = (x * factor * gain_ref[...]).astype(BF16)


def ref_norm(x, gain):
    return call(
        ref_norm_kernel, "ref_norm", jax.ShapeDtypeStruct(x.shape, BF16),
        [], [x, gain], cost(2_000_000, 2_000_000),
    )


def score_kernel(
    columns, block, place_ref, core_ref, ref_ref, own_ref, far_ref, target_ref, head_ref, out_ref,
    head, rows, logits_a, logits_b, tops, sums, picks, sems,
):
    wide = head.shape[1]
    low = float(jnp.finfo(F32).min)
    cuts = [(c, min(c + block, wide)) for c in range(0, wide, block)]
    copies = []
    for k, (c, d) in enumerate(cuts):
        copies.append(pltpu.make_async_copy(head_ref.at[:, c:d], head.at[:, c:d], sems.at[k]))
        copies[-1].start()
    half = own_ref.shape[0]
    rows[pl.ds(pl.multiple_of(core_ref[0] * half, half), half)] = own_ref[...]
    rows[pl.ds(pl.multiple_of((1 - core_ref[0]) * half, half), half)] = far_ref[...]
    tops[...] = jnp.full_like(tops, low)
    sums[...] = jnp.zeros_like(sums)
    picks[...] = jnp.zeros_like(picks)
    jobs = []
    for model in range(2):
        first, stop = model * columns, (model + 1) * columns
        for k, (c, d) in enumerate(cuts):
            if c < stop and d > first:
                jobs.append((model, k, c, min(d, (stop + 127) // 128 * 128)))
    lane = lax.broadcasted_iota(jnp.int32, target_ref.shape, 1)
    local = target_ref[...] - place_ref[0] * columns
    local = jnp.where(jnp.logical_and(local >= 0, local < columns), local, -2 * wide)

    def statistics(job, logits):
        model, _, c, d = job
        first, stop = model * columns, (model + 1) * columns
        wanted = local + (first - c)
        old = tops[model]
        top, pick, pieces = old, picks[model], []
        for k in range((d - c) // 128):
            start = c + k * 128
            piece = logits[:, k * 128 : (k + 1) * 128]
            if start < first:
                piece = jnp.where(lane >= first - start, piece, low)
            if start + 128 > stop:
                piece = jnp.where(lane < stop - start, piece, low)
            pick = pick + jnp.where(lane == wanted - k * 128, piece, 0.0)
            pieces.append(piece)
            top = jnp.maximum(top, piece)
        total = sums[model] * jnp.exp(old - top)
        for piece in pieces:
            total = total + jnp.exp(piece - top)
        tops[model] = top
        sums[model] = total
        picks[model] = pick

    waited = set()
    for i, job in enumerate(jobs):
        model, k, c, d = job
        if k not in waited:
            copies[k].wait()
            waited.add(k)
        logits = (logits_a, logits_b)[i % 2]
        left = ref_ref if model == 0 else rows
        logits[:, : d - c] = jnp.dot(left[...], head[:, c:d], preferred_element_type=F32)
        if i:
            statistics(jobs[i - 1], (logits_a, logits_b)[(i - 1) % 2])
    statistics(jobs[-1], (logits_a, logits_b)[(len(jobs) - 1) % 2])
    stats = jnp.zeros(target_ref.shape, F32)
    for model in range(2):
        peak = jnp.max(tops[model], axis=1, keepdims=True)
        whole_sum = jnp.sum(sums[model] * jnp.exp(tops[model] - peak), axis=1, keepdims=True)
        chosen = jnp.sum(picks[model], axis=1, keepdims=True)
        stats = jnp.where(lane == 3 * model, peak, stats)
        stats = jnp.where(lane == 3 * model + 1, whole_sum, stats)
        stats = jnp.where(lane == 3 * model + 2, chosen, stats)
    out_ref[...] = jnp.broadcast_to(stats.T[:8, :][None], out_ref.shape)


def scores(place, core, ref_rows, own_rows, far_rows, target, heads, columns, parts):
    depth, wide = heads.shape
    tokens = ref_rows.shape[0]
    block = 512
    state = pltpu.VMEM((2, tokens, 128), F32)
    out = jax.ShapeDtypeStruct((parts, 8, tokens), F32)
    return pl.pallas_call(
        functools.partial(score_kernel, columns, block),
        out_shape=out,
        grid_spec=pltpu.PrefetchScalarGridSpec(
            num_scalar_prefetch=2,
            grid=(1,),
            in_specs=[whole(x) for x in (ref_rows, own_rows, far_rows, target)]
            + [pl.BlockSpec(memory_space=pltpu.HBM)],
            out_specs=whole(out),
            scratch_shapes=[
                pltpu.VMEM((depth, wide), BF16),
                pltpu.VMEM((tokens, depth), BF16),
                pltpu.VMEM((tokens, block), F32),
                pltpu.VMEM((tokens, block), F32),
                state,
                state,
                state,
                pltpu.SemaphoreType.DMA((pl.cdiv(wide, block),)),
            ],
        ),
        compiler_params=params(),
        cost_estimate=cost(3_400_000_000, 15_000_000, 800_000),
        name="scores",
    )(place, core, ref_rows, own_rows, far_rows, target, heads)


def final_kernel(len_ref, recv_ref, logp_ref, sums_ref):
    recv = recv_ref[...]
    rows = []
    for k in (0, 3):
        tops = recv[:, k]
        top = jnp.max(tops, axis=0, keepdims=True)
        total = jnp.sum(recv[:, k + 1] * jnp.exp(tops - top), axis=0, keepdims=True)
        pick = jnp.sum(recv[:, k + 2], axis=0, keepdims=True)
        rows.append(pick - (top + jnp.log(total)))
    ref, policy = rows
    logp_ref[0:1, :] = policy
    logp_ref[1:2, :] = ref
    token = lax.broadcasted_iota(jnp.int32, policy.shape, 1)
    lane = lax.broadcasted_iota(jnp.int32, sums_ref.shape, 1)
    gap = policy - ref
    total = jnp.zeros(sums_ref.shape, F32)
    row = lax.broadcasted_iota(jnp.int32, sums_ref.shape, 0)
    start = jnp.int32(0)
    for r in range(len_ref.shape[1]):
        stop = start + len_ref[0, r]
        inside = jnp.logical_and(token >= start, token < stop)
        a = jnp.sum(jnp.where(inside, policy, 0.0), axis=1, keepdims=True)
        b = jnp.sum(jnp.where(inside, gap, 0.0), axis=1, keepdims=True)
        total = jnp.where(lane == r, jnp.where(row == 0, a, b), total)
        start = stop
    sums_ref[...] = total


def finish(lengths, recv):
    tokens = recv.shape[2]
    requests = lengths.shape[1]
    return call(
        final_kernel, "finish", (
            jax.ShapeDtypeStruct((2, tokens), F32),
            jax.ShapeDtypeStruct((2, requests), F32),
        ),
        [lengths], [recv], cost(200_000, 150_000),
    )


def from_behind(x, axis, by):
    count = lax.axis_size(axis)
    pairs = [(i, i + by) for i in range(count) if 0 <= i + by < count]
    return lax.ppermute(x, axis, pairs)


def body(
    inner_x,
    gate_z,
    state_b,
    state_c,
    step_raw,
    decay_log,
    step_bias,
    skip_gain,
    norm_gain,
    out_weight,
    residual,
    ref_hidden,
    policy_gain,
    ref_gain,
    policy_head,
    ref_head,
    saved_pages,
    lengths,
    page_owner,
    page_slot,
    resumed,
    targets,
):
    parts = lax.axis_size("vocab")
    tokens, channels = inner_x.shape
    inner_x, gate_z, state_b, state_c, step_raw, out_weight, residual, ref_hidden = map(
        settled, (inner_x, gate_z, state_b, state_c, step_raw, out_weight, residual, ref_hidden)
    )
    lengths, resumed = settled(lengths), settled(resumed)
    norm_gain, policy_gain, ref_gain = map(settled, (norm_gain[None], policy_gain[None], ref_gain[None]))
    groups = lax.axis_size("grp")
    slots = saved_pages.shape[0]
    group = lax.axis_index("grp")
    place = lax.axis_index("vocab")[None].astype(jnp.int32)
    my_group = group[None].astype(jnp.int32)

    core = place & 1
    other = [(i, i ^ 1) for i in range(parts)]
    ring = 8
    span = groups // ring
    lines = [[x * ring + k for k in range(ring)] for x in range(span)]
    deep, columns = policy_head.shape
    spare = jnp.zeros((deep, -2 * columns % 128), policy_head.dtype)
    heads = lax.all_gather(
        jnp.concatenate([ref_head, policy_head, spare], axis=1), "grp", axis=0, tiled=True
    )

    asking = send_rows(page_owner, lengths, resumed, my_group, core, state_c, ring)
    asking, page_owner, page_slot = lax.optimization_barrier((asking, page_owner, page_slot))
    saved_pages = after(asking, settled(saved_pages))
    asking = lax.all_to_all(
        asking, "grp", split_axis=0, concat_axis=0, tiled=True, axis_index_groups=lines
    )
    far_asking = lax.ppermute(asking, "vocab", other)
    pages = [saved_pages]
    for k in range(1, span):
        pairs = [(i, (i + k * ring) % groups) for i in range(groups)]
        pages.append(lax.ppermute(saved_pages, "grp", pairs))

    my_x, my_z = group >> 3, group & 7
    last = page_owner.shape[1] - 1
    before_owner = jnp.concatenate([page_owner[:1, 0], page_owner[:-1, last]])
    before_slot = jnp.concatenate([page_slot[:1, 0], page_slot[:-1, last]])
    first_row = my_x * ring
    asked = lax.dynamic_slice_in_dim(page_owner, first_row, ring, 0)[:, 1:]
    asked_slot = lax.dynamic_slice_in_dim(page_slot, first_row, ring, 0)[:, 1:]
    step = jnp.arange(span, dtype=jnp.int32)
    wanted = ((my_x - step) & (span - 1)) * ring + my_z
    match = asked[:, None, :] == wanted[None, :, None]
    found = jnp.sum(jnp.where(match, asked_slot[:, None, :], 0), axis=2) + slots * step[None, :]
    first_page = ((my_x - (before_owner >> 3)) & (span - 1)) * slots + before_slot
    first_page = lax.dynamic_slice_in_dim(first_page, first_row, ring, 0)
    table = jnp.concatenate([found, first_page[:, None]], axis=1)

    per_head = jnp.broadcast_to(
        jnp.stack([decay_log, step_bias, skip_gain])[:, :, None], (3, decay_log.shape[0], tokens)
    )
    base, decay, ending = scan_parts(
        lengths, resumed, inner_x, gate_z, state_b, state_c, step_raw, per_head
    )
    carried = from_behind(ending, "grp", 1)
    ref_normed = ref_norm(ref_hidden, ref_gain)
    target = jnp.broadcast_to(targets[:, None], (tokens, 128))

    reads = page_reads(table, core, asking, far_asking, pages)
    reads = lax.all_to_all(
        reads, "grp", split_axis=0, concat_axis=0, tiled=True, axis_index_groups=lines
    )
    rails = [[k * 2 + c for k in range(parts // 2)] for c in range(2)]
    theirs, ours = project(
        lengths, my_group, core, state_c, carried, reads, base, decay, norm_gain, out_weight
    )
    summed = pair_sum(ours, lax.ppermute(theirs, "vocab", other))
    recv = lax.all_to_all(
        summed.reshape(parts // 2, tokens // parts, -1), "vocab",
        split_axis=0, concat_axis=0, tiled=True, axis_index_groups=rails,
    )
    mine = norm_rows(core * (parts // 2) + (place >> 1), recv, residual, policy_gain)
    normed = lax.all_to_all(
        mine, "vocab", split_axis=0, concat_axis=0, tiled=True, axis_index_groups=rails
    )
    normed = normed.reshape(tokens // 2, -1)
    far = lax.ppermute(normed, "vocab", other)
    stats = scores(place, core, ref_normed, normed, far, target, heads, columns, parts)
    recv = lax.all_to_all(stats, "vocab", split_axis=0, concat_axis=0, tiled=True)
    return finish(lengths, recv)


def solution(mesh):
    in_specs = (
        P("grp", "vocab"),
        P("grp", "vocab"),
        P("grp", None),
        P("grp", None),
        P("vocab", "grp"),
        P("vocab"),
        P("vocab"),
        P("vocab"),
        P("vocab"),
        P("vocab", None),
        P("grp", None),
        P("grp", None),
        P(),
        P(),
        P("grp", "vocab"),
        P("grp", "vocab"),
        P("grp", "vocab", None),
        P("grp", None),
        P(),
        P(),
        P("grp", None),
        P("grp"),
    )
    out_specs = (P(None, "grp"), P(None, "grp"))
    return jax.shard_map(body, mesh=mesh, in_specs=in_specs, out_specs=out_specs, check_vma=False)
```

```python
import functools

import jax
import jax.numpy as jnp
from jax import lax
from jax.experimental import pallas as pl
from jax.experimental.pallas import tpu as pltpu
from jax.sharding import PartitionSpec as P

INNER = 4096
EPS = 1e-05
F32 = jnp.float32
BF16 = jnp.bfloat16
NT = (((1,), (1,)), ((), ()))
TN = (((0,), (0,)), ((), ()))


def params(limit=48 << 20):
    return pltpu.CompilerParams(vmem_limit_bytes=limit)


def cost(flops, moved, transcendentals=0):
    return pl.CostEstimate(flops=flops, bytes_accessed=moved, transcendentals=transcendentals)


def settled(x):
    return pltpu.with_memory_space_constraint(x, pltpu.HBM)


def whole(x):
    zeros = (0,) * len(x.shape)
    return pl.BlockSpec(x.shape, lambda *_: zeros)


def call(kernel, name, outs, scalars, arrays, estimate, scratch=()):
    return pl.pallas_call(
        kernel,
        out_shape=outs,
        grid_spec=pltpu.PrefetchScalarGridSpec(
            num_scalar_prefetch=len(scalars),
            grid=(1,),
            in_specs=[whole(x) for x in arrays],
            out_specs=jax.tree.map(whole, outs),
            scratch_shapes=list(scratch),
        ),
        compiler_params=params(),
        cost_estimate=estimate,
        name=name,
    )(*scalars, *arrays)


def split(value):
    high = value.astype(BF16)
    low = (value - high.astype(F32)).astype(BF16)
    return high, low


def send_kernel(own_ref, len_ref, res_ref, group_ref, core_ref, c_ref, out_ref):
    reach = out_ref.shape[0]
    tokens, states = c_ref.shape
    requests = len_ref.shape[1]
    span = own_ref.shape[0] // reach
    my_x = group_ref[0] // reach
    half = tokens // 2
    begin = pl.multiple_of(core_ref[0] * half, half)
    c = c_ref[pl.ds(begin, half)]
    shape = (out_ref.shape[1] - half, states)
    token = lax.broadcasted_iota(jnp.int32, shape, 1) + begin
    group = group_ref[0]
    number = jnp.full(shape, -1, jnp.int32)
    home = jnp.full(shape, -1, jnp.int32)
    start = jnp.int32(0)
    for r in range(requests):
        stop = start + len_ref[0, r]
        if r:
            owner = own_ref[group, r]
            page = (my_x - owner // reach + span) % span
            live = res_ref[0, r]
        else:
            behind = own_ref[jnp.maximum(group - 1, 0), requests - 1]
            owner = jnp.where(group > 0, behind, own_ref[0, 0])
            page = jnp.int32(span)
            live = jnp.where(group > 0, 1, res_ref[0, 0])
        page = jnp.where(live > 0, page, -1)
        inside = jnp.logical_and(token >= start, token < stop)
        number = jnp.where(inside, page, number)
        home = jnp.where(inside, owner % reach, home)
        start = stop
    for dest in range(reach):
        out_ref[dest, :half, :] = c
        mine = jnp.where(home == dest, number, -1)
        out_ref[dest, half:, :] = mine.astype(F32).astype(BF16)


def send_rows(page_owner, lengths, resumed, group, core, c, reach):
    tokens, states = c.shape
    return call(
        send_kernel, "send_rows", jax.ShapeDtypeStruct((reach, tokens // 2 + 16, states), BF16),
        [page_owner, lengths, resumed, group, core], [c], cost(100_000, 700_000),
    )


def after_kernel(_, pages_ref, out_ref):
    out_ref[...] = pages_ref[...]


def after(first, pages):
    return pl.pallas_call(
        after_kernel,
        out_shape=jax.ShapeDtypeStruct(pages.shape, pages.dtype),
        grid=(1,),
        in_specs=[pl.BlockSpec(memory_space=pltpu.HBM), whole(pages)],
        out_specs=whole(pages),
        compiler_params=params(),
        cost_estimate=cost(0, 500_000),
        name="after",
    )(first, pages)


def reads_kernel(table_ref, core_ref, side_ref, own_ref, far_ref, *refs):
    *page_refs, keep_ref, low_ref, high_ref, pages = refs
    groups, wide, states = own_ref.shape
    half = wide - 16
    count = table_ref.shape[1]
    slots = page_refs[0].shape[0]
    for k, ref in enumerate(page_refs):
        pages[k * slots : (k + 1) * slots] = ref[...]
    split_at = low_ref.shape[2]
    for pick in range(groups):
        mine = pick % 2 == 0
        j = pick // 2 * 2 + (side_ref[0] if mine else 1 - side_ref[0])
        halves, numbers = [], []
        for ref in (own_ref, far_ref):
            halves.append(ref[j, :half, :].astype(F32))
            turned = ref[j, half:, :].astype(F32).T
            numbers.append(jnp.broadcast_to(turned[:, :1], (half, states)))
        c = jnp.concatenate(halves, axis=0)
        number = jnp.concatenate(numbers, axis=0)
        lhs, rhs = [], []
        for s in range(count):
            lhs.append(jnp.where(number == float(s), c, 0.0).astype(BF16))
            rhs.append(pages[table_ref[j, s]])
        term = lax.dot_general(
            jnp.concatenate(lhs, axis=1),
            jnp.concatenate(rhs, axis=1),
            NT,
            preferred_element_type=F32,
        ).astype(BF16)
        for part, where in ((term[:half], core_ref[0]), (term[half:], 1 - core_ref[0])):
            at = pl.ds(pl.multiple_of(where * half, half), half)
            if mine:
                keep_ref[pick // 2, at] = part
            else:
                low_ref[pick // 2, at] = part[:, :split_at]
                high_ref[pick // 2, at] = part[:, split_at:]


def page_reads(table, core, side, own, far, pages):
    groups = own.shape[0]
    tokens = 2 * (own.shape[1] - 16)
    slots, channels, states = pages[0].shape
    kept = jax.ShapeDtypeStruct((groups // 2, tokens, channels), BF16)
    sent = jax.ShapeDtypeStruct((groups // 2, tokens, channels // 2), BF16)
    return call(
        reads_kernel, "page_reads", (kept, sent, sent),
        [table, core, side], [own, far, *pages], cost(700_000_000, 3_000_000),
        [pltpu.VMEM((len(pages) * slots, channels, states), BF16)],
    )


def join_kernel(keep_ref, low_ref, high_ref, out_ref):
    at = low_ref.shape[2]
    keep = keep_ref[...].astype(F32)
    out_ref[:, :, :at] = (keep[:, :, :at] + low_ref[...].astype(F32)).astype(BF16)
    out_ref[:, :, at:] = (keep[:, :, at:] + high_ref[...].astype(F32)).astype(BF16)


def join(keep, low, high):
    return call(
        join_kernel, "join", jax.ShapeDtypeStruct(keep.shape, BF16),
        [], [keep, low, high], cost(300_000, 1_600_000),
    )


def scan_kernel(
    len_ref, res_ref, x_ref, z_ref, b_ref, c_ref, raw_ref, par_ref, base_ref, decay_ref, carry_ref
):
    tokens, channels = x_ref.shape
    heads = raw_ref.shape[0]
    width = channels // heads
    rows = lax.broadcasted_iota(jnp.int32, (tokens, tokens), 0)
    cols = lax.broadcasted_iota(jnp.int32, (tokens, tokens), 1)
    row_req = jnp.zeros((tokens, tokens), jnp.int32)
    col_req = jnp.zeros((tokens, tokens), jnp.int32)
    end = jnp.int32(0)
    last_start = jnp.int32(0)
    requests = len_ref.shape[1]
    for r in range(requests):
        last_start = end
        end = end + len_ref[0, r]
        row_req = row_req + (rows >= end).astype(jnp.int32)
        col_req = col_req + (cols >= end).astype(jnp.int32)
    same = row_req == col_req
    causal = jnp.logical_and(same, cols <= rows)
    upto = jnp.logical_and(same, rows <= cols).astype(F32)
    step = jax.nn.softplus(raw_ref[...] + par_ref[1])
    log_decay = -jnp.exp(par_ref[0]) * step
    seg = jnp.dot(
        jnp.concatenate([log_decay, log_decay], axis=0),
        upto,
        precision=lax.Precision.HIGHEST,
        preferred_element_type=F32,
    )
    both = jnp.concatenate([seg[:heads], step], axis=0)
    turned = both.T
    scores = lax.dot_general(c_ref[...], b_ref[...], NT, preferred_element_type=F32)
    x = x_ref[...]
    x_f = x.astype(F32)
    channel_head = lax.broadcasted_iota(jnp.int32, (tokens, channels), 1) // width
    mixed = jnp.zeros((tokens, channels), F32)
    reach = jnp.zeros((tokens, channels), F32)
    weight = jnp.zeros((tokens, channels), F32)
    in_last = rows[:, :1] >= last_start
    for h in range(heads):
        column = turned[:, h : h + 1]
        row = both[h : h + 1, :]
        fade = jnp.exp(jnp.where(causal, column - row, 0.0))
        mixing = jnp.where(causal, fade * scores * both[heads + h : heads + h + 1, :], 0.0)
        out = jnp.dot(mixing.astype(BF16), x, preferred_element_type=F32)
        mine = channel_head == h
        skip = par_ref[2, h : h + 1, :]
        mixed = jnp.where(mine, out + skip * x_f, mixed)
        reach = jnp.where(mine, jnp.exp(column), reach)
        tail = jnp.where(in_last, column[tokens - 1 :, :] - column, 0.0)
        tail = jnp.where(in_last, jnp.exp(tail) * turned[:, heads + h : heads + h + 1], 0.0)
        weight = jnp.where(mine, tail, weight)
    gate = jax.nn.silu(z_ref[...].astype(F32))
    base_ref[...] = mixed * gate
    decay_ref[...] = reach * gate
    high, low = split(x_f * weight)
    b = b_ref[...]
    states = b.shape[1]
    carry_ref[:channels, :] = lax.dot_general(
        high, b, TN, preferred_element_type=F32
    ) + lax.dot_general(low, b, TN, preferred_element_type=F32)
    live = (res_ref[0, requests - 1] > 0).astype(F32)
    keep = reach[tokens - 1 :, :] * live
    sub = lax.broadcasted_iota(jnp.int32, (8, states), 0)
    tail = jnp.zeros((8, states), F32)
    for k in range(channels // states):
        piece = jnp.broadcast_to(keep[:, k * states : (k + 1) * states], (8, states))
        tail = jnp.where(sub == k, piece, tail)
    carry_ref[channels:, :] = tail


def scan_parts(lengths, resumed, x, z, b, c, raw, per_head):
    tokens, channels = x.shape
    states = b.shape[1]
    big = jax.ShapeDtypeStruct((tokens, channels), F32)
    return call(
        scan_kernel, "scan_parts", (big, big, jax.ShapeDtypeStruct((channels + 8, states), F32)),
        [lengths, resumed], [x, z, b, c, raw, per_head], cost(400_000_000, 2_000_000, 500_000),
    )


def project_kernel(
    len_ref, group_ref, core_ref, c_ref, carry_ref, reads_ref, base_ref, decay_ref, gain_ref, w_ref,
    send_ref, keep_ref, ready, pairs,
):
    c = c_ref[...]
    token = lax.broadcasted_iota(jnp.int32, c.shape, 0)
    stop = len_ref[0, 0] * (group_ref[0] > 0).astype(jnp.int32)
    first = jnp.where(token < stop, c, jnp.zeros_like(c))
    tokens, channels = base_ref.shape
    states = c.shape[1]
    high, low = split(carry_ref[:channels, :])
    start = jnp.sum(reads_ref[...].astype(F32), axis=0)
    rows = [carry_ref[channels + k : channels + k + 1, :] for k in range(channels // states)]
    keep = jnp.concatenate(rows, axis=1)
    among = lax.broadcasted_iota(jnp.int32, (tokens, channels), 0) < stop
    start = jnp.where(among, start * keep, start)
    start = start + lax.dot_general(first, high, NT, preferred_element_type=F32)
    start = start + lax.dot_general(first, low, NT, preferred_element_type=F32)
    gated = base_ref[...] + decay_ref[...] * start
    square = jnp.sum(gated * gated, axis=1, keepdims=True)
    weighted = (gated * gain_ref[...]).astype(BF16)
    model = w_ref.shape[1]
    lane = lax.broadcasted_iota(jnp.int32, (c.shape[0], 128), 1)
    rounded = square.astype(BF16).astype(F32)
    pair = jnp.where(lane == 0, rounded, jnp.where(lane == 1, square - rounded, 0.0))
    ready[...] = weighted
    pairs[...] = pair.astype(BF16)
    half = send_ref.shape[0]
    for out_ref, which in ((send_ref, 1 - core_ref[0]), (keep_ref, core_ref[0])):
        part = pl.ds(pl.multiple_of(which * half, half), half)
        out_ref[:, :model] = jnp.dot(ready[part], w_ref[...], preferred_element_type=F32).astype(BF16)
        out_ref[:, model:] = pairs[part]


def project(lengths, group, core, c, carry, reads, base, decay, gain, w):
    tokens, channels = base.shape
    model = w.shape[1]
    half = jax.ShapeDtypeStruct((tokens // 2, model + 128), BF16)
    return call(
        project_kernel, "project", (half, half),
        [lengths, group, core], [c, carry, reads, base, decay, gain, w], cost(300_000_000, 3_500_000), [pltpu.VMEM((tokens, channels), BF16), pltpu.VMEM((tokens, 128), BF16)],
    )


def pair_kernel(a_ref, b_ref, out_ref):
    model = a_ref.shape[1] - 128
    a, b = a_ref[...].astype(F32), b_ref[...].astype(F32)
    total = a + b
    out_ref[:, :model] = total[:, :model].astype(BF16)
    square = total[:, model : model + 1] + total[:, model + 1 : model + 2]
    lane = lax.broadcasted_iota(jnp.int32, (a.shape[0], 128), 1)
    rounded = square.astype(BF16).astype(F32)
    pair = jnp.where(lane == 0, rounded, jnp.where(lane == 1, square - rounded, 0.0))
    out_ref[:, model:] = pair.astype(BF16)


def pair_sum(a, b):
    return call(
        pair_kernel, "pair_sum", jax.ShapeDtypeStruct(a.shape, BF16),
        [], [a, b], cost(300_000, 1_700_000),
    )


def norm_kernel(place_ref, recv_ref, res_ref, gain_ref, out_ref):
    model = res_ref.shape[1]
    total = jnp.sum(recv_ref[...].astype(F32), axis=0)
    square = total[:, model : model + 1] + total[:, model + 1 : model + 2]
    hidden = res_ref[...].astype(F32) + total[:, :model] * lax.rsqrt(square / INNER + EPS)
    factor = lax.rsqrt(jnp.mean(hidden * hidden, axis=1, keepdims=True) + EPS)
    normed = (hidden * factor * gain_ref[...]).astype(BF16)
    for k in range(out_ref.shape[0]):
        out_ref[k] = normed


def norm_rows(place, recv, residual, gain):
    parts, mine, wide = recv.shape
    model = residual.shape[1]
    return pl.pallas_call(
        norm_kernel,
        out_shape=jax.ShapeDtypeStruct((parts, mine, model), BF16),
        grid_spec=pltpu.PrefetchScalarGridSpec(
            num_scalar_prefetch=1,
            grid=(1,),
            in_specs=[
                pl.BlockSpec((parts, mine, wide), lambda i, p: (0, 0, 0)),
                pl.BlockSpec((mine, model), lambda i, p: (p[0], 0)),
                pl.BlockSpec((1, model), lambda i, p: (0, 0)),
            ],
            out_specs=pl.BlockSpec((parts, mine, model), lambda i, p: (0, 0, 0)),
        ),
        compiler_params=params(),
        cost_estimate=cost(1_000_000, 3_200_000),
        name="norm_rows",
    )(place, recv, residual, gain)


def ref_norm_kernel(x_ref, gain_ref, out_ref):
    x = x_ref[...].astype(F32)
    factor = lax.rsqrt(jnp.mean(x * x, axis=1, keepdims=True) + EPS)
    out_ref[...] = (x * factor * gain_ref[...]).astype(BF16)


def ref_norm(x, gain):
    return call(
        ref_norm_kernel, "ref_norm", jax.ShapeDtypeStruct(x.shape, BF16),
        [], [x, gain], cost(2_000_000, 2_000_000),
    )


def score_kernel(
    columns, block, place_ref, core_ref, ref_ref, own_ref, far_ref, target_ref, head_ref, out_ref,
    head, rows, logits_a, logits_b, tops, sums, picks, sems,
):
    wide = head.shape[1]
    low = float(jnp.finfo(F32).min)
    cuts = [(c, min(c + block, wide)) for c in range(0, wide, block)]
    copies = []
    for k, (c, d) in enumerate(cuts):
        copies.append(pltpu.make_async_copy(head_ref.at[:, c:d], head.at[:, c:d], sems.at[k]))
        copies[-1].start()
    half = own_ref.shape[0]
    rows[pl.ds(pl.multiple_of(core_ref[0] * half, half), half)] = own_ref[...]
    rows[pl.ds(pl.multiple_of((1 - core_ref[0]) * half, half), half)] = far_ref[...]
    tops[...] = jnp.full_like(tops, low)
    sums[...] = jnp.zeros_like(sums)
    picks[...] = jnp.zeros_like(picks)
    jobs = []
    for model in range(2):
        first, stop = model * columns, (model + 1) * columns
        for k, (c, d) in enumerate(cuts):
            if c < stop and d > first:
                jobs.append((model, k, c, min(d, (stop + 127) // 128 * 128)))
    lane = lax.broadcasted_iota(jnp.int32, target_ref.shape, 1)
    local = target_ref[...] - place_ref[0] * columns
    local = jnp.where(jnp.logical_and(local >= 0, local < columns), local, -2 * wide)

    def statistics(job, logits):
        model, _, c, d = job
        first, stop = model * columns, (model + 1) * columns
        wanted = local + (first - c)
        old = tops[model]
        top, pick, pieces = old, picks[model], []
        for k in range((d - c) // 128):
            start = c + k * 128
            piece = logits[:, k * 128 : (k + 1) * 128]
            if start < first:
                piece = jnp.where(lane >= first - start, piece, low)
            if start + 128 > stop:
                piece = jnp.where(lane < stop - start, piece, low)
            pick = pick + jnp.where(lane == wanted - k * 128, piece, 0.0)
            pieces.append(piece)
            top = jnp.maximum(top, piece)
        total = sums[model] * jnp.exp(old - top)
        for piece in pieces:
            total = total + jnp.exp(piece - top)
        tops[model] = top
        sums[model] = total
        picks[model] = pick

    waited = set()
    for i, job in enumerate(jobs):
        model, k, c, d = job
        if k not in waited:
            copies[k].wait()
            waited.add(k)
        logits = (logits_a, logits_b)[i % 2]
        left = ref_ref if model == 0 else rows
        logits[:, : d - c] = jnp.dot(left[...], head[:, c:d], preferred_element_type=F32)
        if i:
            statistics(jobs[i - 1], (logits_a, logits_b)[(i - 1) % 2])
    statistics(jobs[-1], (logits_a, logits_b)[(len(jobs) - 1) % 2])
    stats = jnp.zeros(target_ref.shape, F32)
    for model in range(2):
        peak = jnp.max(tops[model], axis=1, keepdims=True)
        whole_sum = jnp.sum(sums[model] * jnp.exp(tops[model] - peak), axis=1, keepdims=True)
        chosen = jnp.sum(picks[model], axis=1, keepdims=True)
        stats = jnp.where(lane == 3 * model, peak, stats)
        stats = jnp.where(lane == 3 * model + 1, whole_sum, stats)
        stats = jnp.where(lane == 3 * model + 2, chosen, stats)
    out_ref[...] = jnp.broadcast_to(stats.T[:8, :][None], out_ref.shape)


def scores(place, core, ref_rows, own_rows, far_rows, target, heads, columns, parts):
    depth, wide = heads.shape
    tokens = ref_rows.shape[0]
    block = 512
    state = pltpu.VMEM((2, tokens, 128), F32)
    out = jax.ShapeDtypeStruct((parts, 8, tokens), F32)
    return pl.pallas_call(
        functools.partial(score_kernel, columns, block),
        out_shape=out,
        grid_spec=pltpu.PrefetchScalarGridSpec(
            num_scalar_prefetch=2,
            grid=(1,),
            in_specs=[whole(x) for x in (ref_rows, own_rows, far_rows, target)]
            + [pl.BlockSpec(memory_space=pltpu.HBM)],
            out_specs=whole(out),
            scratch_shapes=[
                pltpu.VMEM((depth, wide), BF16),
                pltpu.VMEM((tokens, depth), BF16),
                pltpu.VMEM((tokens, block), F32),
                pltpu.VMEM((tokens, block), F32),
                state,
                state,
                state,
                pltpu.SemaphoreType.DMA((pl.cdiv(wide, block),)),
            ],
        ),
        compiler_params=params(),
        cost_estimate=cost(3_400_000_000, 15_000_000, 800_000),
        name="scores",
    )(place, core, ref_rows, own_rows, far_rows, target, heads)


def final_kernel(len_ref, recv_ref, logp_ref, sums_ref):
    recv = recv_ref[...]
    rows = []
    for k in (0, 3):
        tops = recv[:, k]
        top = jnp.max(tops, axis=0, keepdims=True)
        total = jnp.sum(recv[:, k + 1] * jnp.exp(tops - top), axis=0, keepdims=True)
        pick = jnp.sum(recv[:, k + 2], axis=0, keepdims=True)
        rows.append(pick - (top + jnp.log(total)))
    ref, policy = rows
    logp_ref[0:1, :] = policy
    logp_ref[1:2, :] = ref
    token = lax.broadcasted_iota(jnp.int32, policy.shape, 1)
    lane = lax.broadcasted_iota(jnp.int32, sums_ref.shape, 1)
    gap = policy - ref
    total = jnp.zeros(sums_ref.shape, F32)
    row = lax.broadcasted_iota(jnp.int32, sums_ref.shape, 0)
    start = jnp.int32(0)
    for r in range(len_ref.shape[1]):
        stop = start + len_ref[0, r]
        inside = jnp.logical_and(token >= start, token < stop)
        a = jnp.sum(jnp.where(inside, policy, 0.0), axis=1, keepdims=True)
        b = jnp.sum(jnp.where(inside, gap, 0.0), axis=1, keepdims=True)
        total = jnp.where(lane == r, jnp.where(row == 0, a, b), total)
        start = stop
    sums_ref[...] = total


def finish(lengths, recv):
    tokens = recv.shape[2]
    requests = lengths.shape[1]
    return call(
        final_kernel, "finish", (
            jax.ShapeDtypeStruct((2, tokens), F32),
            jax.ShapeDtypeStruct((2, requests), F32),
        ),
        [lengths], [recv], cost(200_000, 150_000),
    )


def from_behind(x, axis, by):
    count = lax.axis_size(axis)
    pairs = [(i, i + by) for i in range(count) if 0 <= i + by < count]
    return lax.ppermute(x, axis, pairs)


def body(
    inner_x,
    gate_z,
    state_b,
    state_c,
    step_raw,
    decay_log,
    step_bias,
    skip_gain,
    norm_gain,
    out_weight,
    residual,
    ref_hidden,
    policy_gain,
    ref_gain,
    policy_head,
    ref_head,
    saved_pages,
    lengths,
    page_owner,
    page_slot,
    resumed,
    targets,
):
    parts = lax.axis_size("vocab")
    tokens, channels = inner_x.shape
    inner_x, gate_z, state_b, state_c, step_raw, out_weight, residual, ref_hidden = map(
        settled, (inner_x, gate_z, state_b, state_c, step_raw, out_weight, residual, ref_hidden)
    )
    lengths, resumed = settled(lengths), settled(resumed)
    norm_gain, policy_gain, ref_gain = map(settled, (norm_gain[None], policy_gain[None], ref_gain[None]))
    groups = lax.axis_size("grp")
    slots = saved_pages.shape[0]
    group = lax.axis_index("grp")
    place = lax.axis_index("vocab")[None].astype(jnp.int32)
    my_group = group[None].astype(jnp.int32)

    core = place & 1
    other = [(i, i ^ 1) for i in range(parts)]
    ring = 8
    span = groups // ring
    lines = [[x * ring + k for k in range(ring)] for x in range(span)]
    deep, columns = policy_head.shape
    spare = jnp.zeros((deep, -2 * columns % 128), policy_head.dtype)
    heads = lax.all_gather(
        jnp.concatenate([ref_head, policy_head, spare], axis=1), "grp", axis=0, tiled=True
    )

    asking = send_rows(page_owner, lengths, resumed, my_group, core, state_c, ring)
    asking, page_owner, page_slot = lax.optimization_barrier((asking, page_owner, page_slot))
    saved_pages = after(asking, settled(saved_pages))
    asking = lax.all_to_all(
        asking, "grp", split_axis=0, concat_axis=0, tiled=True, axis_index_groups=lines
    )
    far_asking = lax.ppermute(asking, "vocab", other)
    pages = [saved_pages]
    for k in range(1, span):
        pairs = [(i, (i + k * ring) % groups) for i in range(groups)]
        pages.append(lax.ppermute(saved_pages, "grp", pairs))

    my_x, my_z = group >> 3, group & 7
    last = page_owner.shape[1] - 1
    before_owner = jnp.concatenate([page_owner[:1, 0], page_owner[:-1, last]])
    before_slot = jnp.concatenate([page_slot[:1, 0], page_slot[:-1, last]])
    first_row = my_x * ring
    asked = lax.dynamic_slice_in_dim(page_owner, first_row, ring, 0)[:, 1:]
    asked_slot = lax.dynamic_slice_in_dim(page_slot, first_row, ring, 0)[:, 1:]
    step = jnp.arange(span, dtype=jnp.int32)
    wanted = ((my_x - step) & (span - 1)) * ring + my_z
    match = asked[:, None, :] == wanted[None, :, None]
    found = jnp.sum(jnp.where(match, asked_slot[:, None, :], 0), axis=2) + slots * step[None, :]
    first_page = ((my_x - (before_owner >> 3)) & (span - 1)) * slots + before_slot
    first_page = lax.dynamic_slice_in_dim(first_page, first_row, ring, 0)
    table = jnp.concatenate([found, first_page[:, None]], axis=1)

    per_head = jnp.broadcast_to(
        jnp.stack([decay_log, step_bias, skip_gain])[:, :, None], (3, decay_log.shape[0], tokens)
    )
    base, decay, ending = scan_parts(
        lengths, resumed, inner_x, gate_z, state_b, state_c, step_raw, per_head
    )
    carried = from_behind(ending, "grp", 1)
    ref_normed = ref_norm(ref_hidden, ref_gain)
    target = jnp.broadcast_to(targets[:, None], (tokens, 128))

    keep, low, high = page_reads(table, core, my_z[None] & 1, asking, far_asking, pages)
    beside = [(x * ring + z, x * ring + (z ^ 1)) for x in range(span) for z in range(ring)]
    beyond = [
        (x * ring + z, x * ring + (z + (1 if z % 2 else ring - 1)) % ring)
        for x in range(span)
        for z in range(ring)
    ]
    reads = join(keep, lax.ppermute(low, "grp", beside), lax.ppermute(high, "grp", beyond))
    sides = [[x * ring + k for k in range(p, ring, 2)] for x in range(span) for p in range(2)]
    reads = lax.all_to_all(
        reads, "grp", split_axis=0, concat_axis=0, tiled=True, axis_index_groups=sides
    )
    rails = [[k * 2 + c for k in range(parts // 2)] for c in range(2)]
    theirs, ours = project(
        lengths, my_group, core, state_c, carried, reads, base, decay, norm_gain, out_weight
    )
    summed = pair_sum(ours, lax.ppermute(theirs, "vocab", other))
    recv = lax.all_to_all(
        summed.reshape(parts // 2, tokens // parts, -1), "vocab",
        split_axis=0, concat_axis=0, tiled=True, axis_index_groups=rails,
    )
    mine = norm_rows(core * (parts // 2) + (place >> 1), recv, residual, policy_gain)
    normed = lax.all_to_all(
        mine, "vocab", split_axis=0, concat_axis=0, tiled=True, axis_index_groups=rails
    )
    normed = normed.reshape(tokens // 2, -1)
    far = lax.ppermute(normed, "vocab", other)
    stats = scores(place, core, ref_normed, normed, far, target, heads, columns, parts)
    recv = lax.all_to_all(stats, "vocab", split_axis=0, concat_axis=0, tiled=True)
    return finish(lengths, recv)


def solution(mesh):
    in_specs = (
        P("grp", "vocab"),
        P("grp", "vocab"),
        P("grp", None),
        P("grp", None),
        P("vocab", "grp"),
        P("vocab"),
        P("vocab"),
        P("vocab"),
        P("vocab"),
        P("vocab", None),
        P("grp", None),
        P("grp", None),
        P(),
        P(),
        P("grp", "vocab"),
        P("grp", "vocab"),
        P("grp", "vocab", None),
        P("grp", None),
        P(),
        P(),
        P("grp", None),
        P("grp"),
    )
    out_specs = (P(None, "grp"), P(None, "grp"))
    return jax.shard_map(body, mesh=mesh, in_specs=in_specs, out_specs=out_specs, check_vma=False)
```

```python
import functools

import jax
import jax.numpy as jnp
from jax import lax
from jax.experimental import pallas as pl
from jax.experimental.pallas import tpu as pltpu
from jax.sharding import PartitionSpec as P

INNER = 4096
EPS = 1e-05
F32 = jnp.float32
BF16 = jnp.bfloat16
NT = (((1,), (1,)), ((), ()))
TN = (((0,), (0,)), ((), ()))


def params(limit=48 << 20):
    return pltpu.CompilerParams(vmem_limit_bytes=limit)


def cost(flops, moved, transcendentals=0):
    return pl.CostEstimate(flops=flops, bytes_accessed=moved, transcendentals=transcendentals)


def settled(x):
    return pltpu.with_memory_space_constraint(x, pltpu.HBM)


def whole(x):
    zeros = (0,) * len(x.shape)
    return pl.BlockSpec(x.shape, lambda *_: zeros)


def call(kernel, name, outs, scalars, arrays, estimate, scratch=()):
    return pl.pallas_call(
        kernel,
        out_shape=outs,
        grid_spec=pltpu.PrefetchScalarGridSpec(
            num_scalar_prefetch=len(scalars),
            grid=(1,),
            in_specs=[whole(x) for x in arrays],
            out_specs=jax.tree.map(whole, outs),
            scratch_shapes=list(scratch),
        ),
        compiler_params=params(),
        cost_estimate=estimate,
        name=name,
    )(*scalars, *arrays)


def split(value):
    high = value.astype(BF16)
    low = (value - high.astype(F32)).astype(BF16)
    return high, low


def send_kernel(own_ref, len_ref, res_ref, group_ref, core_ref, c_ref, out_ref):
    reach = out_ref.shape[0]
    tokens, states = c_ref.shape
    requests = len_ref.shape[1]
    span = own_ref.shape[0] // reach
    my_x = group_ref[0] // reach
    half = tokens // 2
    begin = pl.multiple_of(core_ref[0] * half, half)
    c = c_ref[pl.ds(begin, half)]
    shape = (out_ref.shape[1] - half, states)
    token = lax.broadcasted_iota(jnp.int32, shape, 1) + begin
    group = group_ref[0]
    number = jnp.full(shape, -1, jnp.int32)
    home = jnp.full(shape, -1, jnp.int32)
    start = jnp.int32(0)
    for r in range(requests):
        stop = start + len_ref[0, r]
        if r:
            owner = own_ref[group, r]
            page = (my_x - owner // reach + span) % span
            live = res_ref[0, r]
        else:
            behind = own_ref[jnp.maximum(group - 1, 0), requests - 1]
            owner = jnp.where(group > 0, behind, own_ref[0, 0])
            page = jnp.int32(span)
            live = jnp.where(group > 0, 1, res_ref[0, 0])
        page = jnp.where(live > 0, page, -1)
        inside = jnp.logical_and(token >= start, token < stop)
        number = jnp.where(inside, page, number)
        home = jnp.where(inside, owner % reach, home)
        start = stop
    for dest in range(reach):
        out_ref[dest, :half, :] = c
        mine = jnp.where(home == dest, number, -1)
        out_ref[dest, half:, :] = mine.astype(F32).astype(BF16)


def send_rows(page_owner, lengths, resumed, group, core, c, reach):
    tokens, states = c.shape
    return call(
        send_kernel, "send_rows", jax.ShapeDtypeStruct((reach, tokens // 2 + 16, states), BF16),
        [page_owner, lengths, resumed, group, core], [c], cost(100_000, 700_000),
    )


def after_kernel(_, pages_ref, out_ref):
    out_ref[...] = pages_ref[...]


def after(first, pages):
    return pl.pallas_call(
        after_kernel,
        out_shape=jax.ShapeDtypeStruct(pages.shape, pages.dtype),
        grid=(1,),
        in_specs=[pl.BlockSpec(memory_space=pltpu.HBM), whole(pages)],
        out_specs=whole(pages),
        compiler_params=params(),
        cost_estimate=cost(0, 500_000),
        name="after",
    )(first, pages)


def reads_kernel(table_ref, core_ref, own_ref, far_ref, *refs):
    *page_refs, out_ref, pages = refs
    groups, wide, states = own_ref.shape
    half = wide - 16
    count = table_ref.shape[1]
    slots = page_refs[0].shape[0]
    for k, ref in enumerate(page_refs):
        pages[k * slots : (k + 1) * slots] = ref[...]
    for j in range(groups):
        halves, numbers = [], []
        for ref in (own_ref, far_ref):
            halves.append(ref[j, :half, :].astype(F32))
            turned = ref[j, half:, :].astype(F32).T
            numbers.append(jnp.broadcast_to(turned[:, :1], (half, states)))
        c = jnp.concatenate(halves, axis=0)
        number = jnp.concatenate(numbers, axis=0)
        lhs, rhs = [], []
        for s in range(count):
            lhs.append(jnp.where(number == float(s), c, 0.0).astype(BF16))
            rhs.append(pages[table_ref[j, s]])
        term = lax.dot_general(
            jnp.concatenate(lhs, axis=1),
            jnp.concatenate(rhs, axis=1),
            NT,
            preferred_element_type=F32,
        )
        term = term.astype(BF16)
        out_ref[j, pl.ds(pl.multiple_of(core_ref[0] * half, half), half)] = term[:half]
        out_ref[j, pl.ds(pl.multiple_of((1 - core_ref[0]) * half, half), half)] = term[half:]


def page_reads(table, core, own, far, pages):
    groups = own.shape[0]
    tokens = 2 * (own.shape[1] - 16)
    slots, channels, states = pages[0].shape
    return call(
        reads_kernel, "page_reads", jax.ShapeDtypeStruct((groups, tokens, channels), BF16),
        [table, core], [own, far, *pages], cost(700_000_000, 3_000_000), [pltpu.VMEM((len(pages) * slots, channels, states), BF16)],
    )


def scan_kernel(
    len_ref, res_ref, x_ref, z_ref, b_ref, c_ref, raw_ref, par_ref, base_ref, decay_ref, carry_ref
):
    tokens, channels = x_ref.shape
    heads = raw_ref.shape[0]
    width = channels // heads
    rows = lax.broadcasted_iota(jnp.int32, (tokens, tokens), 0)
    cols = lax.broadcasted_iota(jnp.int32, (tokens, tokens), 1)
    row_req = jnp.zeros((tokens, tokens), jnp.int32)
    col_req = jnp.zeros((tokens, tokens), jnp.int32)
    end = jnp.int32(0)
    last_start = jnp.int32(0)
    requests = len_ref.shape[1]
    for r in range(requests):
        last_start = end
        end = end + len_ref[0, r]
        row_req = row_req + (rows >= end).astype(jnp.int32)
        col_req = col_req + (cols >= end).astype(jnp.int32)
    same = row_req == col_req
    causal = jnp.logical_and(same, cols <= rows)
    upto = jnp.logical_and(same, rows <= cols).astype(F32)
    step = jax.nn.softplus(raw_ref[...] + par_ref[1])
    log_decay = -jnp.exp(par_ref[0]) * step
    seg = jnp.dot(
        jnp.concatenate([log_decay, log_decay], axis=0),
        upto,
        precision=lax.Precision.HIGHEST,
        preferred_element_type=F32,
    )
    both = jnp.concatenate([seg[:heads], step], axis=0)
    turned = both.T
    scores = lax.dot_general(c_ref[...], b_ref[...], NT, preferred_element_type=F32)
    x = x_ref[...]
    x_f = x.astype(F32)
    channel_head = lax.broadcasted_iota(jnp.int32, (tokens, channels), 1) // width
    mixed = jnp.zeros((tokens, channels), F32)
    reach = jnp.zeros((tokens, channels), F32)
    weight = jnp.zeros((tokens, channels), F32)
    in_last = rows[:, :1] >= last_start
    for h in range(heads):
        column = turned[:, h : h + 1]
        row = both[h : h + 1, :]
        fade = jnp.exp(jnp.where(causal, column - row, 0.0))
        mixing = jnp.where(causal, fade * scores * both[heads + h : heads + h + 1, :], 0.0)
        out = jnp.dot(mixing.astype(BF16), x, preferred_element_type=F32)
        mine = channel_head == h
        skip = par_ref[2, h : h + 1, :]
        mixed = jnp.where(mine, out + skip * x_f, mixed)
        reach = jnp.where(mine, jnp.exp(column), reach)
        tail = jnp.where(in_last, column[tokens - 1 :, :] - column, 0.0)
        tail = jnp.where(in_last, jnp.exp(tail) * turned[:, heads + h : heads + h + 1], 0.0)
        weight = jnp.where(mine, tail, weight)
    gate = jax.nn.silu(z_ref[...].astype(F32))
    base_ref[...] = mixed * gate
    decay_ref[...] = reach * gate
    high, low = split(x_f * weight)
    b = b_ref[...]
    states = b.shape[1]
    carry_ref[:channels, :] = lax.dot_general(
        high, b, TN, preferred_element_type=F32
    ) + lax.dot_general(low, b, TN, preferred_element_type=F32)
    live = (res_ref[0, requests - 1] > 0).astype(F32)
    keep = reach[tokens - 1 :, :] * live
    sub = lax.broadcasted_iota(jnp.int32, (8, states), 0)
    tail = jnp.zeros((8, states), F32)
    for k in range(channels // states):
        piece = jnp.broadcast_to(keep[:, k * states : (k + 1) * states], (8, states))
        tail = jnp.where(sub == k, piece, tail)
    carry_ref[channels:, :] = tail


def scan_parts(lengths, resumed, x, z, b, c, raw, per_head):
    tokens, channels = x.shape
    states = b.shape[1]
    big = jax.ShapeDtypeStruct((tokens, channels), F32)
    return call(
        scan_kernel, "scan_parts", (big, big, jax.ShapeDtypeStruct((channels + 8, states), F32)),
        [lengths, resumed], [x, z, b, c, raw, per_head], cost(400_000_000, 2_000_000, 500_000),
    )


def project_kernel(
    len_ref, group_ref, core_ref, c_ref, carry_ref, reads_ref, base_ref, decay_ref, gain_ref, w_ref,
    send_ref, keep_ref, ready, pairs,
):
    c = c_ref[...]
    token = lax.broadcasted_iota(jnp.int32, c.shape, 0)
    stop = len_ref[0, 0] * (group_ref[0] > 0).astype(jnp.int32)
    first = jnp.where(token < stop, c, jnp.zeros_like(c))
    tokens, channels = base_ref.shape
    states = c.shape[1]
    high, low = split(carry_ref[:channels, :])
    start = jnp.sum(reads_ref[...].astype(F32), axis=0)
    rows = [carry_ref[channels + k : channels + k + 1, :] for k in range(channels // states)]
    keep = jnp.concatenate(rows, axis=1)
    among = lax.broadcasted_iota(jnp.int32, (tokens, channels), 0) < stop
    start = jnp.where(among, start * keep, start)
    start = start + lax.dot_general(first, high, NT, preferred_element_type=F32)
    start = start + lax.dot_general(first, low, NT, preferred_element_type=F32)
    gated = base_ref[...] + decay_ref[...] * start
    square = jnp.sum(gated * gated, axis=1, keepdims=True)
    weighted = (gated * gain_ref[...]).astype(BF16)
    model = w_ref.shape[1]
    lane = lax.broadcasted_iota(jnp.int32, (c.shape[0], 128), 1)
    rounded = square.astype(BF16).astype(F32)
    pair = jnp.where(lane == 0, rounded, jnp.where(lane == 1, square - rounded, 0.0))
    ready[...] = weighted
    pairs[...] = pair.astype(BF16)
    half = send_ref.shape[0]
    for out_ref, which in ((send_ref, 1 - core_ref[0]), (keep_ref, core_ref[0])):
        part = pl.ds(pl.multiple_of(which * half, half), half)
        out_ref[:, :model] = jnp.dot(ready[part], w_ref[...], preferred_element_type=F32).astype(BF16)
        out_ref[:, model:] = pairs[part]


def project(lengths, group, core, c, carry, reads, base, decay, gain, w):
    tokens, channels = base.shape
    model = w.shape[1]
    half = jax.ShapeDtypeStruct((tokens // 2, model + 128), BF16)
    return call(
        project_kernel, "project", (half, half),
        [lengths, group, core], [c, carry, reads, base, decay, gain, w], cost(300_000_000, 3_500_000), [pltpu.VMEM((tokens, channels), BF16), pltpu.VMEM((tokens, 128), BF16)],
    )


def pair_kernel(a_ref, b_ref, out_ref):
    model = a_ref.shape[1] - 128
    a, b = a_ref[...].astype(F32), b_ref[...].astype(F32)
    total = a + b
    out_ref[:, :model] = total[:, :model].astype(BF16)
    square = total[:, model : model + 1] + total[:, model + 1 : model + 2]
    lane = lax.broadcasted_iota(jnp.int32, (a.shape[0], 128), 1)
    rounded = square.astype(BF16).astype(F32)
    pair = jnp.where(lane == 0, rounded, jnp.where(lane == 1, square - rounded, 0.0))
    out_ref[:, model:] = pair.astype(BF16)


def pair_sum(a, b):
    return call(
        pair_kernel, "pair_sum", jax.ShapeDtypeStruct(a.shape, BF16),
        [], [a, b], cost(300_000, 1_700_000),
    )


def norm_kernel(place_ref, recv_ref, res_ref, gain_ref, out_ref):
    model = res_ref.shape[1]
    total = jnp.sum(recv_ref[...].astype(F32), axis=0)
    square = total[:, model : model + 1] + total[:, model + 1 : model + 2]
    hidden = res_ref[...].astype(F32) + total[:, :model] * lax.rsqrt(square / INNER + EPS)
    factor = lax.rsqrt(jnp.mean(hidden * hidden, axis=1, keepdims=True) + EPS)
    normed = (hidden * factor * gain_ref[...]).astype(BF16)
    for k in range(out_ref.shape[0]):
        out_ref[k] = normed


def norm_rows(place, recv, residual, gain):
    parts, mine, wide = recv.shape
    model = residual.shape[1]
    return pl.pallas_call(
        norm_kernel,
        out_shape=jax.ShapeDtypeStruct((parts, mine, model), BF16),
        grid_spec=pltpu.PrefetchScalarGridSpec(
            num_scalar_prefetch=1,
            grid=(1,),
            in_specs=[
                pl.BlockSpec((parts, mine, wide), lambda i, p: (0, 0, 0)),
                pl.BlockSpec((mine, model), lambda i, p: (p[0], 0)),
                pl.BlockSpec((1, model), lambda i, p: (0, 0)),
            ],
            out_specs=pl.BlockSpec((parts, mine, model), lambda i, p: (0, 0, 0)),
        ),
        compiler_params=params(),
        cost_estimate=cost(1_000_000, 3_200_000),
        name="norm_rows",
    )(place, recv, residual, gain)


def ref_norm_kernel(x_ref, gain_ref, out_ref):
    x = x_ref[...].astype(F32)
    factor = lax.rsqrt(jnp.mean(x * x, axis=1, keepdims=True) + EPS)
    out_ref[...] = (x * factor * gain_ref[...]).astype(BF16)


def ref_norm(x, gain):
    return call(
        ref_norm_kernel, "ref_norm", jax.ShapeDtypeStruct(x.shape, BF16),
        [], [x, gain], cost(2_000_000, 2_000_000),
    )


def score_kernel(
    columns, block, place_ref, core_ref, ref_ref, own_ref, far_ref, target_ref, head_ref, out_ref,
    head, rows, logits_a, logits_b, tops, sums, picks, sems,
):
    wide = head.shape[1]
    low = float(jnp.finfo(F32).min)
    ends = [0, *range(block // 2, wide, block), wide]
    cuts = list(zip(ends[:-1], ends[1:]))
    copies = []
    for k, (c, d) in enumerate(cuts):
        copies.append(pltpu.make_async_copy(head_ref.at[:, c:d], head.at[:, c:d], sems.at[k]))
        copies[-1].start()
    half = own_ref.shape[0]
    rows[pl.ds(pl.multiple_of(core_ref[0] * half, half), half)] = own_ref[...]
    rows[pl.ds(pl.multiple_of((1 - core_ref[0]) * half, half), half)] = far_ref[...]
    tops[...] = jnp.full_like(tops, low)
    sums[...] = jnp.zeros_like(sums)
    picks[...] = jnp.zeros_like(picks)
    jobs = []
    for model in range(2):
        first, stop = model * columns, (model + 1) * columns
        found = []
        for k, (c, d) in enumerate(cuts):
            if c < stop and d > first:
                found.append((model, k, max(c, first // 128 * 128), min(d, (stop + 127) // 128 * 128)))
        jobs += found if model == 0 else found[1:] + found[:1]
    lane = lax.broadcasted_iota(jnp.int32, target_ref.shape, 1)
    local = target_ref[...] - place_ref[0] * columns
    local = jnp.where(jnp.logical_and(local >= 0, local < columns), local, -2 * wide)

    def statistics(job, logits):
        model, _, c, d = job
        first, stop = model * columns, (model + 1) * columns
        wanted = local + (first - c)
        old = tops[model]
        top, pick, pieces = old, picks[model], []
        for k in range((d - c) // 128):
            start = c + k * 128
            piece = logits[:, k * 128 : (k + 1) * 128]
            if start < first:
                piece = jnp.where(lane >= first - start, piece, low)
            if start + 128 > stop:
                piece = jnp.where(lane < stop - start, piece, low)
            pick = pick + jnp.where(lane == wanted - k * 128, piece, 0.0)
            pieces.append(piece)
            top = jnp.maximum(top, piece)
        total = sums[model] * jnp.exp(old - top)
        for piece in pieces:
            total = total + jnp.exp(piece - top)
        tops[model] = top
        sums[model] = total
        picks[model] = pick

    waited = set()
    for i, job in enumerate(jobs):
        model, k, c, d = job
        if k not in waited:
            copies[k].wait()
            waited.add(k)
        logits = (logits_a, logits_b)[i % 2]
        left = ref_ref if model == 0 else rows
        logits[:, : d - c] = jnp.dot(left[...], head[:, c:d], preferred_element_type=F32)
        if i:
            statistics(jobs[i - 1], (logits_a, logits_b)[(i - 1) % 2])
    statistics(jobs[-1], (logits_a, logits_b)[(len(jobs) - 1) % 2])
    stats = jnp.zeros(target_ref.shape, F32)
    for model in range(2):
        peak = jnp.max(tops[model], axis=1, keepdims=True)
        whole_sum = jnp.sum(sums[model] * jnp.exp(tops[model] - peak), axis=1, keepdims=True)
        chosen = jnp.sum(picks[model], axis=1, keepdims=True)
        stats = jnp.where(lane == 3 * model, peak, stats)
        stats = jnp.where(lane == 3 * model + 1, whole_sum, stats)
        stats = jnp.where(lane == 3 * model + 2, chosen, stats)
    out_ref[...] = jnp.broadcast_to(stats.T[:8, :][None], out_ref.shape)


def scores(place, core, ref_rows, own_rows, far_rows, target, heads, columns, parts):
    depth, wide = heads.shape
    tokens = ref_rows.shape[0]
    block = 512
    state = pltpu.VMEM((2, tokens, 128), F32)
    out = jax.ShapeDtypeStruct((parts, 8, tokens), F32)
    return pl.pallas_call(
        functools.partial(score_kernel, columns, block),
        out_shape=out,
        grid_spec=pltpu.PrefetchScalarGridSpec(
            num_scalar_prefetch=2,
            grid=(1,),
            in_specs=[whole(x) for x in (ref_rows, own_rows, far_rows, target)]
            + [pl.BlockSpec(memory_space=pltpu.HBM)],
            out_specs=whole(out),
            scratch_shapes=[
                pltpu.VMEM((depth, wide), BF16),
                pltpu.VMEM((tokens, depth), BF16),
                pltpu.VMEM((tokens, block), F32),
                pltpu.VMEM((tokens, block), F32),
                state,
                state,
                state,
                pltpu.SemaphoreType.DMA((pl.cdiv(wide, block) + 1,)),
            ],
        ),
        compiler_params=params(),
        cost_estimate=cost(3_400_000_000, 15_000_000, 800_000),
        name="scores",
    )(place, core, ref_rows, own_rows, far_rows, target, heads)


def final_kernel(len_ref, recv_ref, logp_ref, sums_ref):
    recv = recv_ref[...]
    rows = []
    for k in (0, 3):
        tops = recv[:, k]
        top = jnp.max(tops, axis=0, keepdims=True)
        total = jnp.sum(recv[:, k + 1] * jnp.exp(tops - top), axis=0, keepdims=True)
        pick = jnp.sum(recv[:, k + 2], axis=0, keepdims=True)
        rows.append(pick - (top + jnp.log(total)))
    ref, policy = rows
    logp_ref[0:1, :] = policy
    logp_ref[1:2, :] = ref
    token = lax.broadcasted_iota(jnp.int32, policy.shape, 1)
    lane = lax.broadcasted_iota(jnp.int32, sums_ref.shape, 1)
    gap = policy - ref
    total = jnp.zeros(sums_ref.shape, F32)
    row = lax.broadcasted_iota(jnp.int32, sums_ref.shape, 0)
    start = jnp.int32(0)
    for r in range(len_ref.shape[1]):
        stop = start + len_ref[0, r]
        inside = jnp.logical_and(token >= start, token < stop)
        a = jnp.sum(jnp.where(inside, policy, 0.0), axis=1, keepdims=True)
        b = jnp.sum(jnp.where(inside, gap, 0.0), axis=1, keepdims=True)
        total = jnp.where(lane == r, jnp.where(row == 0, a, b), total)
        start = stop
    sums_ref[...] = total


def finish(lengths, recv):
    tokens = recv.shape[2]
    requests = lengths.shape[1]
    return call(
        final_kernel, "finish", (
            jax.ShapeDtypeStruct((2, tokens), F32),
            jax.ShapeDtypeStruct((2, requests), F32),
        ),
        [lengths], [recv], cost(200_000, 150_000),
    )


def from_behind(x, axis, by):
    count = lax.axis_size(axis)
    pairs = [(i, i + by) for i in range(count) if 0 <= i + by < count]
    return lax.ppermute(x, axis, pairs)


def body(
    inner_x,
    gate_z,
    state_b,
    state_c,
    step_raw,
    decay_log,
    step_bias,
    skip_gain,
    norm_gain,
    out_weight,
    residual,
    ref_hidden,
    policy_gain,
    ref_gain,
    policy_head,
    ref_head,
    saved_pages,
    lengths,
    page_owner,
    page_slot,
    resumed,
    targets,
):
    parts = lax.axis_size("vocab")
    tokens, channels = inner_x.shape
    inner_x, gate_z, state_b, state_c, step_raw, out_weight, residual, ref_hidden = map(
        settled, (inner_x, gate_z, state_b, state_c, step_raw, out_weight, residual, ref_hidden)
    )
    lengths, resumed = settled(lengths), settled(resumed)
    norm_gain, policy_gain, ref_gain = map(settled, (norm_gain[None], policy_gain[None], ref_gain[None]))
    groups = lax.axis_size("grp")
    slots = saved_pages.shape[0]
    group = lax.axis_index("grp")
    place = lax.axis_index("vocab")[None].astype(jnp.int32)
    my_group = group[None].astype(jnp.int32)

    core = place & 1
    other = [(i, i ^ 1) for i in range(parts)]
    ring = 8
    span = groups // ring
    lines = [[x * ring + k for k in range(ring)] for x in range(span)]
    deep, columns = policy_head.shape
    spare = jnp.zeros((deep, -2 * columns % 128), policy_head.dtype)
    heads = lax.all_gather(
        jnp.concatenate([ref_head, policy_head, spare], axis=1), "grp", axis=0, tiled=True
    )

    asking = send_rows(page_owner, lengths, resumed, my_group, core, state_c, ring)
    asking, page_owner, page_slot = lax.optimization_barrier((asking, page_owner, page_slot))
    saved_pages = after(asking, settled(saved_pages))
    asking = lax.all_to_all(
        asking, "grp", split_axis=0, concat_axis=0, tiled=True, axis_index_groups=lines
    )
    far_asking = lax.ppermute(asking, "vocab", other)
    pages = [saved_pages]
    for k in range(1, span):
        pairs = [(i, (i + k * ring) % groups) for i in range(groups)]
        pages.append(lax.ppermute(saved_pages, "grp", pairs))

    my_x, my_z = group >> 3, group & 7
    last = page_owner.shape[1] - 1
    before_owner = jnp.concatenate([page_owner[:1, 0], page_owner[:-1, last]])
    before_slot = jnp.concatenate([page_slot[:1, 0], page_slot[:-1, last]])
    first_row = my_x * ring
    asked = lax.dynamic_slice_in_dim(page_owner, first_row, ring, 0)[:, 1:]
    asked_slot = lax.dynamic_slice_in_dim(page_slot, first_row, ring, 0)[:, 1:]
    step = jnp.arange(span, dtype=jnp.int32)
    wanted = ((my_x - step) & (span - 1)) * ring + my_z
    match = asked[:, None, :] == wanted[None, :, None]
    found = jnp.sum(jnp.where(match, asked_slot[:, None, :], 0), axis=2) + slots * step[None, :]
    first_page = ((my_x - (before_owner >> 3)) & (span - 1)) * slots + before_slot
    first_page = lax.dynamic_slice_in_dim(first_page, first_row, ring, 0)
    table = jnp.concatenate([found, first_page[:, None]], axis=1)

    per_head = jnp.broadcast_to(
        jnp.stack([decay_log, step_bias, skip_gain])[:, :, None], (3, decay_log.shape[0], tokens)
    )
    base, decay, ending = scan_parts(
        lengths, resumed, inner_x, gate_z, state_b, state_c, step_raw, per_head
    )
    carried = from_behind(ending, "grp", 1)
    ref_normed = ref_norm(ref_hidden, ref_gain)
    target = jnp.broadcast_to(targets[:, None], (tokens, 128))

    reads = page_reads(table, core, asking, far_asking, pages)
    reads = lax.all_to_all(
        reads, "grp", split_axis=0, concat_axis=0, tiled=True, axis_index_groups=lines
    )
    rails = [[k * 2 + c for k in range(parts // 2)] for c in range(2)]
    theirs, ours = project(
        lengths, my_group, core, state_c, carried, reads, base, decay, norm_gain, out_weight
    )
    summed = pair_sum(ours, lax.ppermute(theirs, "vocab", other))
    recv = lax.all_to_all(
        summed.reshape(parts // 2, tokens // parts, -1), "vocab",
        split_axis=0, concat_axis=0, tiled=True, axis_index_groups=rails,
    )
    mine = norm_rows(core * (parts // 2) + (place >> 1), recv, residual, policy_gain)
    normed = lax.all_to_all(
        mine, "vocab", split_axis=0, concat_axis=0, tiled=True, axis_index_groups=rails
    )
    normed = normed.reshape(tokens // 2, -1)
    far = lax.ppermute(normed, "vocab", other)
    stats = scores(place, core, ref_normed, normed, far, target, heads, columns, parts)
    recv = lax.all_to_all(stats, "vocab", split_axis=0, concat_axis=0, tiled=True)
    return finish(lengths, recv)


def solution(mesh):
    in_specs = (
        P("grp", "vocab"),
        P("grp", "vocab"),
        P("grp", None),
        P("grp", None),
        P("vocab", "grp"),
        P("vocab"),
        P("vocab"),
        P("vocab"),
        P("vocab"),
        P("vocab", None),
        P("grp", None),
        P("grp", None),
        P(),
        P(),
        P("grp", "vocab"),
        P("grp", "vocab"),
        P("grp", "vocab", None),
        P("grp", None),
        P(),
        P(),
        P("grp", None),
        P("grp"),
    )
    out_specs = (P(None, "grp"), P(None, "grp"))
    return jax.shard_map(body, mesh=mesh, in_specs=in_specs, out_specs=out_specs, check_vma=False)
```

```python
import functools

import jax
import jax.numpy as jnp
from jax import lax
from jax.experimental import pallas as pl
from jax.experimental.pallas import tpu as pltpu
from jax.sharding import PartitionSpec as P

INNER = 4096
EPS = 1e-05
F32 = jnp.float32
BF16 = jnp.bfloat16
NT = (((1,), (1,)), ((), ()))
TN = (((0,), (0,)), ((), ()))


def params(limit=48 << 20):
    return pltpu.CompilerParams(vmem_limit_bytes=limit)


def cost(flops, moved, transcendentals=0):
    return pl.CostEstimate(flops=flops, bytes_accessed=moved, transcendentals=transcendentals)


def settled(x):
    return pltpu.with_memory_space_constraint(x, pltpu.HBM)


def whole(x):
    zeros = (0,) * len(x.shape)
    return pl.BlockSpec(x.shape, lambda *_: zeros)


def call(kernel, name, outs, scalars, arrays, estimate, scratch=()):
    return pl.pallas_call(
        kernel,
        out_shape=outs,
        grid_spec=pltpu.PrefetchScalarGridSpec(
            num_scalar_prefetch=len(scalars),
            grid=(1,),
            in_specs=[whole(x) for x in arrays],
            out_specs=jax.tree.map(whole, outs),
            scratch_shapes=list(scratch),
        ),
        compiler_params=params(),
        cost_estimate=estimate,
        name=name,
    )(*scalars, *arrays)


def split(value):
    high = value.astype(BF16)
    low = (value - high.astype(F32)).astype(BF16)
    return high, low


def send_kernel(own_ref, len_ref, res_ref, group_ref, core_ref, c_ref, out_ref):
    reach = out_ref.shape[0]
    tokens, states = c_ref.shape
    requests = len_ref.shape[1]
    span = own_ref.shape[0] // reach
    my_x = group_ref[0] // reach
    half = tokens // 2
    begin = pl.multiple_of(core_ref[0] * half, half)
    c = c_ref[pl.ds(begin, half)]
    shape = (out_ref.shape[1] - half, states)
    token = lax.broadcasted_iota(jnp.int32, shape, 1) + begin
    group = group_ref[0]
    number = jnp.full(shape, -1, jnp.int32)
    home = jnp.full(shape, -1, jnp.int32)
    start = jnp.int32(0)
    for r in range(requests):
        stop = start + len_ref[0, r]
        if r:
            owner = own_ref[group, r]
            page = (my_x - owner // reach + span) % span
            live = res_ref[0, r]
        else:
            behind = own_ref[jnp.maximum(group - 1, 0), requests - 1]
            owner = jnp.where(group > 0, behind, own_ref[0, 0])
            page = jnp.int32(span)
            live = jnp.where(group > 0, 1, res_ref[0, 0])
        page = jnp.where(live > 0, page, -1)
        inside = jnp.logical_and(token >= start, token < stop)
        number = jnp.where(inside, page, number)
        home = jnp.where(inside, owner % reach, home)
        start = stop
    for dest in range(reach):
        out_ref[dest, :half, :] = c
        mine = jnp.where(home == dest, number, -1)
        out_ref[dest, half:, :] = mine.astype(F32).astype(BF16)


def send_rows(page_owner, lengths, resumed, group, core, c, reach):
    tokens, states = c.shape
    return call(
        send_kernel, "send_rows", jax.ShapeDtypeStruct((reach, tokens // 2 + 16, states), BF16),
        [page_owner, lengths, resumed, group, core], [c], cost(100_000, 700_000),
    )


def after_kernel(_, pages_ref, out_ref):
    out_ref[...] = pages_ref[...]


def after(first, pages):
    return pl.pallas_call(
        after_kernel,
        out_shape=jax.ShapeDtypeStruct(pages.shape, pages.dtype),
        grid=(1,),
        in_specs=[pl.BlockSpec(memory_space=pltpu.HBM), whole(pages)],
        out_specs=whole(pages),
        compiler_params=params(),
        cost_estimate=cost(0, 500_000),
        name="after",
    )(first, pages)


def reads_kernel(table_ref, core_ref, own_ref, far_ref, *refs):
    *page_refs, out_ref, pages = refs
    groups, wide, states = own_ref.shape
    half = wide - 16
    count = table_ref.shape[1]
    slots = page_refs[0].shape[0]
    for k, ref in enumerate(page_refs):
        pages[k * slots : (k + 1) * slots] = ref[...]
    for j in range(groups):
        halves, numbers = [], []
        for ref in (own_ref, far_ref):
            halves.append(ref[j, :half, :].astype(F32))
            turned = ref[j, half:, :].astype(F32).T
            numbers.append(jnp.broadcast_to(turned[:, :1], (half, states)))
        c = jnp.concatenate(halves, axis=0)
        number = jnp.concatenate(numbers, axis=0)
        lhs, rhs = [], []
        for s in range(count):
            lhs.append(jnp.where(number == float(s), c, 0.0).astype(BF16))
            rhs.append(pages[table_ref[j, s]])
        term = lax.dot_general(
            jnp.concatenate(lhs, axis=1),
            jnp.concatenate(rhs, axis=1),
            NT,
            preferred_element_type=F32,
        )
        term = term.astype(BF16)
        out_ref[j, pl.ds(pl.multiple_of(core_ref[0] * half, half), half)] = term[:half]
        out_ref[j, pl.ds(pl.multiple_of((1 - core_ref[0]) * half, half), half)] = term[half:]


def page_reads(table, core, own, far, pages):
    groups = own.shape[0]
    tokens = 2 * (own.shape[1] - 16)
    slots, channels, states = pages[0].shape
    return call(
        reads_kernel, "page_reads", jax.ShapeDtypeStruct((groups, tokens, channels), BF16),
        [table, core], [own, far, *pages], cost(700_000_000, 3_000_000), [pltpu.VMEM((len(pages) * slots, channels, states), BF16)],
    )


def scan_kernel(
    len_ref, res_ref, x_ref, z_ref, b_ref, c_ref, raw_ref, par_ref, base_ref, decay_ref, carry_ref
):
    tokens, channels = x_ref.shape
    heads = raw_ref.shape[0]
    width = channels // heads
    rows = lax.broadcasted_iota(jnp.int32, (tokens, tokens), 0)
    cols = lax.broadcasted_iota(jnp.int32, (tokens, tokens), 1)
    row_req = jnp.zeros((tokens, tokens), jnp.int32)
    col_req = jnp.zeros((tokens, tokens), jnp.int32)
    end = jnp.int32(0)
    last_start = jnp.int32(0)
    requests = len_ref.shape[1]
    for r in range(requests):
        last_start = end
        end = end + len_ref[0, r]
        row_req = row_req + (rows >= end).astype(jnp.int32)
        col_req = col_req + (cols >= end).astype(jnp.int32)
    same = row_req == col_req
    causal = jnp.logical_and(same, cols <= rows)
    upto = jnp.logical_and(same, rows <= cols).astype(F32)
    step = jax.nn.softplus(raw_ref[...] + par_ref[1])
    log_decay = -jnp.exp(par_ref[0]) * step
    seg = jnp.dot(
        jnp.concatenate([log_decay, log_decay], axis=0),
        upto,
        precision=lax.Precision.HIGHEST,
        preferred_element_type=F32,
    )
    both = jnp.concatenate([seg[:heads], step], axis=0)
    turned = both.T
    scores = lax.dot_general(c_ref[...], b_ref[...], NT, preferred_element_type=F32)
    x = x_ref[...]
    x_f = x.astype(F32)
    channel_head = lax.broadcasted_iota(jnp.int32, (tokens, channels), 1) // width
    mixed = jnp.zeros((tokens, channels), F32)
    reach = jnp.zeros((tokens, channels), F32)
    weight = jnp.zeros((tokens, channels), F32)
    in_last = rows[:, :1] >= last_start
    for h in range(heads):
        column = turned[:, h : h + 1]
        row = both[h : h + 1, :]
        fade = jnp.exp(jnp.where(causal, column - row, 0.0))
        mixing = jnp.where(causal, fade * scores * both[heads + h : heads + h + 1, :], 0.0)
        out = jnp.dot(mixing.astype(BF16), x, preferred_element_type=F32)
        mine = channel_head == h
        skip = par_ref[2, h : h + 1, :]
        mixed = jnp.where(mine, out + skip * x_f, mixed)
        reach = jnp.where(mine, jnp.exp(column), reach)
        tail = jnp.where(in_last, column[tokens - 1 :, :] - column, 0.0)
        tail = jnp.where(in_last, jnp.exp(tail) * turned[:, heads + h : heads + h + 1], 0.0)
        weight = jnp.where(mine, tail, weight)
    gate = jax.nn.silu(z_ref[...].astype(F32))
    base_ref[...] = mixed * gate
    decay_ref[...] = reach * gate
    high, low = split(x_f * weight)
    b = b_ref[...]
    states = b.shape[1]
    carry_ref[:channels, :] = lax.dot_general(
        high, b, TN, preferred_element_type=F32
    ) + lax.dot_general(low, b, TN, preferred_element_type=F32)
    live = (res_ref[0, requests - 1] > 0).astype(F32)
    keep = reach[tokens - 1 :, :] * live
    sub = lax.broadcasted_iota(jnp.int32, (8, states), 0)
    tail = jnp.zeros((8, states), F32)
    for k in range(channels // states):
        piece = jnp.broadcast_to(keep[:, k * states : (k + 1) * states], (8, states))
        tail = jnp.where(sub == k, piece, tail)
    carry_ref[channels:, :] = tail


def scan_parts(lengths, resumed, x, z, b, c, raw, per_head):
    tokens, channels = x.shape
    states = b.shape[1]
    big = jax.ShapeDtypeStruct((tokens, channels), F32)
    return call(
        scan_kernel, "scan_parts", (big, big, jax.ShapeDtypeStruct((channels + 8, states), F32)),
        [lengths, resumed], [x, z, b, c, raw, per_head], cost(400_000_000, 2_000_000, 500_000),
    )


def project_kernel(
    len_ref, group_ref, core_ref, c_ref, carry_ref, reads_ref, base_ref, decay_ref, gain_ref, w_ref,
    send_ref, keep_ref, ready, pairs,
):
    c = c_ref[...]
    token = lax.broadcasted_iota(jnp.int32, c.shape, 0)
    stop = len_ref[0, 0] * (group_ref[0] > 0).astype(jnp.int32)
    first = jnp.where(token < stop, c, jnp.zeros_like(c))
    tokens, channels = base_ref.shape
    states = c.shape[1]
    high, low = split(carry_ref[:channels, :])
    start = jnp.sum(reads_ref[...].astype(F32), axis=0)
    rows = [carry_ref[channels + k : channels + k + 1, :] for k in range(channels // states)]
    keep = jnp.concatenate(rows, axis=1)
    among = lax.broadcasted_iota(jnp.int32, (tokens, channels), 0) < stop
    start = jnp.where(among, start * keep, start)
    start = start + lax.dot_general(first, high, NT, preferred_element_type=F32)
    start = start + lax.dot_general(first, low, NT, preferred_element_type=F32)
    gated = base_ref[...] + decay_ref[...] * start
    square = jnp.sum(gated * gated, axis=1, keepdims=True)
    weighted = (gated * gain_ref[...]).astype(BF16)
    model = w_ref.shape[1]
    lane = lax.broadcasted_iota(jnp.int32, (c.shape[0], 128), 1)
    rounded = square.astype(BF16).astype(F32)
    pair = jnp.where(lane == 0, rounded, jnp.where(lane == 1, square - rounded, 0.0))
    ready[...] = weighted
    pairs[...] = pair.astype(BF16)
    half = send_ref.shape[0]
    for out_ref, which in ((send_ref, 1 - core_ref[0]), (keep_ref, core_ref[0])):
        part = pl.ds(pl.multiple_of(which * half, half), half)
        out_ref[:, :model] = jnp.dot(ready[part], w_ref[...], preferred_element_type=F32).astype(BF16)
        out_ref[:, model:] = pairs[part]


def project(lengths, group, core, c, carry, reads, base, decay, gain, w):
    tokens, channels = base.shape
    model = w.shape[1]
    half = jax.ShapeDtypeStruct((tokens // 2, model + 128), BF16)
    return call(
        project_kernel, "project", (half, half),
        [lengths, group, core], [c, carry, reads, base, decay, gain, w], cost(300_000_000, 3_500_000), [pltpu.VMEM((tokens, channels), BF16), pltpu.VMEM((tokens, 128), BF16)],
    )


def pair_kernel(a_ref, b_ref, out_ref):
    model = a_ref.shape[1] - 128
    a, b = a_ref[...].astype(F32), b_ref[...].astype(F32)
    total = a + b
    out_ref[:, :model] = total[:, :model].astype(BF16)
    square = total[:, model : model + 1] + total[:, model + 1 : model + 2]
    lane = lax.broadcasted_iota(jnp.int32, (a.shape[0], 128), 1)
    rounded = square.astype(BF16).astype(F32)
    pair = jnp.where(lane == 0, rounded, jnp.where(lane == 1, square - rounded, 0.0))
    out_ref[:, model:] = pair.astype(BF16)


def pair_sum(a, b):
    return call(
        pair_kernel, "pair_sum", jax.ShapeDtypeStruct(a.shape, BF16),
        [], [a, b], cost(300_000, 1_700_000),
    )


def norm_kernel(place_ref, recv_ref, res_ref, gain_ref, out_ref):
    model = res_ref.shape[1]
    total = jnp.sum(recv_ref[...].astype(F32), axis=0)
    square = total[:, model : model + 1] + total[:, model + 1 : model + 2]
    hidden = res_ref[...].astype(F32) + total[:, :model] * lax.rsqrt(square / INNER + EPS)
    factor = lax.rsqrt(jnp.mean(hidden * hidden, axis=1, keepdims=True) + EPS)
    normed = (hidden * factor * gain_ref[...]).astype(BF16)
    for k in range(out_ref.shape[0]):
        out_ref[k] = normed


def norm_rows(place, recv, residual, gain):
    parts, mine, wide = recv.shape
    model = residual.shape[1]
    return pl.pallas_call(
        norm_kernel,
        out_shape=jax.ShapeDtypeStruct((parts, mine, model), BF16),
        grid_spec=pltpu.PrefetchScalarGridSpec(
            num_scalar_prefetch=1,
            grid=(1,),
            in_specs=[
                pl.BlockSpec((parts, mine, wide), lambda i, p: (0, 0, 0)),
                pl.BlockSpec((mine, model), lambda i, p: (p[0], 0)),
                pl.BlockSpec((1, model), lambda i, p: (0, 0)),
            ],
            out_specs=pl.BlockSpec((parts, mine, model), lambda i, p: (0, 0, 0)),
        ),
        compiler_params=params(),
        cost_estimate=cost(1_000_000, 3_200_000),
        name="norm_rows",
    )(place, recv, residual, gain)


def ref_norm_kernel(x_ref, gain_ref, out_ref):
    x = x_ref[...].astype(F32)
    factor = lax.rsqrt(jnp.mean(x * x, axis=1, keepdims=True) + EPS)
    out_ref[...] = (x * factor * gain_ref[...]).astype(BF16)


def ref_norm(x, gain):
    return call(
        ref_norm_kernel, "ref_norm", jax.ShapeDtypeStruct(x.shape, BF16),
        [], [x, gain], cost(2_000_000, 2_000_000),
    )


def score_kernel(
    columns, block, place_ref, core_ref, ref_ref, own_ref, far_ref, target_ref, head_ref, out_ref,
    head, rows, logits_a, logits_b, tops, sums, picks, sems,
):
    wide = head.shape[1]
    low = float(jnp.finfo(F32).min)
    cuts = [(c, min(c + block, wide)) for c in range(0, wide, block)]
    copies = []
    for k, (c, d) in enumerate(cuts):
        copies.append(pltpu.make_async_copy(head_ref.at[:, c:d], head.at[:, c:d], sems.at[k]))
        copies[-1].start()
    half = own_ref.shape[0]
    rows[pl.ds(pl.multiple_of(core_ref[0] * half, half), half)] = own_ref[...]
    rows[pl.ds(pl.multiple_of((1 - core_ref[0]) * half, half), half)] = far_ref[...]
    tops[...] = jnp.full_like(tops, low)
    sums[...] = jnp.zeros_like(sums)
    picks[...] = jnp.zeros_like(picks)
    jobs = []
    for model in range(2):
        first, stop = model * columns, (model + 1) * columns
        for k, (c, d) in enumerate(cuts):
            if c < stop and d > first:
                jobs.append((model, k, c, min(d, (stop + 127) // 128 * 128)))
    lane = lax.broadcasted_iota(jnp.int32, target_ref.shape, 1)
    local = target_ref[...] - place_ref[0] * columns
    local = jnp.where(jnp.logical_and(local >= 0, local < columns), local, -2 * wide)

    def statistics(job, logits):
        model, _, c, d = job
        first, stop = model * columns, (model + 1) * columns
        wanted = local + (first - c)
        old = tops[model]
        top, pick, pieces = old, picks[model], []
        for k in range((d - c) // 128):
            start = c + k * 128
            piece = logits[:, k * 128 : (k + 1) * 128]
            if start < first:
                piece = jnp.where(lane >= first - start, piece, low)
            if start + 128 > stop:
                piece = jnp.where(lane < stop - start, piece, low)
            pick = pick + jnp.where(lane == wanted - k * 128, piece, 0.0)
            pieces.append(piece)
            top = jnp.maximum(top, piece)
        total = sums[model] * jnp.exp(old - top)
        for piece in pieces:
            total = total + jnp.exp(piece - top)
        tops[model] = top
        sums[model] = total
        picks[model] = pick

    waited = set()
    for i, job in enumerate(jobs):
        model, k, c, d = job
        if k not in waited:
            copies[k].wait()
            waited.add(k)
        logits = (logits_a, logits_b)[i % 2]
        left = ref_ref if model == 0 else rows
        logits[:, : d - c] = jnp.dot(left[...], head[:, c:d], preferred_element_type=F32)
        if i:
            statistics(jobs[i - 1], (logits_a, logits_b)[(i - 1) % 2])
    statistics(jobs[-1], (logits_a, logits_b)[(len(jobs) - 1) % 2])
    stats = jnp.zeros(target_ref.shape, F32)
    for model in range(2):
        peak = jnp.max(tops[model], axis=1, keepdims=True)
        whole_sum = jnp.sum(sums[model] * jnp.exp(tops[model] - peak), axis=1, keepdims=True)
        chosen = jnp.sum(picks[model], axis=1, keepdims=True)
        stats = jnp.where(lane == 3 * model, peak, stats)
        stats = jnp.where(lane == 3 * model + 1, whole_sum, stats)
        stats = jnp.where(lane == 3 * model + 2, chosen, stats)
    out_ref[...] = jnp.broadcast_to(stats.T[:8, :][None], out_ref.shape)


def scores(place, core, ref_rows, own_rows, far_rows, target, heads, columns, parts):
    depth, wide = heads.shape
    tokens = ref_rows.shape[0]
    block = 512
    state = pltpu.VMEM((2, tokens, 128), F32)
    out = jax.ShapeDtypeStruct((parts, 8, tokens), F32)
    return pl.pallas_call(
        functools.partial(score_kernel, columns, block),
        out_shape=out,
        grid_spec=pltpu.PrefetchScalarGridSpec(
            num_scalar_prefetch=2,
            grid=(1,),
            in_specs=[whole(x) for x in (ref_rows, own_rows, far_rows, target)]
            + [pl.BlockSpec(memory_space=pltpu.HBM)],
            out_specs=whole(out),
            scratch_shapes=[
                pltpu.VMEM((depth, wide), BF16),
                pltpu.VMEM((tokens, depth), BF16),
                pltpu.VMEM((tokens, block), F32),
                pltpu.VMEM((tokens, block), F32),
                state,
                state,
                state,
                pltpu.SemaphoreType.DMA((pl.cdiv(wide, block),)),
            ],
        ),
        compiler_params=params(),
        cost_estimate=cost(3_400_000_000, 15_000_000, 800_000),
        name="scores",
    )(place, core, ref_rows, own_rows, far_rows, target, heads)


def final_kernel(len_ref, recv_ref, logp_ref, sums_ref):
    recv = recv_ref[...]
    rows = []
    for k in (0, 3):
        tops = recv[:, k]
        top = jnp.max(tops, axis=0, keepdims=True)
        total = jnp.sum(recv[:, k + 1] * jnp.exp(tops - top), axis=0, keepdims=True)
        pick = jnp.sum(recv[:, k + 2], axis=0, keepdims=True)
        rows.append(pick - (top + jnp.log(total)))
    ref, policy = rows
    logp_ref[0:1, :] = policy
    logp_ref[1:2, :] = ref
    token = lax.broadcasted_iota(jnp.int32, policy.shape, 1)
    lane = lax.broadcasted_iota(jnp.int32, sums_ref.shape, 1)
    gap = policy - ref
    total = jnp.zeros(sums_ref.shape, F32)
    row = lax.broadcasted_iota(jnp.int32, sums_ref.shape, 0)
    start = jnp.int32(0)
    for r in range(len_ref.shape[1]):
        stop = start + len_ref[0, r]
        inside = jnp.logical_and(token >= start, token < stop)
        a = jnp.sum(jnp.where(inside, policy, 0.0), axis=1, keepdims=True)
        b = jnp.sum(jnp.where(inside, gap, 0.0), axis=1, keepdims=True)
        total = jnp.where(lane == r, jnp.where(row == 0, a, b), total)
        start = stop
    sums_ref[...] = total


def finish(lengths, recv):
    tokens = recv.shape[2]
    requests = lengths.shape[1]
    return call(
        final_kernel, "finish", (
            jax.ShapeDtypeStruct((2, tokens), F32),
            jax.ShapeDtypeStruct((2, requests), F32),
        ),
        [lengths], [recv], cost(200_000, 150_000),
    )


def from_behind(x, axis, by):
    count = lax.axis_size(axis)
    pairs = [(i, i + by) for i in range(count) if 0 <= i + by < count]
    return lax.ppermute(x, axis, pairs)


def body(
    inner_x,
    gate_z,
    state_b,
    state_c,
    step_raw,
    decay_log,
    step_bias,
    skip_gain,
    norm_gain,
    out_weight,
    residual,
    ref_hidden,
    policy_gain,
    ref_gain,
    policy_head,
    ref_head,
    saved_pages,
    lengths,
    page_owner,
    page_slot,
    resumed,
    targets,
):
    parts = lax.axis_size("vocab")
    tokens, channels = inner_x.shape
    inner_x, gate_z, state_b, state_c, step_raw, out_weight, residual, ref_hidden = map(
        settled, (inner_x, gate_z, state_b, state_c, step_raw, out_weight, residual, ref_hidden)
    )
    lengths, resumed = settled(lengths), settled(resumed)
    norm_gain, policy_gain, ref_gain = map(settled, (norm_gain[None], policy_gain[None], ref_gain[None]))
    groups = lax.axis_size("grp")
    slots = saved_pages.shape[0]
    group = lax.axis_index("grp")
    place = lax.axis_index("vocab")[None].astype(jnp.int32)
    my_group = group[None].astype(jnp.int32)

    core = place & 1
    other = [(i, i ^ 1) for i in range(parts)]
    ring = 8
    span = groups // ring
    lines = [[x * ring + k for k in range(ring)] for x in range(span)]
    deep, columns = policy_head.shape
    spare = jnp.zeros((deep, -2 * columns % 128), policy_head.dtype)
    heads = lax.all_gather(
        jnp.concatenate([ref_head, policy_head, spare], axis=1), "grp", axis=0, tiled=True
    )

    asking = send_rows(page_owner, lengths, resumed, my_group, core, state_c, ring)
    asking, page_owner, page_slot = lax.optimization_barrier((asking, page_owner, page_slot))
    saved_pages = settled(saved_pages)
    asking = lax.all_to_all(
        asking, "grp", split_axis=0, concat_axis=0, tiled=True, axis_index_groups=lines
    )
    far_asking = lax.ppermute(asking, "vocab", other)
    pages = [saved_pages]
    for k in range(1, span):
        pairs = [(i, (i + k * ring) % groups) for i in range(groups)]
        pages.append(lax.ppermute(saved_pages, "grp", pairs))

    my_x, my_z = group >> 3, group & 7
    last = page_owner.shape[1] - 1
    before_owner = jnp.concatenate([page_owner[:1, 0], page_owner[:-1, last]])
    before_slot = jnp.concatenate([page_slot[:1, 0], page_slot[:-1, last]])
    first_row = my_x * ring
    asked = lax.dynamic_slice_in_dim(page_owner, first_row, ring, 0)[:, 1:]
    asked_slot = lax.dynamic_slice_in_dim(page_slot, first_row, ring, 0)[:, 1:]
    step = jnp.arange(span, dtype=jnp.int32)
    wanted = ((my_x - step) & (span - 1)) * ring + my_z
    match = asked[:, None, :] == wanted[None, :, None]
    found = jnp.sum(jnp.where(match, asked_slot[:, None, :], 0), axis=2) + slots * step[None, :]
    first_page = ((my_x - (before_owner >> 3)) & (span - 1)) * slots + before_slot
    first_page = lax.dynamic_slice_in_dim(first_page, first_row, ring, 0)
    table = jnp.concatenate([found, first_page[:, None]], axis=1)

    per_head = jnp.broadcast_to(
        jnp.stack([decay_log, step_bias, skip_gain])[:, :, None], (3, decay_log.shape[0], tokens)
    )
    base, decay, ending = scan_parts(
        lengths, resumed, inner_x, gate_z, state_b, state_c, step_raw, per_head
    )
    carried = from_behind(ending, "grp", 1)
    ref_normed = ref_norm(ref_hidden, ref_gain)
    target = jnp.broadcast_to(targets[:, None], (tokens, 128))

    reads = page_reads(table, core, asking, far_asking, pages)
    reads = lax.all_to_all(
        reads, "grp", split_axis=0, concat_axis=0, tiled=True, axis_index_groups=lines
    )
    rails = [[k * 2 + c for k in range(parts // 2)] for c in range(2)]
    theirs, ours = project(
        lengths, my_group, core, state_c, carried, reads, base, decay, norm_gain, out_weight
    )
    summed = pair_sum(ours, lax.ppermute(theirs, "vocab", other))
    recv = lax.all_to_all(
        summed.reshape(parts // 2, tokens // parts, -1), "vocab",
        split_axis=0, concat_axis=0, tiled=True, axis_index_groups=rails,
    )
    mine = norm_rows(core * (parts // 2) + (place >> 1), recv, residual, policy_gain)
    normed = lax.all_to_all(
        mine, "vocab", split_axis=0, concat_axis=0, tiled=True, axis_index_groups=rails
    )
    normed = normed.reshape(tokens // 2, -1)
    far = lax.ppermute(normed, "vocab", other)
    stats = scores(place, core, ref_normed, normed, far, target, heads, columns, parts)
    recv = lax.all_to_all(stats, "vocab", split_axis=0, concat_axis=0, tiled=True)
    return finish(lengths, recv)


def solution(mesh):
    in_specs = (
        P("grp", "vocab"),
        P("grp", "vocab"),
        P("grp", None),
        P("grp", None),
        P("vocab", "grp"),
        P("vocab"),
        P("vocab"),
        P("vocab"),
        P("vocab"),
        P("vocab", None),
        P("grp", None),
        P("grp", None),
        P(),
        P(),
        P("grp", "vocab"),
        P("grp", "vocab"),
        P("grp", "vocab", None),
        P("grp", None),
        P(),
        P(),
        P("grp", None),
        P("grp"),
    )
    out_specs = (P(None, "grp"), P(None, "grp"))
    return jax.shard_map(body, mesh=mesh, in_specs=in_specs, out_specs=out_specs, check_vma=False)
```
